32 devices in a mesh: fsdp: 16 (over z, y, core), tensor: 2 (over x).
Axes of the slice: x: 2, y: 2, z: 4, core: 2. Of those that a mesh axis runs over, the one named last changes fastest.
Arguments:
- embedded: bfloat16 [8192, 768], P(('fsdp', 'tensor')), may hold values from -6 to 6
- segments: int32 [32, 256], P('fsdp'), may hold values from 0 to 3, never falling along the last dimension, each value on 1 to 128 neighbouring positions
- thoughts: int32 [32, 64], P(('fsdp', 'tensor')), may hold values from -1 to 255, as said below
- cotangent: bfloat16 [8192, 768], P(('fsdp', 'tensor')), may hold values from -6 to 6
- norm_gains: bfloat16 [2, 2, 768], replicated, may hold values from 0.5 to 1.5
- norm_shifts: bfloat16 [2, 2, 768], replicated, may hold values from -1 to 1
- joint_weight: bfloat16 [2, 768, 3, 768], P(None, 'fsdp', None, 'tensor'), may hold values from -0.21875 to 0.21875
- joint_bias: bfloat16 [2, 2, 768], P(None, None, 'tensor'), may hold values from -1 to 1
- merge_weight: bfloat16 [2, 768, 768], P(None, 'tensor', 'fsdp'), may hold values from -0.875 to 0.875
- expand_weight: bfloat16 [2, 768, 3072], P(None, 'fsdp', 'tensor'), may hold values from -0.21875 to 0.21875
- expand_bias: bfloat16 [2, 3072], P(None, 'tensor'), may hold values from -1 to 1
- shrink_weight: bfloat16 [2, 3072, 768], P(None, 'tensor', 'fsdp'), may hold values from -0.109375 to 0.109375
- branch_biases: bfloat16 [2, 2, 768], replicated, may hold values from -1 to 1
Outputs:
- latent_out: bfloat16 [8192, 768], P(('fsdp', 'tensor'))
- language_out: bfloat16 [8192, 768], P(('fsdp', 'tensor'))
- embedded_grad: float32 [8192, 768], P(('fsdp', 'tensor'))
- gains_grad: float32 [2, 2, 768], replicated
- shifts_grad: float32 [2, 2, 768], replicated
- joint_grad: float32 [2, 768, 3, 768], P(None, 'fsdp', None, 'tensor')
- joint_bias_grad: float32 [2, 2, 768], P(None, None, 'tensor')
- merge_grad: float32 [2, 768, 768], P(None, 'tensor', 'fsdp')
- expand_grad: float32 [2, 768, 3072], P(None, 'fsdp', 'tensor')
- expand_bias_grad: float32 [2, 3072], P(None, 'tensor')
- shrink_grad: float32 [2, 3072, 768], P(None, 'tensor', 'fsdp')
- branch_grad: float32 [2, 2, 768], replicated
The draws below stay inside these ranges and needn't reach their ends.
Inputs may be any that keep to these rules, and one draw needn't show every extreme that they name: `segments`: within a sequence the document numbers never fall; a document spans 1 to 128 positions, and some document spans exactly 128. `thoughts`: each row lists distinct positions of its sequence, at least 1, in its used entries, followed by -1 in the unused ones; every row uses 64 // 2 entries or more, and the first row uses all 64.
All inputs are finite; a program needn't handle non-finite values.
Results may differ from the reference program's by a relative error of at most 0.02.
Values may be sent and summed in bfloat16 or wider, within the bound.
No kernel may reach another device: no remote copies, remote signals or barrier semaphores. Data moves between devices by JAX's collectives and lax.ppermute only.
A program may use at most 128 MiB of HBM per device.

```python
import math
import jax
import jax.numpy as jnp
import numpy as np
from jax import lax

D = 768
HEADS = 12
HEAD = 64
FF = 3072
SEQ = 256
SLOTS = 64
DOCS = 4
NSEQ = 32
TOKENS = 8192


def draw_thoughts(key, part):

    def one_row(row_key, index):
        order_key, count_key = jax.random.split(row_key)
        order = jax.random.permutation(order_key, SEQ - 2) + 1
        chosen = order[:SLOTS]
        entries = jnp.arange(SLOTS)
        chosen = jnp.where((index == 0) & (entries == 0), SEQ - 1, chosen)
        used = jax.random.randint(count_key, (), SLOTS // 2, SLOTS)
        used = jnp.where(index == 0, SLOTS, used)
        return jnp.where(entries < used, chosen, -1).astype(jnp.int32)
    row_keys = jax.random.split(key, NSEQ)
    return jax.vmap(one_row)(row_keys, jnp.arange(NSEQ))


def steps_of(rng, dims, shards, smallest, high):
    def one(position, shards_of):
        draws = jax.random.uniform(jax.random.fold_in(jax.random.fold_in(rng, 6), position), (shards_of,), jnp.float32, smallest / len(shards), high / len(shards))
        return jnp.repeat(jnp.exp(draws), dims[position] // shards_of).reshape((-1,) + (1,) * (len(dims) - position - 1))

    loudness = one(*shards[0])
    for cut in shards[1:]:
        loudness = loudness * one(*cut)
    return loudness


def split_up(count, total, bound, lean):
    portions = [(1 << 20) // math.isqrt(standing ** lean) + 1 for standing in range(2, count + 1)]
    spare, given = total - bound - (count - 1), [1] * (count - 1)
    while spare > 0:
        movable = [i for i in range(count - 1) if given[i] < bound]
        pool, left = sum([portions[i] for i in movable]), spare
        for i in movable:
            more = min(bound - given[i], max(1, left * portions[i] // pool), spare)
            given[i] = given[i] + more
            spare = spare - more
    return np.array([bound] + given)


def ragged(key, number_of, total, most, skew):
    if number_of == 2:
        one = jax.random.randint(key, (), max(1, total - most), min(most, total - 1) + 1)
        return jnp.stack([one, total - one])
    sizes = jnp.asarray(split_up(number_of, total, most, skew), jnp.int32)
    pairs = (number_of - 1) // 2
    giver, taker = sizes[1:1 + 2 * pairs:2], sizes[2:2 + 2 * pairs:2]
    room = jnp.minimum(giver - 1, most - taker)
    moved = jax.random.randint(jax.random.fold_in(key, 1), (pairs,), 0, 1 << 20) % (room + 1)
    sizes = sizes.at[1:1 + 2 * pairs:2].set(giver - moved).at[2:2 + 2 * pairs:2].set(taker + moved)
    return sizes[jax.random.permutation(jax.random.fold_in(key, 2), number_of)]


def centred(rng, shape, deviation, bound, shards=(), kind=jnp.bfloat16):
    loudness = steps_of(rng, shape, shards, -0.22, 0.18) if shards else 1.0
    values = jax.random.normal(rng, shape, jnp.float32) * deviation * loudness
    return jnp.minimum(jnp.maximum(values, -bound), bound).astype(kind)


def setup_inputs(seed: int = 0) -> dict:
    streams_of = jax.random.split(jax.random.key(seed), 14)
    return {
        "embedded": centred(streams_of[0], (TOKENS, D), 1.0, 6.0, ((0, 32),)),
        "segments": jax.vmap(lambda own: jnp.searchsorted(jnp.cumsum(ragged(own, DOCS, SEQ, SEQ // 2, 2)), jnp.arange(SEQ), side="right"))(jax.random.split(streams_of[1], NSEQ)).reshape((NSEQ, SEQ)).astype(jnp.int32),
        "thoughts": draw_thoughts(jax.random.fold_in(streams_of[13], 71), 0),
        "cotangent": centred(streams_of[3], (TOKENS, D), 1.0, 6.0, ((0, 32),)),
        "norm_gains": jnp.clip(1.0 + 0.1 * jax.random.normal(streams_of[4], (2, 2, D), jnp.float32), 0.5, 1.5).astype(jnp.bfloat16),
        "norm_shifts": centred(streams_of[5], (2, 2, D), 0.2, 1.0),
        "joint_weight": centred(streams_of[6], (2, D, 3, D), D ** -0.5, 0.21875, ((1, 16), (3, 2))),
        "joint_bias": centred(streams_of[7], (2, 2, D), 0.2, 1.0, ((2, 2),)),
        "merge_weight": centred(streams_of[8], (2, D, D), (D // 16) ** -0.5, 0.875, ((1, 2), (2, 16))),
        "expand_weight": centred(streams_of[9], (2, D, FF), D ** -0.5, 0.21875, ((1, 16), (2, 2))),
        "expand_bias": centred(streams_of[10], (2, FF), 0.2, 1.0, ((1, 2),)),
        "shrink_weight": centred(streams_of[11], (2, FF, D), FF ** -0.5, 0.109375, ((1, 2), (2, 16))),
        "branch_biases": centred(streams_of[12], (2, 2, D), 0.2, 1.0),
    }


HIGHEST = lax.Precision.HIGHEST
EPSILON = 1e-05

@jax.custom_vjp
def low(v):
    return lax.optimization_barrier(v.astype(jnp.bfloat16)).astype(jnp.float32)

@jax.custom_vjp
def low_back(v):
    return v

def low_keep(v):
    return (low(v), None)

def low_pass(kept, grad):
    return (grad,)

def back_keep(v):
    return (v, None)

def back_low(kept, grad):
    return (low(grad),)
low.defvjp(low_keep, low_pass)
low_back.defvjp(back_keep, back_low)

def layer_norm(rows, gain, shift):
    center = rows - lax.optimization_barrier(jnp.mean(rows, axis=-1, keepdims=True))
    spread = lax.optimization_barrier(jnp.mean(center * center, axis=-1, keepdims=True))
    return center * lax.rsqrt(spread + EPSILON) * gain + shift

def layer_block(rows, params, segment_row):
    gains, shifts, joint, pair_bias, merge, expand, expand_shift, shrink, biases = params
    seq_len = rows.shape[0]
    normed = low(layer_norm(rows, gains[0], shifts[0]))
    joint_out = low_back(jnp.einsum('rd,dch->rch', normed, joint, precision=HIGHEST))
    query = low(joint_out[:, 0] + pair_bias[0]).reshape(seq_len, HEADS, HEAD)
    keys = low(joint_out[:, 1]).reshape(seq_len, HEADS, HEAD)
    values = low(joint_out[:, 2] + pair_bias[1]).reshape(seq_len, HEADS, HEAD)
    scores = low_back(jnp.einsum('qhd,khd->hqk', query, keys, precision=HIGHEST)) * HEAD ** (-0.5)
    places = jnp.arange(seq_len)
    allowed = (segment_row[:, None] == segment_row[None, :]) & (places[None, :] <= places[:, None])
    scores = jnp.where(allowed[None], scores, -1e+30)
    attend = low(jax.nn.softmax(scores, axis=-1))
    mixed = low(low_back(jnp.einsum('hqk,khd->qhd', attend, values, precision=HIGHEST))).reshape(seq_len, D)
    middle = rows + low_back(jnp.dot(mixed, merge, precision=HIGHEST)) + biases[0]
    normed_two = low(layer_norm(middle, gains[1], shifts[1]))
    hidden = low_back(jnp.dot(normed_two, expand, precision=HIGHEST)) + expand_shift
    active = low(jax.nn.gelu(hidden, approximate=True))
    return middle + low_back(jnp.dot(active, shrink, precision=HIGHEST)) + biases[1]

def both_passes(params_one, params_two, rows, segment_row, slot_row):
    latent = layer_block(rows, params_one, segment_row)
    latent_low = low(latent)
    places = jnp.arange(rows.shape[0])
    slot_hit = (places[:, None] == slot_row[None, :]).astype(jnp.float32)
    source_hit = ((slot_row - 1)[:, None] == places[None, :]).astype(jnp.float32)
    picked = jnp.dot(source_hit, latent_low, precision=HIGHEST)
    occupied = lax.optimization_barrier(jnp.sum(slot_hit, axis=1))
    second = rows * (1.0 - occupied)[:, None] + jnp.dot(slot_hit, picked, precision=HIGHEST)
    language = layer_block(second, params_two, segment_row)
    return (latent_low, language)

def reference(embedded, segments, thoughts, cotangent, norm_gains, norm_shifts, joint_weight, joint_bias, merge_weight, expand_weight, expand_bias, shrink_weight, branch_biases):
    params = tuple((item.astype(jnp.float32) for item in (norm_gains, norm_shifts, joint_weight, joint_bias, merge_weight, expand_weight, expand_bias, shrink_weight, branch_biases)))
    rows_all = embedded.astype(jnp.float32).reshape(NSEQ, SEQ, D)
    grads_all = cotangent.astype(jnp.float32).reshape(NSEQ, SEQ, D)

    def step(totals, item):
        rows, segment_row, slot_row, grad_out = item

        def forward(prm, inputs):
            return both_passes(tuple((a[0] for a in prm)), tuple((a[1] for a in prm)), inputs, segment_row, slot_row)
        (latent, language), pull = jax.vjp(forward, params, rows)
        grad_params, grad_rows = pull((jnp.zeros_like(latent), grad_out))
        totals = jax.tree.map(jnp.add, totals, grad_params)
        return (totals, (latent.astype(jnp.bfloat16), language.astype(jnp.bfloat16), grad_rows))
    start = jax.tree.map(jnp.zeros_like, params)
    totals, (latent_all, language_all, grad_rows_all) = lax.scan(step, start, (rows_all, segments, thoughts, grads_all))
    return (latent_all.reshape(TOKENS, D), language_all.reshape(TOKENS, D), grad_rows_all.reshape(TOKENS, D), totals[0], totals[1], totals[2], totals[3], totals[4], totals[5], totals[6], totals[7], totals[8])
```

```python
from functools import partial

import jax
import jax.numpy as jnp
from jax import lax
from jax.experimental import pallas as pl
from jax.experimental.pallas import tpu as pltpu
from jax.sharding import PartitionSpec as P

HEAD = 64
LANES = 128
EPSILON = 1e-05
BF = jnp.bfloat16
F32 = jnp.float32
GELU_C = 0.7978845608028654
GELU_A = 0.044715
MIB = 1 << 20


def dot(a, b):
    return lax.dot_general(a, b, (((1,), (0,)), ((), ())), preferred_element_type=F32)


def dot_nt(a, b):
    return lax.dot_general(a, b, (((1,), (1,)), ((), ())), preferred_element_type=F32)


def dot_tn(a, b):
    return lax.dot_general(a, b, (((0,), (0,)), ((), ())), preferred_element_type=F32)


def factors_of(count):
    found = []
    if count % 2 == 0:
        found.append(2)
        count //= 2
    if count % 2 == 0 and (count.bit_length() - 1) % 2 == 1:
        found.append(2)
        count //= 2
    while count > 1:
        step = 4 if count % 4 == 0 else 2 if count % 2 == 0 else count
        found.append(step)
        count //= step
    return found


def shift_pairs(count, stride, size, by):
    pairs = []
    for source in range(count):
        place = (source // stride) % size
        target = source + ((place + by) % size - place) * stride
        pairs.append((source, target))
    return pairs


def swap(value):
    return lax.ppermute(value, "tensor", [(0, 1), (1, 0)])


def gather_shards(shard, count):
    me = lax.axis_index("fsdp")
    index = jnp.arange(count)
    place = jnp.zeros((count,), jnp.int32)
    sizes = factors_of(count)
    strides = [1]
    for size in sizes:
        strides.append(strides[-1] * size)
    held = shard[None]
    for size, stride in reversed(list(zip(sizes, strides))):
        width = held.shape[0]
        parts = [held]
        for by in range(1, size):
            parts.append(lax.ppermute(held, "fsdp", shift_pairs(count, stride, size, by)))
        held = jnp.concatenate(parts, axis=0)
        mine = (me // stride) % size
        theirs = (index // stride) % size
        place = place + ((mine - theirs) % size) * width
    return (held, place)


def unpack_kernel(place_ref, held_ref, *outs):
    del place_ref
    first = 0
    for out in outs:
        if out.ndim == 3:
            rows = out.shape[1]
            out[...] = held_ref[:, first : first + rows, :]
            first += rows
        else:
            rows = out.shape[2]
            for one in range(out.shape[0]):
                out[one] = held_ref[:, first : first + rows, :]
                first += rows


def unpack(held, place, kinds):
    count, rows, width = held.shape
    each = rows // sum(max(kind, 1) for kind in kinds)
    shapes, specs = [], []
    for kind in kinds:
        if kind:
            shapes.append(jax.ShapeDtypeStruct((kind, count, each, width), held.dtype))
            specs.append(pl.BlockSpec((kind, 1, each, width), lambda i, p: (0, i, 0, 0)))
        else:
            shapes.append(jax.ShapeDtypeStruct((count, each, width), held.dtype))
            specs.append(pl.BlockSpec((1, each, width), lambda i, p: (i, 0, 0)))
    outs = pl.pallas_call(
        unpack_kernel,
        name="unpack",
        out_shape=shapes,
        grid_spec=pltpu.PrefetchScalarGridSpec(
            num_scalar_prefetch=1,
            grid=(count,),
            in_specs=[pl.BlockSpec((1, rows, width), lambda i, p: (p[i], 0, 0))],
            out_specs=specs,
        ),
        compiler_params=pltpu.CompilerParams(vmem_limit_bytes=16 * MIB),
        cost_estimate=pl.CostEstimate(
            flops=0, transcendentals=0, bytes_accessed=4 * count * rows * width
        ),
    )(place, held)
    return [
        out.reshape(out.shape[:-3] + (out.shape[-3] * out.shape[-2], width)) for out in outs
    ]


def reduce_shards(blocks, count):
    me = lax.axis_index("fsdp")
    held = blocks
    stride = 1
    for size in factors_of(count):
        mine = (me // stride) % size
        split = held.reshape((held.shape[0] // size, size) + held.shape[1:])
        total = lax.dynamic_index_in_dim(split, mine, 1, keepdims=False).astype(F32)
        for by in range(1, size):
            sent = lax.dynamic_index_in_dim(split, (mine + by) % size, 1, keepdims=False)
            got = lax.ppermute(
                sent.astype(BF), "fsdp", shift_pairs(count, stride, size, by)
            )
            total = total + got.astype(F32)
        held = total
        stride *= size
    return held[0]


def sum_everywhere(value, count):
    stride = 1
    while stride < count and count % (2 * stride) == 0:
        pairs = [(source, source ^ stride) for source in range(count)]
        value = value + lax.ppermute(value, "fsdp", pairs)
        stride *= 2
    if stride < count:
        groups = [list(range(first, count, stride)) for first in range(stride)]
        value = lax.psum(value, "fsdp", axis_index_groups=groups)
    return value


def lane_masks(rows):
    lane = lax.broadcasted_iota(jnp.int32, (rows, LANES), 1)
    return (lane < HEAD, lane >= HEAD)


def attend_forward_kernel(
    n_ref, wj_ref, wm_ref, bias_ref, seg_col_ref, seg_row_ref,
    part_ref, q_ref, k_ref, v_ref, mixed_ref, neg_ref,
):
    seq = n_ref.shape[0]
    half = seq // 2
    n = n_ref[...]
    q_ref[...] = (dot(n, wj_ref[0]) + bias_ref[0:1, :]).astype(BF)
    k_ref[...] = dot(n, wj_ref[1]).astype(BF)
    v_ref[...] = (dot(n, wj_ref[2]) + bias_ref[1:2, :]).astype(BF)
    rows = lax.broadcasted_iota(jnp.int32, (seq, seq), 0)
    cols = lax.broadcasted_iota(jnp.int32, (seq, seq), 1)
    allowed = (seg_col_ref[...] == seg_row_ref[...]) & (cols <= rows)
    neg_ref[...] = jnp.where(allowed, 0.0, -1e30)
    masks = lane_masks(half)
    for pair in range(q_ref.shape[1] // LANES):
        lanes = slice(pair * LANES, (pair + 1) * LANES)
        for part in range(2):
            top = slice(part * half, (part + 1) * half)
            keys = slice(0, (part + 1) * half)
            qp = q_ref[top, lanes] * BF(HEAD ** (-0.5))
            kp = k_ref[keys, lanes]
            vp = v_ref[keys, lanes]
            found = []
            for mask in masks:
                s = dot_nt(jnp.where(mask, qp, BF(0)), kp) + neg_ref[top, keys]
                e = jnp.exp(s - jnp.max(s, axis=-1, keepdims=True))
                scale = 1.0 / jnp.sum(e, axis=-1, keepdims=True)
                found.append(dot((e * scale).astype(BF), vp))
            mixed_ref[top, lanes] = jnp.where(masks[0], found[0], found[1]).astype(BF)
    part_ref[...] = dot_nt(mixed_ref[...], wm_ref[...]).astype(BF)


def attend_forward(n, wj, wm, bias, segments):
    seq, d = n.shape
    width = wm.shape[1]
    rows = jax.ShapeDtypeStruct((seq, width), BF)
    flops = 2 * seq * d * width * 4 + 4 * seq * seq * width
    return pl.pallas_call(
        attend_forward_kernel,
        name="attend_forward",
        out_shape=[jax.ShapeDtypeStruct((seq, d), BF), rows, rows, rows, rows],
        scratch_shapes=[pltpu.VMEM((seq, seq), F32)],
        compiler_params=pltpu.CompilerParams(vmem_limit_bytes=24 * MIB),
        cost_estimate=pl.CostEstimate(
            flops=flops,
            transcendentals=seq * seq * width // HEAD,
            bytes_accessed=2 * (4 * d * width + 2 * seq * d + 4 * seq * width),
        ),
    )(n, wj, wm, bias, segments.reshape(seq, 1), segments.reshape(1, seq))


def attend_backward_kernel(
    n_ref, q_ref, k_ref, v_ref, mixed_ref, gm_ref, wj_ref, wm_ref, seg_col_ref, seg_row_ref,
    gn_ref, gj_ref, gw_ref, gb_ref, dj_ref, neg_ref, gx_ref,
):
    count, seq, _ = n_ref.shape
    width = q_ref.shape[2]
    half = seq // 2
    masks = lane_masks(half)
    rows = lax.broadcasted_iota(jnp.int32, (seq, seq), 0)
    cols = lax.broadcasted_iota(jnp.int32, (seq, seq), 1)
    for one in range(count):
        gx_ref[...] = dot(gm_ref[one], wm_ref[...]).astype(BF)
        allowed = (seg_col_ref[one] == seg_row_ref[one]) & (cols <= rows)
        neg_ref[...] = jnp.where(allowed, 0.0, -1e30)
        sums = [[], []]
        for pair in range(width // LANES):
            lanes = slice(pair * LANES, (pair + 1) * LANES)
            dk = [None, None]
            dv = [None, None]
            dq_all = []
            for part in range(2):
                top = slice(part * half, (part + 1) * half)
                keys = slice(0, (part + 1) * half)
                qp = q_ref[one, top, lanes]
                kp = k_ref[one, keys, lanes]
                vp = v_ref[one, keys, lanes]
                gp = gx_ref[top, lanes]
                dq, dk_now, dv_now = [], [], []
                for mask in masks:
                    qm = jnp.where(mask, qp, BF(0)) * BF(HEAD ** (-0.5))
                    s = dot_nt(qm, kp) + neg_ref[top, keys]
                    e = jnp.exp(s - jnp.max(s, axis=-1, keepdims=True))
                    p = e * (1.0 / jnp.sum(e, axis=-1, keepdims=True))
                    gprobs = dot_nt(jnp.where(mask, gp, BF(0)), vp)
                    inner = jnp.sum(gprobs * p, axis=-1, keepdims=True)
                    ds = (p * (gprobs - inner) * HEAD ** (-0.5)).astype(BF)
                    dq.append(dot(ds, kp))
                    dk_now.append(dot_tn(ds, qp))
                    dv_now.append(dot_tn(p.astype(BF), gp))
                dq_all.append(jnp.where(masks[0], dq[0], dq[1]))
                for block in range(part + 1):
                    at = slice(block * half, (block + 1) * half)
                    k_new = jnp.where(masks[0], dk_now[0][at], dk_now[1][at])
                    v_new = jnp.where(masks[0], dv_now[0][at], dv_now[1][at])
                    dk[block] = k_new if dk[block] is None else dk[block] + k_new
                    dv[block] = v_new if dv[block] is None else dv[block] + v_new
            sums[0].append(
                jnp.sum(dq_all[0], axis=0, keepdims=True)
                + jnp.sum(dq_all[1], axis=0, keepdims=True)
            )
            sums[1].append(
                jnp.sum(dv[0], axis=0, keepdims=True) + jnp.sum(dv[1], axis=0, keepdims=True)
            )
            for part in range(2):
                at = slice(part * half, (part + 1) * half)
                dj_ref[0, one, at, lanes] = dq_all[part].astype(BF)
                dj_ref[1, one, at, lanes] = dk[part].astype(BF)
                dj_ref[2, one, at, lanes] = dv[part].astype(BF)
        for which in range(2):
            total = jnp.concatenate(sums[which], axis=1)
            if one == 0:
                gb_ref[which : which + 1, :] = total
            else:
                gb_ref[which : which + 1, :] = gb_ref[which : which + 1, :] + total
        gn = dot_nt(dj_ref[0, one], wj_ref[0])
        gn = gn + dot_nt(dj_ref[1, one], wj_ref[1])
        gn = gn + dot_nt(dj_ref[2, one], wj_ref[2])
        gn_ref[one] = gn.astype(BF)
    d = n_ref.shape[2]
    nt = n_ref[...].reshape(count * seq, d).T
    for which in range(3):
        gj_ref[which] = dot(nt, dj_ref[which].reshape(count * seq, width)).astype(BF)
    gmt = gm_ref[...].reshape(count * seq, d).T
    gw_ref[...] = dot(gmt, mixed_ref[...].reshape(count * seq, width)).astype(BF)


def attend_backward(n, q, k, v, mixed, gm, wj, wm, segments):
    count, seq, d = n.shape
    width = wm.shape[1]
    flops = count * (2 * seq * d * width * 8 + 10 * seq * seq * width)
    return pl.pallas_call(
        attend_backward_kernel,
        name="attend_backward",
        out_shape=[
            jax.ShapeDtypeStruct((count, seq, d), BF),
            jax.ShapeDtypeStruct((3, d, width), BF),
            jax.ShapeDtypeStruct((d, width), BF),
            jax.ShapeDtypeStruct((2, width), F32),
        ],
        scratch_shapes=[
            pltpu.VMEM((3, count, seq, width), BF),
            pltpu.VMEM((seq, seq), F32),
            pltpu.VMEM((seq, width), BF),
        ],
        compiler_params=pltpu.CompilerParams(vmem_limit_bytes=40 * MIB),
        cost_estimate=pl.CostEstimate(
            flops=flops,
            transcendentals=count * seq * seq * width // HEAD,
            bytes_accessed=2 * (8 * d * width + count * (3 * seq * d + 4 * seq * width)),
        ),
    )(n, q, k, v, mixed, gm, wj, wm, segments[:, :, None], segments[:, None, :])


def mlp_forward_kernel(n_ref, we_ref, ws_ref, be_ref, out_ref, acc_ref):
    step = pl.program_id(0)
    u = dot(n_ref[...], we_ref[...]) + be_ref[...]
    t = jnp.tanh(GELU_C * (u + GELU_A * (u * u * u)))
    active = (0.5 * u * (1.0 + t)).astype(BF)
    more = dot_nt(active, ws_ref[...])

    @pl.when(step == 0)
    def _():
        acc_ref[...] = more

    @pl.when(step > 0)
    def _():
        acc_ref[...] = acc_ref[...] + more

    @pl.when(step == pl.num_programs(0) - 1)
    def _():
        out_ref[...] = acc_ref[...].astype(BF)


def mlp_forward(n, we, ws, be):
    rows, d = n.shape
    hidden = we.shape[1]
    block = 512 if hidden % 512 == 0 else hidden
    return pl.pallas_call(
        mlp_forward_kernel,
        name="mlp_forward",
        out_shape=jax.ShapeDtypeStruct((rows, d), BF),
        grid=(hidden // block,),
        in_specs=[
            pl.BlockSpec((rows, d), lambda i: (0, 0)),
            pl.BlockSpec((d, block), lambda i: (0, i)),
            pl.BlockSpec((d, block), lambda i: (0, i)),
            pl.BlockSpec((1, block), lambda i: (0, i)),
        ],
        out_specs=pl.BlockSpec((rows, d), lambda i: (0, 0)),
        scratch_shapes=[pltpu.VMEM((rows, d), F32)],
        compiler_params=pltpu.CompilerParams(vmem_limit_bytes=24 * MIB),
        cost_estimate=pl.CostEstimate(
            flops=4 * rows * d * hidden,
            transcendentals=rows * hidden,
            bytes_accessed=4 * d * hidden + 4 * rows * d,
        ),
    )(n, we, ws, be.reshape(1, hidden))


def mlp_backward_kernel(
    n_ref, g_ref, we_ref, ws_ref, be_ref,
    out_ref, gn_ref, ge_ref, gs_ref, gb_ref, acc_ref, gacc_ref, nt_ref, gt_ref,
):
    step = pl.program_id(0)

    @pl.when(step == 0)
    def _():
        nt_ref[...] = n_ref[...].T
        gt_ref[...] = g_ref[...].T

    u = dot(n_ref[...], we_ref[...]) + be_ref[...]
    square = u * u
    t = jnp.tanh(GELU_C * (u + GELU_A * (square * u)))
    lean = 0.5 * (1.0 + t)
    active = (u * lean).astype(BF)
    slope = lean + (0.5 * u) * (1.0 - t * t) * (GELU_C + (3.0 * GELU_C * GELU_A) * square)
    gh = dot(g_ref[...], ws_ref[...]) * slope
    gb_ref[...] = jnp.sum(gh, axis=0, keepdims=True)
    gh = gh.astype(BF)
    gs_ref[...] = dot(gt_ref[...], active).astype(BF)
    ge_ref[...] = dot(nt_ref[...], gh).astype(BF)
    more = dot_nt(active, ws_ref[...])
    gmore = dot_nt(gh, we_ref[...])

    @pl.when(step == 0)
    def _():
        acc_ref[...] = more
        gacc_ref[...] = gmore

    @pl.when(step > 0)
    def _():
        acc_ref[...] = acc_ref[...] + more
        gacc_ref[...] = gacc_ref[...] + gmore

    @pl.when(step == pl.num_programs(0) - 1)
    def _():
        out_ref[...] = acc_ref[...].astype(BF)
        gn_ref[...] = gacc_ref[...].astype(BF)


def mlp_backward(n, g, we, ws, be):
    rows, d = n.shape
    hidden = we.shape[1]
    block = 512 if hidden % 512 == 0 else hidden
    return pl.pallas_call(
        mlp_backward_kernel,
        name="mlp_backward",
        out_shape=[
            jax.ShapeDtypeStruct((rows, d), BF),
            jax.ShapeDtypeStruct((rows, d), BF),
            jax.ShapeDtypeStruct((d, hidden), BF),
            jax.ShapeDtypeStruct((d, hidden), BF),
            jax.ShapeDtypeStruct((1, hidden), F32),
        ],
        grid=(hidden // block,),
        in_specs=[
            pl.BlockSpec((rows, d), lambda i: (0, 0)),
            pl.BlockSpec((rows, d), lambda i: (0, 0)),
            pl.BlockSpec((d, block), lambda i: (0, i)),
            pl.BlockSpec((d, block), lambda i: (0, i)),
            pl.BlockSpec((1, block), lambda i: (0, i)),
        ],
        out_specs=[
            pl.BlockSpec((rows, d), lambda i: (0, 0)),
            pl.BlockSpec((rows, d), lambda i: (0, 0)),
            pl.BlockSpec((d, block), lambda i: (0, i)),
            pl.BlockSpec((d, block), lambda i: (0, i)),
            pl.BlockSpec((1, block), lambda i: (0, i)),
        ],
        scratch_shapes=[
            pltpu.VMEM((rows, d), F32),
            pltpu.VMEM((rows, d), F32),
            pltpu.VMEM((d, rows), BF),
            pltpu.VMEM((d, rows), BF),
        ],
        compiler_params=pltpu.CompilerParams(vmem_limit_bytes=40 * MIB),
        cost_estimate=pl.CostEstimate(
            flops=12 * rows * d * hidden,
            transcendentals=rows * hidden,
            bytes_accessed=8 * d * hidden + 8 * rows * d,
        ),
    )(n, g, we, ws, be.reshape(1, hidden))


def statistics(rows):
    mean = jnp.mean(rows, axis=-1, keepdims=True)
    center = rows - mean
    scale = lax.rsqrt(jnp.mean(center * center, axis=-1, keepdims=True) + EPSILON)
    return (center, scale)


def layer_norm(rows, gain, shift):
    center, scale = statistics(rows)
    return (center * scale * gain + shift).astype(BF)


def layer_norm_backward(rows, grad, gain):
    center, scale = statistics(rows)
    unit = center * scale
    e = grad * gain
    back = scale * (
        e
        - jnp.mean(e, axis=-1, keepdims=True)
        - unit * jnp.mean(e * unit, axis=-1, keepdims=True)
    )
    return (back, jnp.sum(grad * unit, axis=0), jnp.sum(grad, axis=0))


def exact_dot(a, b):
    return jnp.dot(a, b, precision=lax.Precision.HIGHEST, preferred_element_type=F32)


def own_first(value, mine):
    return jnp.stack(
        (
            lax.dynamic_index_in_dim(value, mine, 0, keepdims=False),
            lax.dynamic_index_in_dim(value, 1 - mine, 0, keepdims=False),
        )
    )


def shards(
    count,
    embedded,
    segments,
    thoughts,
    cotangent,
    norm_gains,
    norm_shifts,
    joint_weight,
    joint_bias,
    merge_weight,
    expand_weight,
    expand_bias,
    shrink_weight,
    branch_biases,
):
    mine = lax.axis_index("tensor")
    gains = norm_gains.astype(F32)
    shifts = norm_shifts.astype(F32)
    pair_bias = joint_bias.astype(F32)
    expand_shift = expand_bias.astype(F32)
    biases = branch_biases.astype(F32)
    seq, d = embedded.shape
    rows_each = joint_weight.shape[1]
    width = joint_weight.shape[3]
    hidden = expand_weight.shape[2]

    def attend_pack(layer):
        return jnp.concatenate(
            (
                joint_weight[layer].transpose(1, 0, 2).reshape(3 * rows_each, width),
                merge_weight[layer].T,
            ),
            axis=0,
        )

    def mlp_pack(layer):
        return jnp.concatenate((expand_weight[layer], shrink_weight[layer].T), axis=0)

    attend_weights, mlp_weights = [], []
    for layer in range(2):
        held, place = gather_shards(attend_pack(layer), count)
        attend_weights.append(unpack(held, place, (3, 0)))
        held, place = gather_shards(mlp_pack(layer), count)
        mlp_weights.append(unpack(held, place, (0, 0)))

    segs = own_first(segments, mine)
    places = jnp.arange(seq)
    slots = thoughts[0]
    slots_peer = swap(thoughts)[0]
    slot_cols = (places[:, None] == slots[None, :]).astype(F32)
    source_cols = (places[:, None] == (slots - 1)[None, :]).astype(F32)
    source_peer = (places[:, None] == (slots_peer - 1)[None, :]).astype(BF)
    known = (slots >= 1)[:, None]
    occupied = jnp.sum(slot_cols, axis=1)[:, None]
    cot_peer = swap(cotangent)

    def attention(layer, own):
        peer = swap(own)
        wj, wm = attend_weights[layer]
        peer_part, *peer_kept = attend_forward(peer, wj, wm, pair_bias[layer], segs[1])
        got = swap(peer_part)
        own_part, *own_kept = attend_forward(own, wj, wm, pair_bias[layer], segs[0])
        kept = [jnp.stack(both) for both in zip([own] + own_kept, [peer] + peer_kept)]
        return (own_part.astype(F32) + got.astype(F32), kept)

    first = embedded.astype(F32)
    normed = layer_norm(first, gains[0, 0], shifts[0, 0])
    part, kept_one = attention(0, normed)
    middle_one = first + part + biases[0, 0]
    n2_one = layer_norm(middle_one, gains[0, 1], shifts[0, 1])

    slot_count = slots.shape[0]
    pick = source_cols.T
    n2_picked = exact_dot(pick, n2_one.astype(F32)).astype(BF)
    middle_picked = exact_dot(pick, middle_one)
    n2_pair = jnp.concatenate((n2_picked, swap(n2_picked)), axis=0)
    we, ws = mlp_weights[0]
    out = mlp_forward(n2_pair, we, ws, expand_shift[0])
    latent_picked = (
        middle_picked
        + out[:slot_count].astype(F32)
        + swap(out[slot_count:]).astype(F32)
        + biases[0, 1]
    ).astype(BF)
    latent_picked = jnp.where(known, latent_picked, BF(0))
    second = first * (1.0 - occupied) + jnp.dot(
        slot_cols.astype(BF), latent_picked, preferred_element_type=F32
    )

    normed = layer_norm(second, gains[1, 0], shifts[1, 0])
    part, kept_two = attention(1, normed)
    middle_two = second + part + biases[1, 0]
    n2_two = layer_norm(middle_two, gains[1, 1], shifts[1, 1])
    n2_all = jnp.concatenate((n2_two, swap(n2_two)), axis=0)
    g_all = jnp.concatenate((cotangent, cot_peer), axis=0)
    we, ws = mlp_weights[1]
    out, gn, ge_two, gs_two, gb_two = mlp_backward(n2_all, g_all, we, ws, expand_shift[1])
    got = swap(gn[seq:])
    language = middle_two + out[:seq].astype(F32) + swap(out[seq:]).astype(F32) + biases[1, 1]

    def rows_of(array):
        return array.reshape((count, rows_each) + array.shape[1:])

    def reduce_mlp(ge, gs):
        done = reduce_shards(jnp.concatenate((rows_of(ge), rows_of(gs)), axis=1), count)
        return (done[:rows_each], done[rows_each:])

    def reduce_attend(gj, gw):
        done = reduce_shards(
            jnp.concatenate([rows_of(one) for one in (gj[0], gj[1], gj[2], gw)], axis=1), count
        ).reshape(4, rows_each, width)
        return (done[:3], done[3])

    expand_two, shrink_two = reduce_mlp(ge_two, gs_two)

    cot = cotangent.astype(F32)
    back, gain_22, shift_22 = layer_norm_backward(
        middle_two, gn[:seq].astype(F32) + got.astype(F32), gains[1, 1]
    )
    grad_middle = cot + back
    gm = grad_middle.astype(BF)

    def attention_back(layer, gm_pair, kept):
        wj, wm = attend_weights[layer]
        gn, gj, gw, gb = attend_backward(*kept, gm_pair, wj, wm, segs)
        return (gn[0].astype(F32) + swap(gn[1]).astype(F32), gj, gw, gb)

    grad_normed, gj_two, gw_two, pair_two = attention_back(
        1, jnp.stack((gm, swap(gm))), kept_two
    )
    joint_two, merge_two = reduce_attend(gj_two, gw_two)
    back, gain_21, shift_21 = layer_norm_backward(second, grad_normed, gains[1, 0])
    grad_second = grad_middle + back

    g_picked = jnp.where(known, exact_dot(slot_cols.T, grad_second), 0.0)
    g_low = g_picked.astype(BF)
    g_pair = jnp.concatenate((g_low, swap(g_low)), axis=0)
    we, ws = mlp_weights[0]
    _, gn, ge_one, gs_one, gb_one = mlp_backward(n2_pair, g_pair, we, ws, expand_shift[0])
    grad_n2 = gn[:slot_count].astype(F32) + swap(gn[slot_count:]).astype(F32)
    expand_one, shrink_one = reduce_mlp(ge_one, gs_one)
    back, gain_12, shift_12 = layer_norm_backward(middle_picked, grad_n2, gains[0, 1])
    gm_picked = g_picked + back
    gm_low = gm_picked.astype(BF)
    gm_own = jnp.dot(source_cols.astype(BF), gm_low, preferred_element_type=F32).astype(BF)
    gm_peer = jnp.dot(source_peer, swap(gm_low), preferred_element_type=F32).astype(BF)
    grad_normed, gj_one, gw_one, pair_one = attention_back(
        0, jnp.stack((gm_own, gm_peer)), kept_one
    )
    joint_one, merge_one = reduce_attend(gj_one, gw_one)
    back, gain_11, shift_11 = layer_norm_backward(first, grad_normed, gains[0, 0])
    grad_first = exact_dot(source_cols, gm_picked) + back
    embedded_grad = grad_second * (1.0 - occupied) + grad_first

    n2_all = jnp.concatenate((n2_one, swap(n2_one)), axis=0)
    we, ws = mlp_weights[0]
    out = mlp_forward(n2_all, we, ws, expand_shift[0])
    latent = middle_one + out[:seq].astype(F32) + swap(out[seq:]).astype(F32) + biases[0, 1]

    vectors = jnp.stack(
        (
            gain_11, gain_12, gain_21, gain_22,
            shift_11, shift_12, shift_21, shift_22,
            jnp.sum(gm_picked, axis=0), jnp.sum(g_picked, axis=0),
            jnp.sum(grad_middle, axis=0), jnp.sum(cot, axis=0),
        )
    ).reshape(-1)
    vectors = vectors + swap(vectors)
    halves = jnp.concatenate(
        (pair_one.reshape(-1), pair_two.reshape(-1), gb_one.reshape(-1), gb_two.reshape(-1))
    )
    total = sum_everywhere(jnp.concatenate((vectors, halves)), count)
    gains_grad = total[: 4 * d].reshape(2, 2, d)
    shifts_grad = total[4 * d : 8 * d].reshape(2, 2, d)
    branch_grad = total[8 * d : 12 * d].reshape(2, 2, d)
    joint_bias_grad = total[12 * d : 12 * d + 4 * width].reshape(2, 2, width)
    expand_bias_grad = total[12 * d + 4 * width :].reshape(2, hidden)

    return (
        latent.astype(BF),
        language.astype(BF),
        embedded_grad,
        gains_grad,
        shifts_grad,
        jnp.stack((joint_one, joint_two)).transpose(0, 2, 1, 3),
        joint_bias_grad,
        jnp.stack((merge_one, merge_two)).transpose(0, 2, 1),
        jnp.stack((expand_one, expand_two)),
        expand_bias_grad,
        jnp.stack((shrink_one, shrink_two)).transpose(0, 2, 1),
        branch_grad,
    )


def solution(mesh):
    placed = (
        P(("fsdp", "tensor"), None),
        P("fsdp", None),
        P(("fsdp", "tensor"), None),
        P(("fsdp", "tensor"), None),
        P(),
        P(),
        P(None, "fsdp", None, "tensor"),
        P(None, None, "tensor"),
        P(None, "tensor", "fsdp"),
        P(None, "fsdp", "tensor"),
        P(None, "tensor"),
        P(None, "tensor", "fsdp"),
        P(),
    )
    return jax.shard_map(
        partial(shards, mesh.shape["fsdp"]),
        mesh=mesh,
        in_specs=placed,
        out_specs=(
            P(("fsdp", "tensor"), None),
            P(("fsdp", "tensor"), None),
            P(("fsdp", "tensor"), None),
            P(),
            P(),
            P(None, "fsdp", None, "tensor"),
            P(None, None, "tensor"),
            P(None, "tensor", "fsdp"),
            P(None, "fsdp", "tensor"),
            P(None, "tensor"),
            P(None, "tensor", "fsdp"),
            P(),
        ),
        check_vma=False,
    )
```

```python
from functools import partial

import jax
import jax.numpy as jnp
from jax import lax
from jax.experimental import pallas as pl
from jax.experimental.pallas import tpu as pltpu
from jax.sharding import PartitionSpec as P

HEAD = 64
LANES = 128
BLOCK = 48
EPSILON = 1e-05
BF = jnp.bfloat16
F32 = jnp.float32
GELU_C = 0.7978845608028654
GELU_A = 0.044715
MIB = 1 << 20


def dot(a, b):
    return lax.dot_general(a, b, (((1,), (0,)), ((), ())), preferred_element_type=F32)


def dot_nt(a, b):
    return lax.dot_general(a, b, (((1,), (1,)), ((), ())), preferred_element_type=F32)


def dot_tn(a, b):
    return lax.dot_general(a, b, (((0,), (0,)), ((), ())), preferred_element_type=F32)


def vmem(mib):
    return pltpu.CompilerParams(vmem_limit_bytes=mib * MIB)


def cost(flops, moved, exps=0):
    return pl.CostEstimate(flops=flops, transcendentals=exps, bytes_accessed=moved)


VMEM = pl.BlockSpec(memory_space=pltpu.VMEM)


def shape(dims, kind):
    return jax.ShapeDtypeStruct(tuple(dims), kind)


def across(value, count, stride):
    return lax.ppermute(value, "fsdp", [(place, place ^ stride) for place in range(count)])


def swap(value):
    return lax.ppermute(value, "tensor", [(0, 1), (1, 0)])


def after(value, *others):
    leaves, tree = jax.tree.flatten(value)
    held = lax.optimization_barrier(tuple(leaves) + tuple(jax.tree.leaves(others)))
    return jax.tree.unflatten(tree, held[: len(leaves)])


def join_kernel(own_ref, got_ref, out_ref):
    half = out_ref.shape[0] // 2
    for index in range(half):
        out_ref[index] = own_ref[index] if own_ref.ndim == 3 else own_ref[...]
        out_ref[half + index] = got_ref[index] if got_ref.ndim == 3 else got_ref[...]


def join(own, got):
    dims = own.shape[-2:]
    blocks = 2 if own.ndim == 2 else 2 * own.shape[0]
    return pl.pallas_call(
        join_kernel,
        name="join",
        out_shape=shape((blocks,) + dims, BF),
        in_specs=[VMEM] * 2,
        compiler_params=vmem(4),
        cost_estimate=cost(0, 4 * blocks * dims[0] * dims[1]),
    )(own, got)


def load_blocks(bufs, target, columns=None):
    if len(bufs) == 1:
        target[...] = bufs[0][...] if columns is None else bufs[0][:, :, columns]
        return
    me = lax.axis_index("fsdp")
    for number, buf in enumerate(bufs):
        for block in range(buf.shape[0]):
            away = (number // 2) + 2 * (number % 2) + 4 * (block // 2) + 8 * (block % 2)
            at = jnp.bitwise_xor(me, away)
            target[at] = buf[block] if columns is None else buf[block, :, columns]


def store_blocks(value, outs, rows, columns=slice(None)):
    if len(outs) == 1:
        outs[0][:, rows, columns] = value
        return
    pairs = value.reshape((value.shape[0] // 2, 2) + value.shape[1:])
    first = lax.rem(lax.axis_index("fsdp"), 2) == 0
    outs[0][:, rows, columns] = jnp.where(first, pairs[:, 0], pairs[:, 1])
    outs[1][:, rows, columns] = jnp.where(first, pairs[:, 1], pairs[:, 0])


def row_of(ref, layer, which):
    return ref[layer].astype(F32)[which : which + 1, :]


def statistics(rows):
    mean = jnp.mean(rows, axis=-1, keepdims=True)
    center = rows - mean
    scale = lax.rsqrt(jnp.mean(center * center, axis=-1, keepdims=True) + EPSILON)
    return (center * scale, scale)


def norm_backward(rows, grad, gain):
    unit, scale = statistics(rows)
    e = grad * gain
    back = scale * (
        e
        - jnp.mean(e, axis=-1, keepdims=True)
        - unit * jnp.mean(e * unit, axis=-1, keepdims=True)
    )
    return (
        back,
        jnp.sum(grad * unit, axis=0, keepdims=True),
        jnp.sum(grad, axis=0, keepdims=True),
    )


def column(row):
    wide = jnp.broadcast_to(row.astype(F32), (8, row.shape[1]))
    return wide.T[:, 0:1]


def place_rows(slots_ref, less, seq):
    slots = slots_ref.shape[1]
    wanted = column(slots_ref[...]) - float(less)
    places = lax.broadcasted_iota(jnp.int32, (slots, seq), 1).astype(F32)
    return wanted == places


def place_columns(slots_ref, less, seq):
    slots = slots_ref.shape[1]
    wanted = slots_ref[...] - less
    places = lax.broadcasted_iota(jnp.int32, (seq, slots), 0)
    return wanted == places


def ones(hit):
    return jnp.where(hit, 1.0, 0.0).astype(BF)


def exact_pick(hit, value):
    high = value.astype(BF)
    rest = value - high.astype(F32)
    middle = rest.astype(BF)
    low = (rest - middle.astype(F32)).astype(BF)
    return dot(hit, high) + dot(hit, middle) + dot(hit, low)


def start_kernel(jt_ref, mt_ref, x_ref, gain_ref, shift_ref, a_ref, n_ref, x_buf, sems):
    rows = mt_ref.shape[1]
    copies = [
        pltpu.make_async_copy(
            jt_ref.at[0, which], a_ref.at[which * rows : (which + 1) * rows], sems.at[which]
        )
        for which in range(3)
    ]
    copies.append(pltpu.make_async_copy(mt_ref.at[0], a_ref.at[3 * rows : 4 * rows], sems.at[3]))
    copies.append(pltpu.make_async_copy(x_ref, x_buf, sems.at[4]))
    for copy in copies[::-1]:
        copy.start()
    copies[4].wait()
    unit, _ = statistics(x_buf[...].astype(F32))
    n_ref[...] = (unit * row_of(gain_ref, 0, 0) + row_of(shift_ref, 0, 0)).astype(BF)
    for copy in copies[:4]:
        copy.wait()


def start(jt, mt, x, gains, shifts):
    rows, width = mt.shape[1:]
    hbm = pl.BlockSpec(memory_space=pltpu.HBM)
    return pl.pallas_call(
        start_kernel,
        name="start",
        out_shape=[shape((4 * rows, width), BF), shape(x.shape, BF)],
        in_specs=[hbm] * 3 + [VMEM] * 2,
        out_specs=[VMEM] * 2,
        scratch_shapes=[pltpu.VMEM(x.shape, BF), pltpu.SemaphoreType.DMA((5,))],
        compiler_params=vmem(8),
        cost_estimate=cost(0, 8 * rows * width + 4 * x.size),
    )(jt, mt, x, gains, shifts)


def rest_kernel(jt_ref, mt_ref, ex_ref, sh_ref, *refs):
    e0_ref, s0_ref, a1_ref, e1_ref, s1_ref, sems = refs
    rows = mt_ref.shape[1]
    pairs = [(ex_ref.at[0], e0_ref), (sh_ref.at[0], s0_ref)]
    pairs += [(jt_ref.at[1, which], a1_ref.at[which * rows : (which + 1) * rows]) for which in range(3)]
    pairs += [(mt_ref.at[1], a1_ref.at[3 * rows : 4 * rows])]
    pairs += [(ex_ref.at[1], e1_ref), (sh_ref.at[1], s1_ref)]
    copies = [
        pltpu.make_async_copy(source, target, sems.at[index])
        for index, (source, target) in enumerate(pairs)
    ]
    for copy in copies:
        copy.start()
    for copy in copies:
        copy.wait()


def rest(jt, mt, ex, sh):
    rows, width = mt.shape[1:]
    plain = shape((rows, ex.shape[2]), BF)
    return pl.pallas_call(
        rest_kernel,
        name="rest",
        out_shape=[plain, plain, shape((4 * rows, width), BF), plain, plain],
        in_specs=[pl.BlockSpec(memory_space=pltpu.HBM)] * 4,
        out_specs=[VMEM] * 5,
        scratch_shapes=[pltpu.SemaphoreType.DMA((8,))],
        compiler_params=vmem(4),
        cost_estimate=cost(0, 8 * rows * width + 16 * rows * ex.shape[2]),
    )(jt, mt, ex, sh)


def segment_row(seg_ref, peer):
    mine = lax.axis_index("tensor")
    which = (1 - mine) if peer else mine
    both = seg_ref[...].astype(F32)
    row = jnp.where(which == 0, both[0:1, :], both[1:2, :])
    return row


def lane_masks(rows):
    lane = lax.broadcasted_iota(jnp.int32, (rows, LANES), 1)
    return (lane < HEAD, lane >= HEAD)


def attend_forward_kernel(count, layer, peer, arrays, n_ref, seg_ref, bias_ref, *refs):
    bufs = refs[:arrays]
    part_ref, q_ref, k_ref, v_ref, mixed_ref, w_ref, neg_ref = refs[arrays:]
    load_blocks(bufs, w_ref)
    seq, d = n_ref.shape
    width = q_ref.shape[1]
    half = seq // 2
    row = segment_row(seg_ref, peer)
    rows = lax.broadcasted_iota(jnp.int32, (seq, seq), 0)
    cols = lax.broadcasted_iota(jnp.int32, (seq, seq), 1)
    allowed = (column(row) == row) & (cols <= rows)
    neg_ref[...] = jnp.where(allowed, 0.0, -1e30)
    n = n_ref[...]

    def weight(which):
        return w_ref[:, which * BLOCK : (which + 1) * BLOCK, :].reshape(d, width)

    q_ref[...] = (dot(n, weight(0)) + row_of(bias_ref, layer, 0)).astype(BF)
    k_ref[...] = dot(n, weight(1)).astype(BF)
    v_ref[...] = (dot(n, weight(2)) + row_of(bias_ref, layer, 1)).astype(BF)
    masks = lane_masks(half)
    for pair in range(width // LANES):
        lanes = slice(pair * LANES, (pair + 1) * LANES)
        for part in range(2):
            top = slice(part * half, (part + 1) * half)
            keys = slice(0, (part + 1) * half)
            qp = q_ref[top, lanes] * BF(HEAD ** (-0.5))
            kp = k_ref[keys, lanes]
            vp = v_ref[keys, lanes]
            found = []
            for mask in masks:
                s = dot_nt(jnp.where(mask, qp, BF(0)), kp) + neg_ref[top, keys]
                e = jnp.exp(s - jnp.max(s, axis=-1, keepdims=True))
                scale = 1.0 / jnp.sum(e, axis=-1, keepdims=True)
                found.append(dot((e * scale).astype(BF), vp))
            mixed_ref[top, lanes] = jnp.where(masks[0], found[0], found[1]).astype(BF)
    part_ref[...] = dot_nt(mixed_ref[...], weight(3)).astype(BF)


def attend_forward(count, layer, peer, n, segments, bias, bufs):
    seq, d = n.shape
    width = bufs[0].shape[-1]
    rows = shape((seq, width), BF)
    return pl.pallas_call(
        partial(attend_forward_kernel, count, layer, peer, len(bufs)),
        name="attend_forward",
        out_shape=[shape((seq, d), BF), rows, rows, rows, rows],
        in_specs=[VMEM] * (3 + len(bufs)),
        scratch_shapes=[
            pltpu.VMEM((d // BLOCK, 4 * BLOCK, width), BF),
            pltpu.VMEM((seq, seq), F32),
        ],
        compiler_params=vmem(16),
        cost_estimate=cost(
            8 * seq * d * width + 4 * seq * seq * width,
            8 * d * width + 4 * seq * d + 8 * seq * width,
            seq * seq * width // HEAD,
        ),
    )(n, segments, bias, *bufs)


def attend_backward_kernel(
    count, layer, peer, picked, arrays,
    q_ref, k_ref, v_ref, gm_ref, seg_ref, slots_ref, *refs,
):
    bufs = refs[:arrays]
    refs = refs[arrays:]
    if picked:
        gn_ref, dj_ref, gb_ref, wide_ref, w_ref, neg_ref, gx_ref, qx_ref = refs
    else:
        gn_ref, dj_ref, gb_ref, w_ref, neg_ref, gx_ref = refs
    load_blocks(bufs, w_ref)
    seq, width = q_ref.shape
    d = gm_ref.shape[1]
    half = seq // 2
    row = segment_row(seg_ref, peer)
    if picked:
        slots = gm_ref.shape[0]
        hit = place_rows(slots_ref, 1, seq)
        at = column(slots_ref[...]) - 1.0
        own = jnp.sum(jnp.where(hit, row, 0.0), axis=-1, keepdims=True)
        cols = lax.broadcasted_iota(jnp.int32, (slots, seq), 1).astype(F32)
        neg_ref[...] = jnp.where((own == row) & (cols <= at), 0.0, -1e30)
        qx_ref[...] = dot(ones(hit), q_ref[...]).astype(BF)
        parts = [(slice(0, slots), slice(0, seq))]
        queries = qx_ref
    else:
        rows = lax.broadcasted_iota(jnp.int32, (seq, seq), 0)
        cols = lax.broadcasted_iota(jnp.int32, (seq, seq), 1)
        allowed = (column(row) == row) & (cols <= rows)
        neg_ref[...] = jnp.where(allowed, 0.0, -1e30)
        parts = [
            (slice(part * half, (part + 1) * half), slice(0, (part + 1) * half))
            for part in range(2)
        ]
        queries = q_ref

    def weight(which):
        return w_ref[:, which * BLOCK : (which + 1) * BLOCK, :].reshape(d, width)

    gx_ref[...] = dot(gm_ref[...], weight(3)).astype(BF)
    if picked:
        back = ones(place_columns(slots_ref, 1, seq))
        wide_ref[...] = dot(back, gm_ref[...]).astype(BF)
    masks = lane_masks(parts[0][0].stop)
    for pair in range(width // LANES):
        lanes = slice(pair * LANES, (pair + 1) * LANES)
        dk = [None, None]
        dv = [None, None]
        dq_all = []
        for top, keys in parts:
            qp = queries[top, lanes]
            kp = k_ref[keys, lanes]
            vp = v_ref[keys, lanes]
            gp = gx_ref[top, lanes]
            dq, dk_now, dv_now = [], [], []
            for mask in masks:
                qm = jnp.where(mask, qp, BF(0)) * BF(HEAD ** (-0.5))
                s = dot_nt(qm, kp) + neg_ref[top, keys]
                e = jnp.exp(s - jnp.max(s, axis=-1, keepdims=True))
                p = e * (1.0 / jnp.sum(e, axis=-1, keepdims=True))
                gprobs = dot_nt(jnp.where(mask, gp, BF(0)), vp)
                inner = jnp.sum(gprobs * p, axis=-1, keepdims=True)
                ds = (p * (gprobs - inner) * HEAD ** (-0.5)).astype(BF)
                dq.append(dot(ds, kp))
                dk_now.append(dot_tn(ds, qp))
                dv_now.append(dot_tn(p.astype(BF), gp))
            dq_all.append(jnp.where(masks[0], dq[0], dq[1]))
            key_mask = lane_masks(half)[0]
            for block in range(keys.stop // half):
                at = slice(block * half, (block + 1) * half)
                k_new = jnp.where(key_mask, dk_now[0][at], dk_now[1][at])
                v_new = jnp.where(key_mask, dv_now[0][at], dv_now[1][at])
                dk[block] = k_new if dk[block] is None else dk[block] + k_new
                dv[block] = v_new if dv[block] is None else dv[block] + v_new
        gb_ref[0:1, lanes] = sum(jnp.sum(one, axis=0, keepdims=True) for one in dq_all)
        gb_ref[1:2, lanes] = sum(jnp.sum(one, axis=0, keepdims=True) for one in dv)
        if picked:
            dj_ref[0, :, lanes] = dot(back, dq_all[0].astype(BF)).astype(BF)
        else:
            for (top, _), one in zip(parts, dq_all):
                dj_ref[0, top, lanes] = one.astype(BF)
        for block in range(2):
            at = slice(block * half, (block + 1) * half)
            dj_ref[1, at, lanes] = dk[block].astype(BF)
            dj_ref[2, at, lanes] = dv[block].astype(BF)
    gn = dot_nt(dj_ref[0], weight(0))
    gn = gn + dot_nt(dj_ref[1], weight(1))
    gn = gn + dot_nt(dj_ref[2], weight(2))
    gn_ref[...] = gn.astype(BF)


def attend_backward(count, layer, peer, kept, gm, segments, slots, bufs, picked):
    q, k, v = kept
    seq, width = q.shape
    rows, d = gm.shape
    outs = [shape((seq, d), BF), shape((3, seq, width), BF), shape((2, width), F32)]
    scratch = [
        pltpu.VMEM((d // BLOCK, 4 * BLOCK, width), BF),
        pltpu.VMEM((rows, seq), F32),
        pltpu.VMEM((rows, width), BF),
    ]
    if picked:
        outs.append(shape((seq, d), BF))
        scratch.append(pltpu.VMEM((rows, width), BF))
    return pl.pallas_call(
        partial(attend_backward_kernel, count, layer, peer, picked, len(bufs)),
        name="attend_backward",
        out_shape=outs,
        in_specs=[VMEM] * (6 + len(bufs)),
        scratch_shapes=scratch,
        compiler_params=vmem(16),
        cost_estimate=cost(
            2 * rows * d * width + 6 * seq * d * width + 10 * rows * seq * width,
            8 * d * width + 4 * seq * d + 12 * seq * width,
            rows * seq * width // HEAD,
        ),
    )(q, k, v, gm, segments, slots, *bufs)


def attend_grads_kernel(n0_ref, n1_ref, d0_ref, d1_ref, g0_ref, g1_ref, m0_ref, m1_ref, *outs):
    d = n0_ref.shape[1]
    width = m0_ref.shape[1]
    groups = d // BLOCK
    nt = [n0_ref[...].T, n1_ref[...].T]
    for which in range(3):
        total = dot(nt[0], d0_ref[which]) + dot(nt[1], d1_ref[which])
        store_blocks(
            total.astype(BF).reshape(groups, BLOCK, width),
            outs,
            slice(which * BLOCK, (which + 1) * BLOCK),
        )
    total = dot(g0_ref[...].T, m0_ref[...]) + dot(g1_ref[...].T, m1_ref[...])
    store_blocks(
        total.astype(BF).reshape(groups, BLOCK, width), outs, slice(3 * BLOCK, 4 * BLOCK)
    )


def grad_shapes(count, groups, rows, width, split):
    if split:
        return [shape((count // 2, rows, width), BF)] * 2
    return [shape((groups, rows, width), BF)]


def attend_grads(count, split, n, dj, gm, mixed):
    seq, d = n[0].shape
    width = mixed[0].shape[1]
    outs = grad_shapes(count, d // BLOCK, 4 * BLOCK, width, split)
    return pl.pallas_call(
        attend_grads_kernel,
        name="attend_grads",
        out_shape=outs,
        in_specs=[VMEM] * 8,
        compiler_params=vmem(16),
        cost_estimate=cost(16 * seq * d * width, 16 * d * width + 8 * seq * d),
    )(*n, *dj, *gm, *mixed)


def chunk_of(hidden):
    return 512 if hidden % 512 == 0 else hidden


def mlp_forward_kernel(count, layer, arrays, n0_ref, n1_ref, be_ref, *refs):
    e_bufs, s_bufs = refs[:arrays], refs[arrays : 2 * arrays]
    out0_ref, out1_ref, n_ref, acc_ref, we_ref, ws_ref = refs[2 * arrays :]
    rows, d = n0_ref.shape
    hidden = e_bufs[0].shape[2]
    chunk = chunk_of(hidden)
    n_ref[:rows, :] = n0_ref[...]
    n_ref[rows:, :] = n1_ref[...]
    acc_ref[...] = jnp.zeros_like(acc_ref)

    @pl.loop(0, hidden // chunk)
    def _(index):
        cols = pl.ds(pl.multiple_of(index * chunk, chunk), chunk)
        load_blocks(e_bufs, we_ref, cols)
        load_blocks(s_bufs, ws_ref, cols)
        shift = be_ref[:, cols].astype(F32)[layer : layer + 1, :]
        u = dot(n_ref[...], we_ref[...].reshape(d, chunk)) + shift
        t = jnp.tanh(GELU_C * (u + GELU_A * (u * u * u)))
        active = (0.5 * u * (1.0 + t)).astype(BF)
        acc_ref[...] = acc_ref[...] + dot_nt(active, ws_ref[...].reshape(d, chunk))

    out0_ref[...] = acc_ref[:rows, :].astype(BF)
    out1_ref[...] = acc_ref[rows:, :].astype(BF)


def mlp_forward(count, layer, n, be, e_bufs, s_bufs):
    rows, d = n[0].shape
    hidden = e_bufs[0].shape[-1]
    return pl.pallas_call(
        partial(mlp_forward_kernel, count, layer, len(e_bufs)),
        name="mlp_forward",
        out_shape=[shape((rows, d), BF)] * 2,
        in_specs=[VMEM] * (3 + 2 * len(e_bufs)),
        scratch_shapes=[
            pltpu.VMEM((2 * rows, d), BF),
            pltpu.VMEM((2 * rows, d), F32),
            pltpu.VMEM((d // BLOCK, BLOCK, chunk_of(hidden)), BF),
            pltpu.VMEM((d // BLOCK, BLOCK, chunk_of(hidden)), BF),
        ],
        compiler_params=vmem(16),
        cost_estimate=cost(
            8 * rows * d * hidden, 4 * d * hidden + 8 * rows * d, 2 * rows * hidden
        ),
    )(*n, be, *e_bufs, *s_bufs)


def mlp_backward_kernel(count, layer, arrays, full, outputs, n0_ref, n1_ref, g0_ref, g1_ref, be_ref, *refs):
    e_bufs, s_bufs = refs[:arrays], refs[arrays : 2 * arrays]
    refs = refs[2 * arrays :]
    if full:
        out0_ref, out1_ref, refs = refs[0], refs[1], refs[2:]
    gn0_ref, gn1_ref, gb_ref = refs[:3]
    outs = refs[3 : 3 + outputs]
    refs = refs[3 + outputs :]
    n_ref, g_ref, nt_ref, gt_ref, gacc_ref, we_ref, ws_ref = refs[:7]
    if full:
        acc_ref = refs[7]
    rows, d = n0_ref.shape
    hidden = e_bufs[0].shape[2]
    chunk = chunk_of(hidden)
    groups = d // BLOCK
    n_ref[:rows, :] = n0_ref[...]
    n_ref[rows:, :] = n1_ref[...]
    g_ref[:rows, :] = g0_ref[...]
    g_ref[rows:, :] = g1_ref[...]
    nt_ref[...] = n_ref[...].T
    gt_ref[...] = g_ref[...].T
    gacc_ref[...] = jnp.zeros_like(gacc_ref)
    if full:
        acc_ref[...] = jnp.zeros_like(acc_ref)

    @pl.loop(0, hidden // chunk)
    def _(index):
        cols = pl.ds(pl.multiple_of(index * chunk, chunk), chunk)
        load_blocks(e_bufs, we_ref, cols)
        load_blocks(s_bufs, ws_ref, cols)
        we = we_ref[...].reshape(d, chunk)
        ws = ws_ref[...].reshape(d, chunk)
        shift = be_ref[:, cols].astype(F32)[layer : layer + 1, :]
        u = dot(n_ref[...], we) + shift
        square = u * u
        t = jnp.tanh(GELU_C * (u + GELU_A * (square * u)))
        lean = 0.5 * (1.0 + t)
        active = (u * lean).astype(BF)
        slope = lean + (0.5 * u) * (1.0 - t * t) * (GELU_C + (3.0 * GELU_C * GELU_A) * square)
        gh = dot(g_ref[...], ws) * slope
        gb_ref[:, cols] = jnp.sum(gh, axis=0, keepdims=True)
        gh = gh.astype(BF)
        ge = dot(nt_ref[...], gh).astype(BF)
        gs = dot(gt_ref[...], active).astype(BF)
        store_blocks(ge.reshape(groups, BLOCK, chunk), outs, slice(0, BLOCK), cols)
        store_blocks(gs.reshape(groups, BLOCK, chunk), outs, slice(BLOCK, 2 * BLOCK), cols)
        gacc_ref[...] = gacc_ref[...] + dot_nt(gh, we)
        if full:
            acc_ref[...] = acc_ref[...] + dot_nt(active, ws)

    gn0_ref[...] = gacc_ref[:rows, :].astype(BF)
    gn1_ref[...] = gacc_ref[rows:, :].astype(BF)
    if full:
        out0_ref[...] = acc_ref[:rows, :].astype(BF)
        out1_ref[...] = acc_ref[rows:, :].astype(BF)


def mlp_backward(count, layer, split, n, g, be, e_bufs, s_bufs, full):
    rows, d = n[0].shape
    hidden = e_bufs[0].shape[-1]
    groups = d // BLOCK
    half = shape((rows, d), BF)
    grads = grad_shapes(count, groups, 2 * BLOCK, hidden, split)
    blocks = pltpu.VMEM((groups, BLOCK, chunk_of(hidden)), BF)
    return pl.pallas_call(
        partial(mlp_backward_kernel, count, layer, len(e_bufs), full, len(grads)),
        name="mlp_backward",
        out_shape=[half] * (4 if full else 2) + [shape((1, hidden), F32)] + grads,
        in_specs=[VMEM] * (5 + 2 * len(e_bufs)),
        scratch_shapes=[
            pltpu.VMEM((2 * rows, d), BF),
            pltpu.VMEM((2 * rows, d), BF),
            pltpu.VMEM((d, 2 * rows), BF),
            pltpu.VMEM((d, 2 * rows), BF),
            pltpu.VMEM((2 * rows, d), F32),
            blocks,
            blocks,
        ]
        + ([pltpu.VMEM((2 * rows, d), F32)] if full else []),
        compiler_params=vmem(28),
        cost_estimate=cost(
            (24 if full else 20) * rows * d * hidden,
            8 * d * hidden + 16 * rows * d,
            2 * rows * hidden,
        ),
    )(*n, *g, be, *e_bufs, *s_bufs)


def middle_kernel(layer, x_ref, own_ref, got_ref, slots_ref, gain_ref, shift_ref, bias_ref, *outs):
    middle = (
        x_ref[...].astype(F32)
        + (own_ref[...].astype(F32) + got_ref[...].astype(F32))
        + row_of(bias_ref, layer, 0)
    )
    unit, _ = statistics(middle)
    normed = (unit * row_of(gain_ref, layer, 1) + row_of(shift_ref, layer, 1)).astype(BF)
    outs[0][...] = middle
    outs[1][...] = normed
    if layer == 0:
        hit = ones(place_rows(slots_ref, 1, x_ref.shape[0]))
        outs[2][...] = exact_pick(hit, middle)
        outs[3][...] = dot(hit, normed).astype(BF)


def second_kernel(
    x_ref, mid_ref, own_ref, got_ref, slots_ref, gain_ref, shift_ref, bias_ref, out_ref, n_ref
):
    seq = x_ref.shape[0]
    latent = (
        mid_ref[...]
        + (own_ref[...].astype(F32) + got_ref[...].astype(F32))
        + row_of(bias_ref, 0, 1)
    )
    known = column(slots_ref[...]) >= 1.0
    latent = jnp.where(known, latent, 0.0).astype(BF)
    hit = place_columns(slots_ref, 0, seq)
    occupied = jnp.sum(jnp.where(hit, 1.0, 0.0), axis=-1, keepdims=True)
    second = x_ref[...].astype(F32) * (1.0 - occupied) + dot(ones(hit), latent)
    unit, _ = statistics(second)
    out_ref[...] = second
    n_ref[...] = (unit * row_of(gain_ref, 1, 0) + row_of(shift_ref, 1, 0)).astype(BF)


def grad_middle_kernel(mid_ref, own_ref, got_ref, cot_ref, gain_ref, out_ref, low_ref, sum_ref):
    cot = cot_ref[...].astype(F32)
    grad = own_ref[...].astype(F32) + got_ref[...].astype(F32)
    back, gain, shift = norm_backward(mid_ref[...], grad, row_of(gain_ref, 1, 1))
    total = cot + back
    out_ref[...] = total
    low_ref[...] = total.astype(BF)
    sum_ref[0:1, :] = gain
    sum_ref[1:2, :] = shift
    sum_ref[2:3, :] = jnp.sum(total, axis=0, keepdims=True)
    sum_ref[3:4, :] = jnp.sum(cot, axis=0, keepdims=True)


def grad_second_kernel(
    x_ref, own_ref, got_ref, gm_ref, slots_ref, gain_ref, out_ref, pick_ref, low_ref, sum_ref
):
    grad = own_ref[...].astype(F32) + got_ref[...].astype(F32)
    back, gain, shift = norm_backward(x_ref[...], grad, row_of(gain_ref, 1, 0))
    total = gm_ref[...] + back
    out_ref[...] = total
    hit = place_rows(slots_ref, 0, x_ref.shape[0])
    known = column(slots_ref[...]) >= 1.0
    pick = jnp.where(known, exact_pick(ones(hit), total), 0.0)
    pick_ref[...] = pick
    low_ref[...] = pick.astype(BF)
    sum_ref[0:1, :] = gain
    sum_ref[1:2, :] = shift


def grad_picked_kernel(mid_ref, own_ref, got_ref, pick_ref, gain_ref, out_ref, low_ref, sum_ref):
    grad = own_ref[...].astype(F32) + got_ref[...].astype(F32)
    back, gain, shift = norm_backward(mid_ref[...], grad, row_of(gain_ref, 0, 1))
    pick = pick_ref[...]
    total = pick + back
    out_ref[...] = total
    low_ref[...] = total.astype(BF)
    sum_ref[0:1, :] = gain
    sum_ref[1:2, :] = shift
    sum_ref[2:3, :] = jnp.sum(total, axis=0, keepdims=True)
    sum_ref[3:4, :] = jnp.sum(pick, axis=0, keepdims=True)


def grad_first_kernel(
    x_ref, own_ref, got_ref, gm_ref, second_ref, slots_ref, gain_ref,
    s22_ref, s21_ref, s12_ref, pair1_ref, pair0_ref, peer1_ref, peer0_ref, be1_ref, be0_ref,
    out_ref, sum_ref,
):
    seq, d = x_ref.shape
    grad = own_ref[...].astype(F32) + got_ref[...].astype(F32)
    back, gain, shift = norm_backward(x_ref[...].astype(F32), grad, row_of(gain_ref, 0, 0))
    hit = place_columns(slots_ref, 0, seq)
    occupied = jnp.sum(jnp.where(hit, 1.0, 0.0), axis=-1, keepdims=True)
    source = ones(place_columns(slots_ref, 1, seq))
    out_ref[...] = second_ref[...] * (1.0 - occupied) + (exact_pick(source, gm_ref[...]) + back)
    width = pair0_ref.shape[1]
    for index, row in enumerate(
        (
            gain, s12_ref[0:1, :], s21_ref[0:1, :], s22_ref[0:1, :],
            shift, s12_ref[1:2, :], s21_ref[1:2, :], s22_ref[1:2, :],
            s12_ref[2:3, :], s12_ref[3:4, :], s22_ref[2:3, :], s22_ref[3:4, :],
        )
    ):
        for part in range(d // width):
            at = index * (d // width) + part
            sum_ref[at : at + 1, :] = row[:, part * width : (part + 1) * width]
    first = 12 * (d // width)
    sum_ref[first : first + 2, :] = pair0_ref[...] + peer0_ref[...]
    sum_ref[first + 2 : first + 4, :] = pair1_ref[...] + peer1_ref[...]
    hidden = be0_ref.shape[1]
    for layer, ref in enumerate((be0_ref, be1_ref)):
        for part in range(hidden // width):
            at = first + 4 + layer * (hidden // width) + part
            sum_ref[at : at + 1, :] = ref[0:1, part * width : (part + 1) * width]


def vectors_kernel(sum_ref, gains_ref, shifts_ref, branch_ref, pair_ref, hidden_ref):
    d = gains_ref.shape[2]
    width = sum_ref.shape[1]
    index = 0
    for ref in (gains_ref, shifts_ref, branch_ref):
        for layer in range(2):
            for which in range(2):
                for part in range(d // width):
                    ref[layer, which : which + 1, part * width : (part + 1) * width] = sum_ref[
                        index : index + 1, :
                    ]
                    index += 1
    for layer in range(2):
        pair_ref[layer] = sum_ref[index : index + 2, :]
        index += 2
    for layer in range(2):
        for part in range(hidden_ref.shape[1] // width):
            hidden_ref[layer : layer + 1, part * width : (part + 1) * width] = sum_ref[
                index : index + 1, :
            ]
            index += 1


def small(kernel, name, outs, *args):
    moved = sum(a.size * a.dtype.itemsize for a in args) + sum(
        o.size * o.dtype.itemsize for o in outs
    )
    return pl.pallas_call(
        kernel,
        name=name,
        out_shape=outs,
        in_specs=[VMEM] * len(args),
        compiler_params=vmem(24),
        cost_estimate=cost(4 * moved, moved),
    )(*args)


def split_kernel(stride, keep_ref, got_ref, kept_ref, sent_ref):
    bit = lax.rem(lax.axis_index("fsdp") // stride, 2)
    for index in range(kept_ref.shape[0]):
        for out, place in ((kept_ref, bit), (sent_ref, 1 - bit)):
            at = 2 * index + place
            out[index] = (keep_ref[at].astype(F32) + got_ref[at].astype(F32)).astype(BF)


def split(keep, got, stride):
    blocks, rows, width = keep.shape
    return pl.pallas_call(
        partial(split_kernel, stride),
        name="split",
        out_shape=[shape((blocks // 2, rows, width), BF)] * 2,
        in_specs=[VMEM] * 2,
        compiler_params=vmem(8),
        cost_estimate=cost(keep.size, 6 * keep.size),
    )(keep, got)


def finish_kernel(kinds, *refs):
    outs = refs[-len(kinds) :]
    each = (len(refs) - len(outs)) // 2
    for layer in range(2):
        parts = refs[layer * each : (layer + 1) * each]
        total = parts[0][0].astype(F32)
        for part in parts[1:]:
            total = total + part[0].astype(F32)
        rows = total.shape[0] // sum(kinds)
        first = 0
        for kind, out in zip(kinds, outs):
            for which in range(kind):
                piece = total[first : first + rows, :]
                if kind == 1:
                    out[layer] = piece
                else:
                    out[layer, which] = piece
                first += rows


def finish(kinds, *states):
    _, rows, width = states[0][0].shape
    each = rows // sum(kinds)
    outs = [
        shape((2, each, width) if kind == 1 else (2, kind, each, width), F32) for kind in kinds
    ]
    return small(partial(finish_kernel, kinds), "finish", outs, *states[0], *states[1])


def sum_everywhere(value, count):
    stride = 1
    while stride < count and count % (2 * stride) == 0:
        pairs = [(source, source ^ stride) for source in range(count)]
        value = value + lax.ppermute(value, "fsdp", pairs)
        stride *= 2
    if stride < count:
        groups = [list(range(first, count, stride)) for first in range(stride)]
        value = lax.psum(value, "fsdp", axis_index_groups=groups)
    return value


def regroup(array, count, kinds):
    rows = array.shape[0] * array.shape[1] // kinds // BLOCK
    each = array.shape[1] // kinds
    width = array.shape[2]
    split = array.reshape(array.shape[0], kinds, each, width).transpose(1, 0, 2, 3)
    return split.reshape(kinds, rows, BLOCK, width).transpose(1, 0, 2, 3).reshape(
        rows, kinds * BLOCK, width
    )


def ungroup(array, count, kinds):
    width = array.shape[2]
    split = array.reshape(array.shape[0], kinds, BLOCK, width).transpose(1, 0, 2, 3)
    each = array.shape[0] * BLOCK // count
    return split.reshape(kinds, count, each, width).transpose(1, 0, 2, 3).reshape(
        count, kinds * each, width
    )


def shards(
    count,
    embedded,
    segments,
    thoughts,
    cotangent,
    gains,
    shifts,
    joint_weight,
    joint_bias,
    merge_weight,
    expand_weight,
    expand_bias,
    shrink_weight,
    branch_biases,
):
    seq, d = embedded.shape
    rows_each = joint_weight.shape[1]
    width = joint_weight.shape[3]
    hidden = expand_weight.shape[2]
    slots = thoughts.shape[1]
    staged = rows_each == BLOCK and count == 16
    rows_f32, rows_bf = shape((seq, d), F32), shape((seq, d), BF)
    few_f32, few_bf = shape((slots, d), F32), shape((slots, d), BF)
    ins = (
        joint_weight.transpose(0, 2, 1, 3),
        merge_weight.transpose(0, 2, 1),
        expand_weight,
        shrink_weight.transpose(0, 2, 1),
    )
    shard, parts, joined, bufs = {}, {}, {}, {}

    def fetch(name, *others):
        if staged:
            own = after(shard[name], *others)
            parts[name] = join(own, across(own, count, 8))
        return parts.get(name, ())

    def further(name, *others):
        if staged:
            own = after(parts[name], *others)
            joined[name] = join(own, across(own, count, 4))
        return joined.get(name, ())

    def arrive(name, *others):
        if staged:
            own = after(joined[name], *others)
            got = across(own, count, 2)
            bufs[name] = [own, got, across(own, count, 1), across(got, count, 1)]

    if staged:
        shard["a0"], normed = start(*ins[:2], embedded, gains, shifts)
        for name, one in zip(("e0", "s0", "a1", "e1", "s1"), rest(*ins)):
            shard[name] = one
    else:
        first = embedded.astype(F32)
        center = first - jnp.mean(first, axis=-1, keepdims=True)
        scale = lax.rsqrt(jnp.mean(center * center, axis=-1, keepdims=True) + EPSILON)
        normed = (
            center * scale * gains[0, 0].astype(F32) + shifts[0, 0].astype(F32)
        ).astype(BF)
        for layer in range(2):
            attend = jnp.concatenate(
                (ins[0][layer].reshape(3 * rows_each, width), ins[1][layer]), axis=0
            )
            for name, one, kind in (("a", attend, 4), ("e", ins[2][layer], 1), ("s", ins[3][layer], 1)):
                whole = lax.all_gather(one, "fsdp", axis=0, tiled=False)
                bufs[f"{name}{layer}"] = [regroup(whole, count, kind)]

    slots_peer = swap(thoughts)
    normed_peer = swap(normed)
    cot_peer = swap(after(cotangent, normed_peer))

    def attention(layer, own, peer, *others):
        weights = bufs[f"a{layer}"]
        part_peer, *kept_peer = attend_forward(count, layer, True, peer, segments, joint_bias, weights)
        got = swap(part_peer)
        part_own, *kept_own = attend_forward(
            count, layer, False, after(own, part_peer, *others), segments, joint_bias, weights
        )
        return (part_own, got, (own, peer), (kept_own, kept_peer))

    here = fetch("a0")
    here = fetch("e0", here)
    further("a0", shard.get("e0", ()))
    arrive("a0")
    ready = further("e0")
    here = fetch("s0", here)
    part, got, n_one, kept_one = attention(0, normed, after(normed_peer, ready), here)
    arrive("e0")
    ready = further("s0")
    here = fetch("a1", here)
    middle_one, n2_one, middle_few, n2_few = small(
        partial(middle_kernel, 0), "middle", [rows_f32, rows_bf, few_f32, few_bf],
        embedded, after(part, ready), got, thoughts, gains, shifts, branch_biases,
    )
    n2_few = (n2_few, swap(n2_few))
    n2_all = (n2_one, swap(after(n2_one, n2_few[1])))
    arrive("s0")
    ready = further("a1")
    here = fetch("e1", here)
    own, peer = mlp_forward(count, 0, after(n2_few, ready), expand_bias, bufs["e0"], bufs["s0"])
    second, normed = small(
        second_kernel, "second", [rows_f32, rows_bf],
        embedded, middle_few, after(own, here), swap(peer), thoughts, gains, shifts, branch_biases,
    )

    arrive("a1")
    ready = further("e1")
    here = fetch("s1", here)
    part, got, n_two, kept_two = attention(1, normed, after(swap(normed), ready, here))
    arrive("e1")
    ready = further("s1")
    middle_two, n2_two = small(
        partial(middle_kernel, 1), "middle", [rows_f32, rows_bf],
        second, after(part, ready), got, thoughts, gains, shifts, branch_biases,
    )
    arrive("s1")
    n2_peer = swap(n2_two)
    latent_own, latent_peer = mlp_forward(
        count, 0, after(n2_all, n2_two), expand_bias, bufs["e0"], bufs["s0"]
    )
    own_two, peer_two, gn_own, gn_peer, gb_two, *m1 = mlp_backward(
        count, 1, staged, (n2_two, after(n2_peer, latent_own)), (cotangent, cot_peer),
        expand_bias, bufs["e1"], bufs["s1"], True,
    )
    latent_got = swap(after(latent_peer, n2_peer))

    def core_step(grads, kind):
        if staged:
            return (grads[0], across(grads[1], count, 1))
        done = lax.psum_scatter(
            ungroup(grads[0], count, kind), "fsdp", scatter_dimension=0, tiled=False
        )
        return (done[None],)

    def send(state, stride):
        return split(*state, stride) if staged else state

    def move(state, stride):
        return (state[0], across(state[1], count, stride)) if staged else state

    got = swap(gn_peer)
    m1 = core_step(m1, 2)
    gm, gm_low, s22 = small(
        grad_middle_kernel, "grad_middle", [rows_f32, rows_bf, shape((4, d), F32)],
        middle_two, after(gn_own, m1), got, cotangent, gains,
    )
    gm_peer = swap(gm_low)
    m1 = send(m1, 2)
    weights = bufs["a1"]
    back_peer = attend_backward(
        count, 1, True, kept_two[1][:3], after(gm_peer, m1), segments, slots_peer, weights, False
    )
    m1 = move(m1, 2)
    got = swap(back_peer[0])
    back_own = attend_backward(
        count, 1, False, kept_two[0][:3], after(gm_low, back_peer[0]), segments, thoughts, weights, False
    )
    a1 = attend_grads(
        count, staged, n_two, (back_own[1], back_peer[1]), (gm_low, gm_peer),
        (kept_two[0][3], kept_two[1][3]),
    )
    grad_second, g_few, g_low, s21 = small(
        grad_second_kernel, "grad_second", [rows_f32, few_f32, few_bf, shape((2, d), F32)],
        second, after(back_own[0], a1), got, gm, thoughts, gains,
    )
    pair_two = (back_own[2], back_peer[2])
    a1 = core_step(a1, 4)
    m1 = send(m1, 4)

    own, peer, gb_one, *m0 = mlp_backward(
        count, 0, staged, n2_few, (g_low, after(swap(g_low), m1, a1)), expand_bias,
        bufs["e0"], bufs["s0"], False,
    )
    m1 = move(m1, 4)
    a1 = send(a1, 2)
    m0 = core_step(m0, 2)
    gm_few, gm_low, s12 = small(
        grad_picked_kernel, "grad_picked", [few_f32, few_bf, shape((4, d), F32)],
        middle_few, after(own, a1), swap(peer), g_few, gains,
    )
    a1 = move(a1, 2)
    m0 = send(m0, 2)
    m1 = send(m1, 8)
    weights = bufs["a0"]
    back_peer = attend_backward(
        count, 0, True, kept_one[1][:3], after(swap(gm_low), m0, m1), segments, slots_peer, weights, True
    )
    m1 = move(m1, 8)
    m0 = move(m0, 2)
    got = swap(back_peer[0])
    back_own = attend_backward(
        count, 0, False, kept_one[0][:3], after(gm_low, back_peer[0]), segments, thoughts, weights, True
    )
    a1 = send(a1, 4)
    a0 = attend_grads(
        count, staged, n_one, (after(back_own[1], a1), back_peer[1]), (back_own[3], back_peer[3]),
        (kept_one[0][3], kept_one[1][3]),
    )
    a1 = move(a1, 4)
    pair_one = (back_own[2], back_peer[2])
    a0 = core_step(a0, 4)
    embedded_grad, vectors = small(
        grad_first_kernel, "grad_first",
        [rows_f32, shape((12 * d // width + 4 + 2 * (hidden // width), width), F32)],
        embedded, back_own[0], got, gm_few, grad_second, thoughts, gains,
        s22, s21, s12, pair_two[0], pair_one[0], pair_two[1], pair_one[1], gb_two, gb_one,
    )
    a1 = move(send(a1, 8), 8)
    a0 = move(send(a0, 2), 2)
    m0 = move(send(m0, 4), 4)
    m0 = move(send(m0, 8), 8)
    a0 = move(send(a0, 4), 4)
    a0 = move(send(a0, 8), 8)

    biases = branch_biases.astype(F32)
    latent = middle_one + (latent_own.astype(F32) + latent_got.astype(F32)) + biases[0, 1]
    language = middle_two + (own_two.astype(F32) + swap(peer_two).astype(F32)) + biases[1, 1]

    joint_grad, merge_grad = finish((3, 1), a0, a1)
    expand_grad, shrink_grad = finish((1, 1), m0, m1)
    shared = jnp.arange(vectors.shape[0])[:, None] < 12 * d // width
    total = sum_everywhere(vectors + jnp.where(shared, swap(vectors), 0.0), count)
    vector = shape((2, 2, d), F32)
    gains_grad, shifts_grad, branch_grad, joint_bias_grad, expand_bias_grad = small(
        vectors_kernel, "vectors",
        [vector, vector, vector, shape((2, 2, width), F32), shape((2, hidden), F32)], total,
    )
    return (
        latent.astype(BF),
        language.astype(BF),
        embedded_grad,
        gains_grad,
        shifts_grad,
        joint_grad.transpose(0, 2, 1, 3),
        joint_bias_grad,
        merge_grad.transpose(0, 2, 1),
        expand_grad,
        expand_bias_grad,
        shrink_grad.transpose(0, 2, 1),
        branch_grad,
    )


def solution(mesh):
    placed = (
        P(("fsdp", "tensor"), None),
        P("fsdp", None),
        P(("fsdp", "tensor"), None),
        P(("fsdp", "tensor"), None),
        P(),
        P(),
        P(None, "fsdp", None, "tensor"),
        P(None, None, "tensor"),
        P(None, "tensor", "fsdp"),
        P(None, "fsdp", "tensor"),
        P(None, "tensor"),
        P(None, "tensor", "fsdp"),
        P(),
    )
    return jax.shard_map(
        partial(shards, mesh.shape["fsdp"]),
        mesh=mesh,
        in_specs=placed,
        out_specs=(
            P(("fsdp", "tensor"), None),
            P(("fsdp", "tensor"), None),
            P(("fsdp", "tensor"), None),
            P(),
            P(),
            P(None, "fsdp", None, "tensor"),
            P(None, None, "tensor"),
            P(None, "tensor", "fsdp"),
            P(None, "fsdp", "tensor"),
            P(None, "tensor"),
            P(None, "tensor", "fsdp"),
            P(),
        ),
        check_vma=False,
    )
```

```python
from functools import partial

import jax
import jax.numpy as jnp
from jax import lax
from jax.experimental import pallas as pl
from jax.experimental.pallas import tpu as pltpu
from jax.sharding import PartitionSpec as P

HEAD = 64
LANES = 128
BLOCK = 48
EPSILON = 1e-05
BF = jnp.bfloat16
F32 = jnp.float32
GELU_C = 0.7978845608028654
GELU_A = 0.044715
MIB = 1 << 20


def dot(a, b):
    return lax.dot_general(a, b, (((1,), (0,)), ((), ())), preferred_element_type=F32)


def dot_nt(a, b):
    return lax.dot_general(a, b, (((1,), (1,)), ((), ())), preferred_element_type=F32)


def dot_tn(a, b):
    return lax.dot_general(a, b, (((0,), (0,)), ((), ())), preferred_element_type=F32)


def vmem(mib):
    return pltpu.CompilerParams(vmem_limit_bytes=mib * MIB)


def cost(flops, moved, exps=0):
    return pl.CostEstimate(flops=flops, transcendentals=exps, bytes_accessed=moved)


VMEM = pl.BlockSpec(memory_space=pltpu.VMEM)


def shape(dims, kind):
    return jax.ShapeDtypeStruct(tuple(dims), kind)


def across(value, count, stride):
    return lax.ppermute(value, "fsdp", [(place, place ^ stride) for place in range(count)])


def swap(value):
    return lax.ppermute(value, "tensor", [(0, 1), (1, 0)])


def after(value, *others):
    leaves, tree = jax.tree.flatten(value)
    held = lax.optimization_barrier(tuple(leaves) + tuple(jax.tree.leaves(others)))
    return jax.tree.unflatten(tree, held[: len(leaves)])


def sync(*values):
    leaves, tree = jax.tree.flatten(values)
    return jax.tree.unflatten(tree, lax.optimization_barrier(tuple(leaves)))


def join_kernel(own_ref, got_ref, out_ref):
    half = out_ref.shape[0] // 2
    for index in range(half):
        out_ref[index] = own_ref[index] if own_ref.ndim == 3 else own_ref[...]
        out_ref[half + index] = got_ref[index] if got_ref.ndim == 3 else got_ref[...]


def join(own, got):
    dims = own.shape[-2:]
    blocks = 2 if own.ndim == 2 else 2 * own.shape[0]
    return pl.pallas_call(
        join_kernel,
        name="join",
        out_shape=shape((blocks,) + dims, BF),
        in_specs=[VMEM] * 2,
        compiler_params=vmem(4),
        cost_estimate=cost(0, 4 * blocks * dims[0] * dims[1]),
    )(own, got)


def load_blocks(bufs, target, columns=None):
    if len(bufs) == 1:
        target[...] = bufs[0][...] if columns is None else bufs[0][:, :, columns]
        return
    me = lax.axis_index("fsdp")
    for number, buf in enumerate(bufs):
        for block in range(buf.shape[0]):
            away = (number // 2) + 2 * (number % 2) + 4 * (block // 2) + 8 * (block % 2)
            at = jnp.bitwise_xor(me, away)
            target[at] = buf[block] if columns is None else buf[block, :, columns]


def store_blocks(value, outs, rows, columns=slice(None)):
    if len(outs) == 1:
        outs[0][:, rows, columns] = value
        return
    pairs = value.reshape((value.shape[0] // 2, 2) + value.shape[1:])
    first = lax.rem(lax.axis_index("fsdp"), 2) == 0
    outs[0][:, rows, columns] = jnp.where(first, pairs[:, 0], pairs[:, 1])
    outs[1][:, rows, columns] = jnp.where(first, pairs[:, 1], pairs[:, 0])


def row_of(ref, layer, which):
    return ref[layer].astype(F32)[which : which + 1, :]


def statistics(rows):
    mean = jnp.mean(rows, axis=-1, keepdims=True)
    center = rows - mean
    scale = lax.rsqrt(jnp.mean(center * center, axis=-1, keepdims=True) + EPSILON)
    return (center * scale, scale)


def norm_backward(rows, grad, gain):
    unit, scale = statistics(rows)
    e = grad * gain
    back = scale * (
        e
        - jnp.mean(e, axis=-1, keepdims=True)
        - unit * jnp.mean(e * unit, axis=-1, keepdims=True)
    )
    return (
        back,
        jnp.sum(grad * unit, axis=0, keepdims=True),
        jnp.sum(grad, axis=0, keepdims=True),
    )


def column(row):
    wide = jnp.broadcast_to(row.astype(F32), (8, row.shape[1]))
    return wide.T[:, 0:1]


def place_rows(slots_ref, less, seq):
    slots = slots_ref.shape[1]
    wanted = column(slots_ref[...]) - float(less)
    places = lax.broadcasted_iota(jnp.int32, (slots, seq), 1).astype(F32)
    return wanted == places


def place_columns(slots_ref, less, seq):
    slots = slots_ref.shape[1]
    wanted = slots_ref[...] - less
    places = lax.broadcasted_iota(jnp.int32, (seq, slots), 0)
    return wanted == places


def ones(hit):
    return jnp.where(hit, 1.0, 0.0).astype(BF)


def exact_pick(hit, value):
    high = value.astype(BF)
    rest = value - high.astype(F32)
    middle = rest.astype(BF)
    low = (rest - middle.astype(F32)).astype(BF)
    return dot(hit, high) + dot(hit, middle) + dot(hit, low)


def pack_kernel(jt_ref, mt_ref, a_ref):
    rows = mt_ref.shape[1]
    for which in range(3):
        a_ref[which * rows : (which + 1) * rows, :] = jt_ref[0, which]
    a_ref[3 * rows :, :] = mt_ref[0]


def start_kernel(
    jt_ref, mt_ref, ex_ref, sh_ref, x_ref, gain_ref, shift_ref,
    n_ref, e0_ref, s0_ref, a1_ref, e1_ref, s1_ref,
):
    unit, _ = statistics(x_ref[...].astype(F32))
    n_ref[...] = (unit * row_of(gain_ref, 0, 0) + row_of(shift_ref, 0, 0)).astype(BF)
    rows = mt_ref.shape[1]
    for which in range(3):
        a1_ref[which * rows : (which + 1) * rows, :] = jt_ref[1, which]
    a1_ref[3 * rows :, :] = mt_ref[1]
    for layer, (e_ref, s_ref) in enumerate(((e0_ref, s0_ref), (e1_ref, s1_ref))):
        e_ref[...] = ex_ref[layer]
        s_ref[...] = sh_ref[layer]


def segment_row(seg_ref, peer):
    mine = lax.axis_index("tensor")
    which = (1 - mine) if peer else mine
    both = seg_ref[...].astype(F32)
    row = jnp.where(which == 0, both[0:1, :], both[1:2, :])
    return row


def lane_masks(rows):
    lane = lax.broadcasted_iota(jnp.int32, (rows, LANES), 1)
    return (lane < HEAD, lane >= HEAD)


def attend_forward_kernel(count, layer, peer, arrays, n_ref, seg_ref, bias_ref, *refs):
    bufs = refs[:arrays]
    part_ref, q_ref, k_ref, v_ref, mixed_ref, w_ref, neg_ref = refs[arrays:]
    load_blocks(bufs, w_ref)
    seq, d = n_ref.shape
    width = q_ref.shape[1]
    half = seq // 2
    row = segment_row(seg_ref, peer)
    rows = lax.broadcasted_iota(jnp.int32, (seq, seq), 0)
    cols = lax.broadcasted_iota(jnp.int32, (seq, seq), 1)
    allowed = (column(row) == row) & (cols <= rows)
    neg_ref[...] = jnp.where(allowed, 0.0, -1e30)
    n = n_ref[...]

    def weight(which):
        return w_ref[:, which * BLOCK : (which + 1) * BLOCK, :].reshape(d, width)

    q_ref[...] = (dot(n, weight(0)) + row_of(bias_ref, layer, 0)).astype(BF)
    k_ref[...] = dot(n, weight(1)).astype(BF)
    v_ref[...] = (dot(n, weight(2)) + row_of(bias_ref, layer, 1)).astype(BF)
    masks = lane_masks(half)
    for pair in range(width // LANES):
        lanes = slice(pair * LANES, (pair + 1) * LANES)
        for part in range(2):
            top = slice(part * half, (part + 1) * half)
            keys = slice(0, (part + 1) * half)
            qp = q_ref[top, lanes] * BF(HEAD ** (-0.5))
            kp = k_ref[keys, lanes]
            vp = v_ref[keys, lanes]
            found = []
            for mask in masks:
                s = dot_nt(jnp.where(mask, qp, BF(0)), kp) + neg_ref[top, keys]
                e = jnp.exp(s - jnp.max(s, axis=-1, keepdims=True))
                scale = 1.0 / jnp.sum(e, axis=-1, keepdims=True)
                found.append(dot((e * scale).astype(BF), vp))
            mixed_ref[top, lanes] = jnp.where(masks[0], found[0], found[1]).astype(BF)
    part_ref[...] = dot_nt(mixed_ref[...], weight(3)).astype(BF)


def attend_forward(count, layer, peer, n, segments, bias, bufs):
    seq, d = n.shape
    width = bufs[0].shape[-1]
    rows = shape((seq, width), BF)
    return pl.pallas_call(
        partial(attend_forward_kernel, count, layer, peer, len(bufs)),
        name="attend_forward",
        out_shape=[shape((seq, d), BF), rows, rows, rows, rows],
        in_specs=[VMEM] * (3 + len(bufs)),
        scratch_shapes=[
            pltpu.VMEM((d // BLOCK, 4 * BLOCK, width), BF),
            pltpu.VMEM((seq, seq), F32),
        ],
        compiler_params=vmem(16),
        cost_estimate=cost(
            8 * seq * d * width + 4 * seq * seq * width,
            8 * d * width + 4 * seq * d + 8 * seq * width,
            seq * seq * width // HEAD,
        ),
    )(n, segments, bias, *bufs)


def attend_backward_kernel(
    count, layer, peer, picked, arrays,
    q_ref, k_ref, v_ref, gm_ref, seg_ref, slots_ref, *refs,
):
    bufs = refs[:arrays]
    refs = refs[arrays:]
    if picked:
        gn_ref, dj_ref, gb_ref, wide_ref, w_ref, neg_ref, gx_ref, qx_ref = refs
    else:
        gn_ref, dj_ref, gb_ref, w_ref, neg_ref, gx_ref = refs
    load_blocks(bufs, w_ref)
    seq, width = q_ref.shape
    d = gm_ref.shape[1]
    half = seq // 2
    row = segment_row(seg_ref, peer)
    if picked:
        slots = gm_ref.shape[0]
        hit = place_rows(slots_ref, 1, seq)
        at = column(slots_ref[...]) - 1.0
        own = jnp.sum(jnp.where(hit, row, 0.0), axis=-1, keepdims=True)
        cols = lax.broadcasted_iota(jnp.int32, (slots, seq), 1).astype(F32)
        neg_ref[...] = jnp.where((own == row) & (cols <= at), 0.0, -1e30)
        qx_ref[...] = dot(ones(hit), q_ref[...]).astype(BF)
        parts = [(slice(0, slots), slice(0, seq))]
        queries = qx_ref
    else:
        rows = lax.broadcasted_iota(jnp.int32, (seq, seq), 0)
        cols = lax.broadcasted_iota(jnp.int32, (seq, seq), 1)
        allowed = (column(row) == row) & (cols <= rows)
        neg_ref[...] = jnp.where(allowed, 0.0, -1e30)
        parts = [
            (slice(part * half, (part + 1) * half), slice(0, (part + 1) * half))
            for part in range(2)
        ]
        queries = q_ref

    def weight(which):
        return w_ref[:, which * BLOCK : (which + 1) * BLOCK, :].reshape(d, width)

    gx_ref[...] = dot(gm_ref[...], weight(3)).astype(BF)
    if picked:
        back = ones(place_columns(slots_ref, 1, seq))
        wide_ref[...] = dot(back, gm_ref[...]).astype(BF)
    masks = lane_masks(parts[0][0].stop)
    for pair in range(width // LANES):
        lanes = slice(pair * LANES, (pair + 1) * LANES)
        dk = [None, None]
        dv = [None, None]
        dq_all = []
        for top, keys in parts:
            qp = queries[top, lanes]
            kp = k_ref[keys, lanes]
            vp = v_ref[keys, lanes]
            gp = gx_ref[top, lanes]
            dq, dk_now, dv_now = [], [], []
            for mask in masks:
                qm = jnp.where(mask, qp, BF(0)) * BF(HEAD ** (-0.5))
                s = dot_nt(qm, kp) + neg_ref[top, keys]
                e = jnp.exp(s - jnp.max(s, axis=-1, keepdims=True))
                p = e * (1.0 / jnp.sum(e, axis=-1, keepdims=True))
                gprobs = dot_nt(jnp.where(mask, gp, BF(0)), vp)
                inner = jnp.sum(gprobs * p, axis=-1, keepdims=True)
                ds = (p * (gprobs - inner) * HEAD ** (-0.5)).astype(BF)
                dq.append(dot(ds, kp))
                dk_now.append(dot_tn(ds, qp))
                dv_now.append(dot_tn(p.astype(BF), gp))
            dq_all.append(jnp.where(masks[0], dq[0], dq[1]))
            key_mask = lane_masks(half)[0]
            for block in range(keys.stop // half):
                at = slice(block * half, (block + 1) * half)
                k_new = jnp.where(key_mask, dk_now[0][at], dk_now[1][at])
                v_new = jnp.where(key_mask, dv_now[0][at], dv_now[1][at])
                dk[block] = k_new if dk[block] is None else dk[block] + k_new
                dv[block] = v_new if dv[block] is None else dv[block] + v_new
        gb_ref[0:1, lanes] = sum(jnp.sum(one, axis=0, keepdims=True) for one in dq_all)
        gb_ref[1:2, lanes] = sum(jnp.sum(one, axis=0, keepdims=True) for one in dv)
        if picked:
            dj_ref[0, :, lanes] = dot(back, dq_all[0].astype(BF)).astype(BF)
        else:
            for (top, _), one in zip(parts, dq_all):
                dj_ref[0, top, lanes] = one.astype(BF)
        for block in range(2):
            at = slice(block * half, (block + 1) * half)
            dj_ref[1, at, lanes] = dk[block].astype(BF)
            dj_ref[2, at, lanes] = dv[block].astype(BF)
    gn = dot_nt(dj_ref[0], weight(0))
    gn = gn + dot_nt(dj_ref[1], weight(1))
    gn = gn + dot_nt(dj_ref[2], weight(2))
    gn_ref[...] = gn.astype(BF)


def attend_backward(count, layer, peer, kept, gm, segments, slots, bufs, picked):
    q, k, v = kept
    seq, width = q.shape
    rows, d = gm.shape
    outs = [shape((seq, d), BF), shape((3, seq, width), BF), shape((2, width), F32)]
    scratch = [
        pltpu.VMEM((d // BLOCK, 4 * BLOCK, width), BF),
        pltpu.VMEM((rows, seq), F32),
        pltpu.VMEM((rows, width), BF),
    ]
    if picked:
        outs.append(shape((seq, d), BF))
        scratch.append(pltpu.VMEM((rows, width), BF))
    return pl.pallas_call(
        partial(attend_backward_kernel, count, layer, peer, picked, len(bufs)),
        name="attend_backward",
        out_shape=outs,
        in_specs=[VMEM] * (6 + len(bufs)),
        scratch_shapes=scratch,
        compiler_params=vmem(16),
        cost_estimate=cost(
            2 * rows * d * width + 6 * seq * d * width + 10 * rows * seq * width,
            8 * d * width + 4 * seq * d + 12 * seq * width,
            rows * seq * width // HEAD,
        ),
    )(q, k, v, gm, segments, slots, *bufs)


def attend_grads_kernel(n0_ref, n1_ref, d0_ref, d1_ref, g0_ref, g1_ref, m0_ref, m1_ref, *outs):
    d = n0_ref.shape[1]
    width = m0_ref.shape[1]
    groups = d // BLOCK
    nt = [n0_ref[...].T, n1_ref[...].T]
    for which in range(3):
        total = dot(nt[0], d0_ref[which]) + dot(nt[1], d1_ref[which])
        store_blocks(
            total.astype(BF).reshape(groups, BLOCK, width),
            outs,
            slice(which * BLOCK, (which + 1) * BLOCK),
        )
    total = dot(g0_ref[...].T, m0_ref[...]) + dot(g1_ref[...].T, m1_ref[...])
    store_blocks(
        total.astype(BF).reshape(groups, BLOCK, width), outs, slice(3 * BLOCK, 4 * BLOCK)
    )


def grad_shapes(count, groups, rows, width, split):
    if split:
        return [shape((count // 2, rows, width), BF)] * 2
    return [shape((groups, rows, width), BF)]


def attend_grads(count, split, n, dj, gm, mixed):
    seq, d = n[0].shape
    width = mixed[0].shape[1]
    outs = grad_shapes(count, d // BLOCK, 4 * BLOCK, width, split)
    return pl.pallas_call(
        attend_grads_kernel,
        name="attend_grads",
        out_shape=outs,
        in_specs=[VMEM] * 8,
        compiler_params=vmem(16),
        cost_estimate=cost(16 * seq * d * width, 16 * d * width + 8 * seq * d),
    )(*n, *dj, *gm, *mixed)


def chunk_of(hidden):
    return 512 if hidden % 512 == 0 else hidden


def mlp_forward_kernel(count, layer, arrays, n0_ref, n1_ref, be_ref, *refs):
    e_bufs, s_bufs = refs[:arrays], refs[arrays : 2 * arrays]
    out0_ref, out1_ref, n_ref, acc_ref, we_ref, ws_ref = refs[2 * arrays :]
    rows, d = n0_ref.shape
    hidden = e_bufs[0].shape[2]
    chunk = chunk_of(hidden)
    n_ref[:rows, :] = n0_ref[...]
    n_ref[rows:, :] = n1_ref[...]
    acc_ref[...] = jnp.zeros_like(acc_ref)

    @pl.loop(0, hidden // chunk)
    def _(index):
        cols = pl.ds(pl.multiple_of(index * chunk, chunk), chunk)
        load_blocks(e_bufs, we_ref, cols)
        load_blocks(s_bufs, ws_ref, cols)
        shift = be_ref[:, cols].astype(F32)[layer : layer + 1, :]
        u = dot(n_ref[...], we_ref[...].reshape(d, chunk)) + shift
        t = jnp.tanh(GELU_C * (u + GELU_A * (u * u * u)))
        active = (0.5 * u * (1.0 + t)).astype(BF)
        acc_ref[...] = acc_ref[...] + dot_nt(active, ws_ref[...].reshape(d, chunk))

    out0_ref[...] = acc_ref[:rows, :].astype(BF)
    out1_ref[...] = acc_ref[rows:, :].astype(BF)


def mlp_forward(count, layer, n, be, e_bufs, s_bufs):
    rows, d = n[0].shape
    hidden = e_bufs[0].shape[-1]
    return pl.pallas_call(
        partial(mlp_forward_kernel, count, layer, len(e_bufs)),
        name="mlp_forward",
        out_shape=[shape((rows, d), BF)] * 2,
        in_specs=[VMEM] * (3 + 2 * len(e_bufs)),
        scratch_shapes=[
            pltpu.VMEM((2 * rows, d), BF),
            pltpu.VMEM((2 * rows, d), F32),
            pltpu.VMEM((d // BLOCK, BLOCK, chunk_of(hidden)), BF),
            pltpu.VMEM((d // BLOCK, BLOCK, chunk_of(hidden)), BF),
        ],
        compiler_params=vmem(16),
        cost_estimate=cost(
            8 * rows * d * hidden, 4 * d * hidden + 8 * rows * d, 2 * rows * hidden
        ),
    )(*n, be, *e_bufs, *s_bufs)


def mlp_backward_kernel(count, layer, arrays, full, outputs, n0_ref, n1_ref, g0_ref, g1_ref, be_ref, *refs):
    e_bufs, s_bufs = refs[:arrays], refs[arrays : 2 * arrays]
    refs = refs[2 * arrays :]
    if full:
        out0_ref, out1_ref, refs = refs[0], refs[1], refs[2:]
    gn0_ref, gn1_ref, gb_ref = refs[:3]
    outs = refs[3 : 3 + outputs]
    refs = refs[3 + outputs :]
    n_ref, g_ref, nt_ref, gt_ref, gacc_ref, we_ref, ws_ref = refs[:7]
    if full:
        acc_ref = refs[7]
    rows, d = n0_ref.shape
    hidden = e_bufs[0].shape[2]
    chunk = chunk_of(hidden)
    groups = d // BLOCK
    n_ref[:rows, :] = n0_ref[...]
    n_ref[rows:, :] = n1_ref[...]
    g_ref[:rows, :] = g0_ref[...]
    g_ref[rows:, :] = g1_ref[...]
    nt_ref[...] = n_ref[...].T
    gt_ref[...] = g_ref[...].T
    gacc_ref[...] = jnp.zeros_like(gacc_ref)
    if full:
        acc_ref[...] = jnp.zeros_like(acc_ref)

    @pl.loop(0, hidden // chunk)
    def _(index):
        cols = pl.ds(pl.multiple_of(index * chunk, chunk), chunk)
        load_blocks(e_bufs, we_ref, cols)
        load_blocks(s_bufs, ws_ref, cols)
        we = we_ref[...].reshape(d, chunk)
        ws = ws_ref[...].reshape(d, chunk)
        shift = be_ref[:, cols].astype(F32)[layer : layer + 1, :]
        u = dot(n_ref[...], we) + shift
        square = u * u
        t = jnp.tanh(GELU_C * (u + GELU_A * (square * u)))
        lean = 0.5 * (1.0 + t)
        active = (u * lean).astype(BF)
        slope = lean + (0.5 * u) * (1.0 - t * t) * (GELU_C + (3.0 * GELU_C * GELU_A) * square)
        gh = dot(g_ref[...], ws) * slope
        gb_ref[:, cols] = jnp.sum(gh, axis=0, keepdims=True)
        gh = gh.astype(BF)
        ge = dot(nt_ref[...], gh).astype(BF)
        gs = dot(gt_ref[...], active).astype(BF)
        every = slice(0, BLOCK)
        store_blocks(ge.reshape(groups, BLOCK, chunk), outs[: outputs // 2], every, cols)
        store_blocks(gs.reshape(groups, BLOCK, chunk), outs[outputs // 2 :], every, cols)
        gacc_ref[...] = gacc_ref[...] + dot_nt(gh, we)
        if full:
            acc_ref[...] = acc_ref[...] + dot_nt(active, ws)

    gn0_ref[...] = gacc_ref[:rows, :].astype(BF)
    gn1_ref[...] = gacc_ref[rows:, :].astype(BF)
    if full:
        out0_ref[...] = acc_ref[:rows, :].astype(BF)
        out1_ref[...] = acc_ref[rows:, :].astype(BF)


def mlp_backward(count, layer, split, n, g, be, e_bufs, s_bufs, full):
    rows, d = n[0].shape
    hidden = e_bufs[0].shape[-1]
    groups = d // BLOCK
    half = shape((rows, d), BF)
    grads = 2 * grad_shapes(count, groups, BLOCK, hidden, split)
    blocks = pltpu.VMEM((groups, BLOCK, chunk_of(hidden)), BF)
    return pl.pallas_call(
        partial(mlp_backward_kernel, count, layer, len(e_bufs), full, len(grads)),
        name="mlp_backward",
        out_shape=[half] * (4 if full else 2) + [shape((1, hidden), F32)] + grads,
        in_specs=[VMEM] * (5 + 2 * len(e_bufs)),
        scratch_shapes=[
            pltpu.VMEM((2 * rows, d), BF),
            pltpu.VMEM((2 * rows, d), BF),
            pltpu.VMEM((d, 2 * rows), BF),
            pltpu.VMEM((d, 2 * rows), BF),
            pltpu.VMEM((2 * rows, d), F32),
            blocks,
            blocks,
        ]
        + ([pltpu.VMEM((2 * rows, d), F32)] if full else []),
        compiler_params=vmem(28),
        cost_estimate=cost(
            (24 if full else 20) * rows * d * hidden,
            8 * d * hidden + 16 * rows * d,
            2 * rows * hidden,
        ),
    )(*n, *g, be, *e_bufs, *s_bufs)


def middle_kernel(layer, x_ref, own_ref, got_ref, slots_ref, gain_ref, shift_ref, bias_ref, *outs):
    middle = (
        x_ref[...].astype(F32)
        + (own_ref[...].astype(F32) + got_ref[...].astype(F32))
        + row_of(bias_ref, layer, 0)
    )
    unit, _ = statistics(middle)
    normed = (unit * row_of(gain_ref, layer, 1) + row_of(shift_ref, layer, 1)).astype(BF)
    outs[0][...] = middle
    outs[1][...] = normed
    if layer == 0:
        hit = ones(place_rows(slots_ref, 1, x_ref.shape[0]))
        outs[2][...] = exact_pick(hit, middle)
        outs[3][...] = dot(hit, normed).astype(BF)


def second_kernel(
    x_ref, mid_ref, own_ref, got_ref, slots_ref, gain_ref, shift_ref, bias_ref, out_ref, n_ref
):
    seq = x_ref.shape[0]
    latent = (
        mid_ref[...]
        + (own_ref[...].astype(F32) + got_ref[...].astype(F32))
        + row_of(bias_ref, 0, 1)
    )
    known = column(slots_ref[...]) >= 1.0
    latent = jnp.where(known, latent, 0.0).astype(BF)
    hit = place_columns(slots_ref, 0, seq)
    occupied = jnp.sum(jnp.where(hit, 1.0, 0.0), axis=-1, keepdims=True)
    second = x_ref[...].astype(F32) * (1.0 - occupied) + dot(ones(hit), latent)
    unit, _ = statistics(second)
    out_ref[...] = second
    n_ref[...] = (unit * row_of(gain_ref, 1, 0) + row_of(shift_ref, 1, 0)).astype(BF)


def grad_middle_kernel(mid_ref, own_ref, got_ref, cot_ref, gain_ref, out_ref, low_ref, sum_ref):
    cot = cot_ref[...].astype(F32)
    grad = own_ref[...].astype(F32) + got_ref[...].astype(F32)
    back, gain, shift = norm_backward(mid_ref[...], grad, row_of(gain_ref, 1, 1))
    total = cot + back
    out_ref[...] = total
    low_ref[...] = total.astype(BF)
    sum_ref[0:1, :] = gain
    sum_ref[1:2, :] = shift
    sum_ref[2:3, :] = jnp.sum(total, axis=0, keepdims=True)
    sum_ref[3:4, :] = jnp.sum(cot, axis=0, keepdims=True)


def grad_second_kernel(
    x_ref, own_ref, got_ref, gm_ref, slots_ref, gain_ref, out_ref, pick_ref, low_ref, sum_ref
):
    grad = own_ref[...].astype(F32) + got_ref[...].astype(F32)
    back, gain, shift = norm_backward(x_ref[...], grad, row_of(gain_ref, 1, 0))
    total = gm_ref[...] + back
    out_ref[...] = total
    hit = place_rows(slots_ref, 0, x_ref.shape[0])
    known = column(slots_ref[...]) >= 1.0
    pick = jnp.where(known, exact_pick(ones(hit), total), 0.0)
    pick_ref[...] = pick
    low_ref[...] = pick.astype(BF)
    sum_ref[0:1, :] = gain
    sum_ref[1:2, :] = shift


def grad_picked_kernel(mid_ref, own_ref, got_ref, pick_ref, gain_ref, out_ref, low_ref, sum_ref):
    grad = own_ref[...].astype(F32) + got_ref[...].astype(F32)
    back, gain, shift = norm_backward(mid_ref[...], grad, row_of(gain_ref, 0, 1))
    pick = pick_ref[...]
    total = pick + back
    out_ref[...] = total
    low_ref[...] = total.astype(BF)
    sum_ref[0:1, :] = gain
    sum_ref[1:2, :] = shift
    sum_ref[2:3, :] = jnp.sum(total, axis=0, keepdims=True)
    sum_ref[3:4, :] = jnp.sum(pick, axis=0, keepdims=True)


def grad_first_kernel(
    x_ref, own_ref, got_ref, gm_ref, second_ref, slots_ref, gain_ref,
    s22_ref, s21_ref, s12_ref, pair1_ref, pair0_ref, peer1_ref, peer0_ref, be1_ref, be0_ref,
    out_ref, sum_ref,
):
    seq, d = x_ref.shape
    grad = own_ref[...].astype(F32) + got_ref[...].astype(F32)
    back, gain, shift = norm_backward(x_ref[...].astype(F32), grad, row_of(gain_ref, 0, 0))
    hit = place_columns(slots_ref, 0, seq)
    occupied = jnp.sum(jnp.where(hit, 1.0, 0.0), axis=-1, keepdims=True)
    source = ones(place_columns(slots_ref, 1, seq))
    out_ref[...] = second_ref[...] * (1.0 - occupied) + (exact_pick(source, gm_ref[...]) + back)
    width = pair0_ref.shape[1]
    for index, row in enumerate(
        (
            gain, s12_ref[0:1, :], s21_ref[0:1, :], s22_ref[0:1, :],
            shift, s12_ref[1:2, :], s21_ref[1:2, :], s22_ref[1:2, :],
            s12_ref[2:3, :], s12_ref[3:4, :], s22_ref[2:3, :], s22_ref[3:4, :],
        )
    ):
        for part in range(d // width):
            at = index * (d // width) + part
            sum_ref[at : at + 1, :] = row[:, part * width : (part + 1) * width]
    first = 12 * (d // width)
    sum_ref[first : first + 2, :] = pair0_ref[...] + peer0_ref[...]
    sum_ref[first + 2 : first + 4, :] = pair1_ref[...] + peer1_ref[...]
    hidden = be0_ref.shape[1]
    for layer, ref in enumerate((be0_ref, be1_ref)):
        for part in range(hidden // width):
            at = first + 4 + layer * (hidden // width) + part
            sum_ref[at : at + 1, :] = ref[0:1, part * width : (part + 1) * width]


def vectors_kernel(sum_ref, gains_ref, shifts_ref, branch_ref, pair_ref, hidden_ref):
    d = gains_ref.shape[2]
    width = sum_ref.shape[1]
    index = 0
    for ref in (gains_ref, shifts_ref, branch_ref):
        for layer in range(2):
            for which in range(2):
                for part in range(d // width):
                    ref[layer, which : which + 1, part * width : (part + 1) * width] = sum_ref[
                        index : index + 1, :
                    ]
                    index += 1
    for layer in range(2):
        pair_ref[layer] = sum_ref[index : index + 2, :]
        index += 2
    for layer in range(2):
        for part in range(hidden_ref.shape[1] // width):
            hidden_ref[layer : layer + 1, part * width : (part + 1) * width] = sum_ref[
                index : index + 1, :
            ]
            index += 1


def small(kernel, name, outs, *args):
    moved = sum(a.size * a.dtype.itemsize for a in args) + sum(
        o.size * o.dtype.itemsize for o in outs
    )
    return pl.pallas_call(
        kernel,
        name=name,
        out_shape=outs,
        in_specs=[VMEM] * len(args),
        compiler_params=vmem(24),
        cost_estimate=cost(4 * moved, moved),
    )(*args)


def split_kernel(stride, keep_ref, got_ref, kept_ref, sent_ref):
    bit = lax.rem(lax.axis_index("fsdp") // stride, 2)
    for index in range(kept_ref.shape[0]):
        for out, place in ((kept_ref, bit), (sent_ref, 1 - bit)):
            at = 2 * index + place
            out[index] = (keep_ref[at].astype(F32) + got_ref[at].astype(F32)).astype(BF)


def split(keep, got, stride):
    blocks, rows, width = keep.shape
    return pl.pallas_call(
        partial(split_kernel, stride),
        name="split",
        out_shape=[shape((blocks // 2, rows, width), BF)] * 2,
        in_specs=[VMEM] * 2,
        compiler_params=vmem(8),
        cost_estimate=cost(keep.size, 6 * keep.size),
    )(keep, got)


def finish_kernel(counts, *refs):
    joint_ref, merge_ref, expand_ref, shrink_ref = refs[-4:]
    totals = []
    first = 0
    for number in counts:
        total = refs[first][0].astype(F32)
        for ref in refs[first + 1 : first + number]:
            total = total + ref[0].astype(F32)
        totals.append(total)
        first += number
    rows = merge_ref.shape[1]
    for layer in range(2):
        attend, expand, shrink = totals[3 * layer : 3 * layer + 3]
        for which in range(3):
            joint_ref[layer, which] = attend[which * rows : (which + 1) * rows, :]
        merge_ref[layer] = attend[3 * rows :, :]
        expand_ref[layer] = expand
        shrink_ref[layer] = shrink


def finish(states):
    _, rows, width = states[0][0].shape
    hidden = states[1][0].shape[2]
    rows = rows // 4
    outs = [shape((2, 3, rows, width), F32), shape((2, rows, width), F32)]
    outs += [shape((2, rows, hidden), F32)] * 2
    counts = tuple(len(state) for state in states)
    return small(
        partial(finish_kernel, counts), "finish", outs, *[one for state in states for one in state]
    )


def sum_everywhere(value, count):
    stride = 1
    while stride < count and count % (2 * stride) == 0:
        pairs = [(source, source ^ stride) for source in range(count)]
        value = value + lax.ppermute(value, "fsdp", pairs)
        stride *= 2
    if stride < count:
        groups = [list(range(first, count, stride)) for first in range(stride)]
        value = lax.psum(value, "fsdp", axis_index_groups=groups)
    return value


def regroup(array, count, kinds):
    rows = array.shape[0] * array.shape[1] // kinds // BLOCK
    each = array.shape[1] // kinds
    width = array.shape[2]
    split = array.reshape(array.shape[0], kinds, each, width).transpose(1, 0, 2, 3)
    return split.reshape(kinds, rows, BLOCK, width).transpose(1, 0, 2, 3).reshape(
        rows, kinds * BLOCK, width
    )


def ungroup(array, count, kinds):
    width = array.shape[2]
    split = array.reshape(array.shape[0], kinds, BLOCK, width).transpose(1, 0, 2, 3)
    each = array.shape[0] * BLOCK // count
    return split.reshape(kinds, count, each, width).transpose(1, 0, 2, 3).reshape(
        count, kinds * each, width
    )


def shards(
    count,
    embedded,
    segments,
    thoughts,
    cotangent,
    gains,
    shifts,
    joint_weight,
    joint_bias,
    merge_weight,
    expand_weight,
    expand_bias,
    shrink_weight,
    branch_biases,
):
    seq, d = embedded.shape
    rows_each = joint_weight.shape[1]
    width = joint_weight.shape[3]
    hidden = expand_weight.shape[2]
    slots = thoughts.shape[1]
    staged = rows_each == BLOCK and count == 16
    rows_f32, rows_bf = shape((seq, d), F32), shape((seq, d), BF)
    few_f32, few_bf = shape((slots, d), F32), shape((slots, d), BF)
    ins = (
        joint_weight.transpose(0, 2, 1, 3),
        merge_weight.transpose(0, 2, 1),
        expand_weight,
        shrink_weight.transpose(0, 2, 1),
    )
    bufs = {}

    def first_step(own):
        return join(own, across(own, count, 8))

    def next_step(own):
        return join(own, across(own, count, 4))

    def third_step(own):
        return (own, across(own, count, 2))

    def last_step(both):
        return [*both, across(both[0], count, 1), across(both[1], count, 1)]

    if staged:
        attend, plain = shape((4 * rows_each, width), BF), shape((rows_each, hidden), BF)
        (a0,) = small(pack_kernel, "pack", [attend], *ins[:2])
        normed, e0, s0, a1, e1, s1 = small(
            start_kernel, "start", [rows_bf, plain, plain, attend, plain, plain],
            *ins, embedded, gains, shifts,
        )
    else:
        first = embedded.astype(F32)
        center = first - jnp.mean(first, axis=-1, keepdims=True)
        scale = lax.rsqrt(jnp.mean(center * center, axis=-1, keepdims=True) + EPSILON)
        normed = (
            center * scale * gains[0, 0].astype(F32) + shifts[0, 0].astype(F32)
        ).astype(BF)
        for layer in range(2):
            attend = jnp.concatenate(
                (ins[0][layer].reshape(3 * rows_each, width), ins[1][layer]), axis=0
            )
            for name, one, kind in (("a", attend, 4), ("e", ins[2][layer], 1), ("s", ins[3][layer], 1)):
                whole = lax.all_gather(one, "fsdp", axis=0, tiled=False)
                bufs[f"{name}{layer}"] = [regroup(whole, count, kind)]

    slots_peer = swap(thoughts)
    normed_peer = swap(normed)

    if staged:
        a0, e0 = sync(first_step(a0), e0)
        a0, e0, s0 = sync(next_step(a0), first_step(e0), s0)
        a0, e0, s0, a1, normed_peer, slots_peer = sync(
            third_step(a0), next_step(e0), first_step(s0), a1, normed_peer, slots_peer
        )
        bufs["a0"] = last_step(a0)

    def attention(layer, own, peer):
        weights = bufs[f"a{layer}"]
        part_peer, *kept_peer = attend_forward(count, layer, True, peer, segments, joint_bias, weights)
        got = swap(part_peer)
        part_own, *kept_own = attend_forward(
            count, layer, False, after(own, part_peer), segments, joint_bias, weights
        )
        return (part_own, got, (own, peer), (kept_own, kept_peer))

    part, got, n_one, kept_one = attention(0, normed, normed_peer)
    if staged:
        e0, s0, a1, part, e1 = sync(third_step(e0), next_step(s0), first_step(a1), part, e1)
        bufs["e0"] = last_step(e0)
    middle_one, n2_one, middle_few, n2_few = small(
        partial(middle_kernel, 0), "middle", [rows_f32, rows_bf, few_f32, few_bf],
        embedded, part, got, thoughts, gains, shifts, branch_biases,
    )
    n2_few = (n2_few, swap(n2_few))
    if staged:
        s0, a1, e1, s1, n2_few, bufs["e0"], n2_one = sync(
            third_step(s0), next_step(a1), first_step(e1), s1, n2_few, bufs["e0"], n2_one
        )
        bufs["s0"] = last_step(s0)
    own, peer = mlp_forward(count, 0, n2_few, expand_bias, bufs["e0"], bufs["s0"])
    second, normed = small(
        second_kernel, "second", [rows_f32, rows_bf],
        embedded, middle_few, own, swap(peer), thoughts, gains, shifts, branch_biases,
    )
    cot_peer = swap(after(cotangent, n2_few))
    n2_all = (n2_one, swap(n2_one))
    normed_peer = swap(normed)

    if staged:
        a1, e1, s1, normed, cot_peer = sync(
            third_step(a1), next_step(e1), first_step(s1), normed, cot_peer
        )
        bufs["a1"] = last_step(a1)
    part, got, n_two, kept_two = attention(1, normed, normed_peer)
    if staged:
        e1, s1, part, n2_all = sync(third_step(e1), next_step(s1), part, n2_all)
        bufs["e1"] = last_step(e1)
    middle_two, n2_two = small(
        partial(middle_kernel, 1), "middle", [rows_f32, rows_bf],
        second, part, got, thoughts, gains, shifts, branch_biases,
    )
    n2_peer = swap(n2_two)
    latent_own, latent_peer = mlp_forward(
        count, 0, after(n2_all, n2_two), expand_bias, bufs["e0"], bufs["s0"]
    )
    if staged:
        s1, n2_two, n2_peer, bufs["e1"], latent_peer = sync(
            third_step(s1), n2_two, n2_peer, bufs["e1"], latent_peer
        )
        bufs["s1"] = last_step(s1)
    own_two, peer_two, gn_own, gn_peer, gb_two, *grads = mlp_backward(
        count, 1, staged, (n2_two, n2_peer), (cotangent, cot_peer),
        expand_bias, bufs["e1"], bufs["s1"], True,
    )

    def begin(grads, kind):
        if staged:
            return (grads[0], across(grads[1], count, 1))
        done = lax.psum_scatter(
            ungroup(grads[0], count, kind), "fsdp", scatter_dimension=0, tiled=False
        )
        return (done[None],)

    def further(state, stride):
        if not staged:
            return state
        kept, sent = split(*state, stride)
        return (kept, across(sent, count, stride))

    def apart(grads):
        return (grads[: len(grads) // 2], grads[len(grads) // 2 :])

    e1, s1 = apart(grads)
    got = swap(gn_peer)
    s1, e1 = begin(s1, 1), begin(e1, 1)
    s1, e1, got, gn_own = sync(s1, e1, got, gn_own)
    gm, gm_low, s22 = small(
        grad_middle_kernel, "grad_middle", [rows_f32, rows_bf, shape((4, d), F32)],
        middle_two, gn_own, got, cotangent, gains,
    )
    gm_peer = swap(gm_low)
    s1 = further(s1, 2)
    weights = bufs["a1"]
    back_peer = attend_backward(
        count, 1, True, kept_two[1][:3], gm_peer, segments, slots_peer, weights, False
    )
    s1, e1, back_peer, gm_low = sync(s1, e1, back_peer, gm_low)
    got = swap(back_peer[0])
    s1, e1 = further(s1, 4), further(e1, 2)
    back_own = attend_backward(
        count, 1, False, kept_two[0][:3], gm_low, segments, thoughts, weights, False
    )
    a1 = attend_grads(
        count, staged, n_two, (back_own[1], back_peer[1]), (gm_low, gm_peer),
        (kept_two[0][3], kept_two[1][3]),
    )
    a1 = begin(a1, 4)
    s1, e1, a1, got, own = sync(s1, e1, a1, got, back_own[0])
    grad_second, g_few, g_low, s21 = small(
        grad_second_kernel, "grad_second", [rows_f32, few_f32, few_bf, shape((2, d), F32)],
        second, own, got, gm, thoughts, gains,
    )
    pair_two = (back_own[2], back_peer[2])

    g_peer = swap(g_low)
    s1, e1, a1 = further(s1, 8), further(e1, 4), further(a1, 2)
    own, peer, gb_one, *grads = mlp_backward(
        count, 0, staged, n2_few, (g_low, g_peer), expand_bias,
        bufs["e0"], bufs["s0"], False,
    )
    e0, s0 = apart(grads)
    s0, e0 = begin(s0, 1), begin(e0, 1)
    gm_few, gm_low, s12 = small(
        grad_picked_kernel, "grad_picked", [few_f32, few_bf, shape((4, d), F32)],
        middle_few, own, swap(peer), g_few, gains,
    )
    gm_peer = swap(gm_low)
    s1, e1, a1, s0, e0, gm_peer, gm_low = sync(s1, e1, a1, s0, e0, gm_peer, gm_low)
    e1, a1, s0 = further(e1, 8), further(a1, 4), further(s0, 2)
    weights = bufs["a0"]
    back_peer = attend_backward(
        count, 0, True, kept_one[1][:3], gm_peer, segments, slots_peer, weights, True
    )
    got = swap(back_peer[0])
    back_own = attend_backward(
        count, 0, False, kept_one[0][:3], after(gm_low, back_peer[0]), segments, thoughts, weights, True
    )
    a0 = attend_grads(
        count, staged, n_one, (back_own[1], back_peer[1]), (back_own[3], back_peer[3]),
        (kept_one[0][3], kept_one[1][3]),
    )
    a0 = begin(a0, 4)
    pair_one = (back_own[2], back_peer[2])
    e1, a1, s0, e0, a0 = sync(e1, a1, s0, e0, a0)
    a1, s0, e0 = further(a1, 8), further(s0, 4), further(e0, 2)
    embedded_grad, vectors = small(
        grad_first_kernel, "grad_first",
        [rows_f32, shape((12 * d // width + 4 + 2 * (hidden // width), width), F32)],
        embedded, back_own[0], got, gm_few, grad_second, thoughts, gains,
        s22, s21, s12, pair_two[0], pair_one[0], pair_two[1], pair_one[1], gb_two, gb_one,
    )
    shared = jnp.arange(vectors.shape[0])[:, None] < 12 * d // width
    vectors = vectors + jnp.where(shared, swap(vectors), 0.0)
    s0, e0, a0, vectors = sync(s0, e0, a0, vectors)
    total = sum_everywhere(vectors, count)
    s0, e0, a0 = further(s0, 8), further(e0, 4), further(a0, 2)
    e0, a0 = further(e0, 8), further(a0, 4)
    a0 = further(a0, 8)

    biases = branch_biases.astype(F32)
    latent_peer, peer_two = swap(after(latent_peer, gn_peer)), swap(after(peer_two, gm_peer))
    latent = middle_one + (latent_own.astype(F32) + latent_peer.astype(F32)) + biases[0, 1]
    language = middle_two + (own_two.astype(F32) + peer_two.astype(F32)) + biases[1, 1]

    joint_grad, merge_grad, expand_grad, shrink_grad = finish((a0, e0, s0, a1, e1, s1))
    vector = shape((2, 2, d), F32)
    gains_grad, shifts_grad, branch_grad, joint_bias_grad, expand_bias_grad = small(
        vectors_kernel, "vectors",
        [vector, vector, vector, shape((2, 2, width), F32), shape((2, hidden), F32)], total,
    )
    return (
        latent.astype(BF),
        language.astype(BF),
        embedded_grad,
        gains_grad,
        shifts_grad,
        joint_grad.transpose(0, 2, 1, 3),
        joint_bias_grad,
        merge_grad.transpose(0, 2, 1),
        expand_grad,
        expand_bias_grad,
        shrink_grad.transpose(0, 2, 1),
        branch_grad,
    )


def solution(mesh):
    placed = (
        P(("fsdp", "tensor"), None),
        P("fsdp", None),
        P(("fsdp", "tensor"), None),
        P(("fsdp", "tensor"), None),
        P(),
        P(),
        P(None, "fsdp", None, "tensor"),
        P(None, None, "tensor"),
        P(None, "tensor", "fsdp"),
        P(None, "fsdp", "tensor"),
        P(None, "tensor"),
        P(None, "tensor", "fsdp"),
        P(),
    )
    return jax.shard_map(
        partial(shards, mesh.shape["fsdp"]),
        mesh=mesh,
        in_specs=placed,
        out_specs=(
            P(("fsdp", "tensor"), None),
            P(("fsdp", "tensor"), None),
            P(("fsdp", "tensor"), None),
            P(),
            P(),
            P(None, "fsdp", None, "tensor"),
            P(None, None, "tensor"),
            P(None, "tensor", "fsdp"),
            P(None, "fsdp", "tensor"),
            P(None, "tensor"),
            P(None, "tensor", "fsdp"),
            P(),
        ),
        check_vma=False,
    )
```

```python
from functools import partial

import jax
import jax.numpy as jnp
from jax import lax
from jax.experimental import pallas as pl
from jax.experimental.pallas import tpu as pltpu
from jax.sharding import PartitionSpec as P

HEAD = 64
LANES = 128
BLOCK = 48
EPSILON = 1e-05
BF = jnp.bfloat16
F32 = jnp.float32
GELU_C = 0.7978845608028654
GELU_A = 0.044715
MIB = 1 << 20


def dot(a, b):
    return lax.dot_general(a, b, (((1,), (0,)), ((), ())), preferred_element_type=F32)


def dot_nt(a, b):
    return lax.dot_general(a, b, (((1,), (1,)), ((), ())), preferred_element_type=F32)


def dot_tn(a, b):
    return lax.dot_general(a, b, (((0,), (0,)), ((), ())), preferred_element_type=F32)


def vmem(mib):
    return pltpu.CompilerParams(vmem_limit_bytes=mib * MIB)


def cost(flops, moved, exps=0):
    return pl.CostEstimate(flops=flops, transcendentals=exps, bytes_accessed=moved)


VMEM = pl.BlockSpec(memory_space=pltpu.VMEM)


def shape(dims, kind):
    return jax.ShapeDtypeStruct(tuple(dims), kind)


def across(value, count, stride):
    return lax.ppermute(value, "fsdp", [(place, place ^ stride) for place in range(count)])


def swap(value):
    return lax.ppermute(value, "tensor", [(0, 1), (1, 0)])


def after(value, *others):
    leaves, tree = jax.tree.flatten(value)
    held = lax.optimization_barrier(tuple(leaves) + tuple(jax.tree.leaves(others)))
    return jax.tree.unflatten(tree, held[: len(leaves)])


def sync(*values):
    leaves, tree = jax.tree.flatten(values)
    return jax.tree.unflatten(tree, lax.optimization_barrier(tuple(leaves)))


def join_kernel(own_ref, got_ref, out_ref):
    half = out_ref.shape[0] // 2
    for index in range(half):
        out_ref[index] = own_ref[index] if own_ref.ndim == 3 else own_ref[...]
        out_ref[half + index] = got_ref[index] if got_ref.ndim == 3 else got_ref[...]


JOIN_WAIT = 2 * 10**9
SPLIT_WAIT = {2: 0, 4: 25 * 10**9, 8: 2 * 10**9}


def join(own, got):
    dims = own.shape[-2:]
    blocks = 2 if own.ndim == 2 else 2 * own.shape[0]
    return pl.pallas_call(
        join_kernel,
        name="join",
        out_shape=shape((blocks,) + dims, BF),
        in_specs=[VMEM] * 2,
        compiler_params=vmem(4),
        cost_estimate=cost(JOIN_WAIT, 4 * blocks * dims[0] * dims[1]),
    )(own, got)


def load_blocks(bufs, target, columns=None):
    if len(bufs) == 1:
        target[...] = bufs[0][...] if columns is None else bufs[0][:, :, columns]
        return
    me = lax.axis_index("fsdp")
    for number, buf in enumerate(bufs):
        for block in range(buf.shape[0]):
            away = (number // 2) + 2 * (number % 2) + 4 * (block // 2) + 8 * (block % 2)
            at = jnp.bitwise_xor(me, away)
            target[at] = buf[block] if columns is None else buf[block, :, columns]


def store_blocks(value, outs, rows, columns=slice(None)):
    if len(outs) == 1:
        outs[0][:, rows, columns] = value
        return
    pairs = value.reshape((value.shape[0] // 2, 2) + value.shape[1:])
    first = lax.rem(lax.axis_index("fsdp"), 2) == 0
    outs[0][:, rows, columns] = jnp.where(first, pairs[:, 0], pairs[:, 1])
    outs[1][:, rows, columns] = jnp.where(first, pairs[:, 1], pairs[:, 0])


def row_of(ref, layer, which):
    return ref[layer].astype(F32)[which : which + 1, :]


def statistics(rows):
    mean = jnp.mean(rows, axis=-1, keepdims=True)
    center = rows - mean
    scale = lax.rsqrt(jnp.mean(center * center, axis=-1, keepdims=True) + EPSILON)
    return (center * scale, scale)


def norm_backward(rows, grad, gain):
    unit, scale = statistics(rows)
    e = grad * gain
    back = scale * (
        e
        - jnp.mean(e, axis=-1, keepdims=True)
        - unit * jnp.mean(e * unit, axis=-1, keepdims=True)
    )
    return (
        back,
        jnp.sum(grad * unit, axis=0, keepdims=True),
        jnp.sum(grad, axis=0, keepdims=True),
    )


def column(row):
    wide = jnp.broadcast_to(row.astype(F32), (8, row.shape[1]))
    return wide.T[:, 0:1]


def place_rows(slots_ref, less, seq):
    slots = slots_ref.shape[1]
    wanted = column(slots_ref[...]) - float(less)
    places = lax.broadcasted_iota(jnp.int32, (slots, seq), 1).astype(F32)
    return wanted == places


def place_columns(slots_ref, less, seq):
    slots = slots_ref.shape[1]
    wanted = slots_ref[...] - less
    places = lax.broadcasted_iota(jnp.int32, (seq, slots), 0)
    return wanted == places


def ones(hit):
    return jnp.where(hit, 1.0, 0.0).astype(BF)


def exact_pick(hit, value):
    high = value.astype(BF)
    rest = value - high.astype(F32)
    middle = rest.astype(BF)
    low = (rest - middle.astype(F32)).astype(BF)
    return dot(hit, high) + dot(hit, middle) + dot(hit, low)


def pack_kernel(jt_ref, mt_ref, a_ref):
    rows = mt_ref.shape[1]
    for which in range(3):
        a_ref[which * rows : (which + 1) * rows, :] = jt_ref[0, which]
    a_ref[3 * rows :, :] = mt_ref[0]


def start_kernel(
    jt_ref, mt_ref, ex_ref, sh_ref, x_ref, gain_ref, shift_ref,
    n_ref, e0_ref, s0_ref, a1_ref, e1_ref, s1_ref,
):
    unit, _ = statistics(x_ref[...].astype(F32))
    n_ref[...] = (unit * row_of(gain_ref, 0, 0) + row_of(shift_ref, 0, 0)).astype(BF)
    rows = mt_ref.shape[1]
    for which in range(3):
        a1_ref[which * rows : (which + 1) * rows, :] = jt_ref[1, which]
    a1_ref[3 * rows :, :] = mt_ref[1]
    for layer, (e_ref, s_ref) in enumerate(((e0_ref, s0_ref), (e1_ref, s1_ref))):
        e_ref[...] = ex_ref[layer]
        s_ref[...] = sh_ref[layer]


def segment_row(seg_ref, peer):
    mine = lax.axis_index("tensor")
    which = (1 - mine) if peer else mine
    both = seg_ref[...].astype(F32)
    row = jnp.where(which == 0, both[0:1, :], both[1:2, :])
    return row


def lane_masks(rows):
    lane = lax.broadcasted_iota(jnp.int32, (rows, LANES), 1)
    return (lane < HEAD, lane >= HEAD)


def attend_forward_kernel(count, layer, peer, arrays, n_ref, seg_ref, bias_ref, *refs):
    bufs = refs[:arrays]
    part_ref, q_ref, k_ref, v_ref, mixed_ref, w_ref, neg_ref = refs[arrays:]
    load_blocks(bufs, w_ref)
    seq, d = n_ref.shape
    width = q_ref.shape[1]
    half = seq // 2
    row = segment_row(seg_ref, peer)
    rows = lax.broadcasted_iota(jnp.int32, (seq, seq), 0)
    cols = lax.broadcasted_iota(jnp.int32, (seq, seq), 1)
    allowed = (column(row) == row) & (cols <= rows)
    neg_ref[...] = jnp.where(allowed, 0.0, -1e30)
    n = n_ref[...]

    def weight(which):
        return w_ref[:, which * BLOCK : (which + 1) * BLOCK, :].reshape(d, width)

    q_ref[...] = (dot(n, weight(0)) + row_of(bias_ref, layer, 0)).astype(BF)
    k_ref[...] = dot(n, weight(1)).astype(BF)
    v_ref[...] = (dot(n, weight(2)) + row_of(bias_ref, layer, 1)).astype(BF)
    masks = lane_masks(half)
    for pair in range(width // LANES):
        lanes = slice(pair * LANES, (pair + 1) * LANES)
        for part in range(2):
            top = slice(part * half, (part + 1) * half)
            keys = slice(0, (part + 1) * half)
            qp = q_ref[top, lanes] * BF(HEAD ** (-0.5))
            kp = k_ref[keys, lanes]
            vp = v_ref[keys, lanes]
            found = []
            for mask in masks:
                s = dot_nt(jnp.where(mask, qp, BF(0)), kp) + neg_ref[top, keys]
                e = jnp.exp(s - jnp.max(s, axis=-1, keepdims=True))
                scale = 1.0 / jnp.sum(e, axis=-1, keepdims=True)
                found.append(dot((e * scale).astype(BF), vp))
            mixed_ref[top, lanes] = jnp.where(masks[0], found[0], found[1]).astype(BF)
    part_ref[...] = dot_nt(mixed_ref[...], weight(3)).astype(BF)


def attend_forward(count, layer, peer, n, segments, bias, bufs):
    seq, d = n.shape
    width = bufs[0].shape[-1]
    rows = shape((seq, width), BF)
    return pl.pallas_call(
        partial(attend_forward_kernel, count, layer, peer, len(bufs)),
        name="attend_forward",
        out_shape=[shape((seq, d), BF), rows, rows, rows, rows],
        in_specs=[VMEM] * (3 + len(bufs)),
        scratch_shapes=[
            pltpu.VMEM((d // BLOCK, 4 * BLOCK, width), BF),
            pltpu.VMEM((seq, seq), F32),
        ],
        compiler_params=vmem(16),
        cost_estimate=cost(
            8 * seq * d * width + 4 * seq * seq * width,
            8 * d * width + 4 * seq * d + 8 * seq * width,
            seq * seq * width // HEAD,
        ),
    )(n, segments, bias, *bufs)


def attend_backward_kernel(
    count, layer, peer, picked, arrays,
    q_ref, k_ref, v_ref, gm_ref, seg_ref, slots_ref, *refs,
):
    bufs = refs[:arrays]
    refs = refs[arrays:]
    if picked:
        gn_ref, dj_ref, gb_ref, wide_ref, w_ref, neg_ref, gx_ref, qx_ref = refs
    else:
        gn_ref, dj_ref, gb_ref, w_ref, neg_ref, gx_ref = refs
    load_blocks(bufs, w_ref)
    seq, width = q_ref.shape
    d = gm_ref.shape[1]
    half = seq // 2
    row = segment_row(seg_ref, peer)
    if picked:
        slots = gm_ref.shape[0]
        hit = place_rows(slots_ref, 1, seq)
        at = column(slots_ref[...]) - 1.0
        own = jnp.sum(jnp.where(hit, row, 0.0), axis=-1, keepdims=True)
        cols = lax.broadcasted_iota(jnp.int32, (slots, seq), 1).astype(F32)
        neg_ref[...] = jnp.where((own == row) & (cols <= at), 0.0, -1e30)
        qx_ref[...] = dot(ones(hit), q_ref[...]).astype(BF)
        parts = [(slice(0, slots), slice(0, seq))]
        queries = qx_ref
    else:
        rows = lax.broadcasted_iota(jnp.int32, (seq, seq), 0)
        cols = lax.broadcasted_iota(jnp.int32, (seq, seq), 1)
        allowed = (column(row) == row) & (cols <= rows)
        neg_ref[...] = jnp.where(allowed, 0.0, -1e30)
        parts = [
            (slice(part * half, (part + 1) * half), slice(0, (part + 1) * half))
            for part in range(2)
        ]
        queries = q_ref

    def weight(which):
        return w_ref[:, which * BLOCK : (which + 1) * BLOCK, :].reshape(d, width)

    gx_ref[...] = dot(gm_ref[...], weight(3)).astype(BF)
    if picked:
        back = ones(place_columns(slots_ref, 1, seq))
        wide_ref[...] = dot(back, gm_ref[...]).astype(BF)
    masks = lane_masks(parts[0][0].stop)
    for pair in range(width // LANES):
        lanes = slice(pair * LANES, (pair + 1) * LANES)
        dk = [None, None]
        dv = [None, None]
        dq_all = []
        for top, keys in parts:
            qp = queries[top, lanes]
            kp = k_ref[keys, lanes]
            vp = v_ref[keys, lanes]
            gp = gx_ref[top, lanes]
            dq, dk_now, dv_now = [], [], []
            for mask in masks:
                qm = jnp.where(mask, qp, BF(0)) * BF(HEAD ** (-0.5))
                s = dot_nt(qm, kp) + neg_ref[top, keys]
                e = jnp.exp(s - jnp.max(s, axis=-1, keepdims=True))
                p = e * (1.0 / jnp.sum(e, axis=-1, keepdims=True))
                gprobs = dot_nt(jnp.where(mask, gp, BF(0)), vp)
                inner = jnp.sum(gprobs * p, axis=-1, keepdims=True)
                ds = (p * (gprobs - inner) * HEAD ** (-0.5)).astype(BF)
                dq.append(dot(ds, kp))
                dk_now.append(dot_tn(ds, qp))
                dv_now.append(dot_tn(p.astype(BF), gp))
            dq_all.append(jnp.where(masks[0], dq[0], dq[1]))
            key_mask = lane_masks(half)[0]
            for block in range(keys.stop // half):
                at = slice(block * half, (block + 1) * half)
                k_new = jnp.where(key_mask, dk_now[0][at], dk_now[1][at])
                v_new = jnp.where(key_mask, dv_now[0][at], dv_now[1][at])
                dk[block] = k_new if dk[block] is None else dk[block] + k_new
                dv[block] = v_new if dv[block] is None else dv[block] + v_new
        gb_ref[0:1, lanes] = sum(jnp.sum(one, axis=0, keepdims=True) for one in dq_all)
        gb_ref[1:2, lanes] = sum(jnp.sum(one, axis=0, keepdims=True) for one in dv)
        if picked:
            dj_ref[0, :, lanes] = dot(back, dq_all[0].astype(BF)).astype(BF)
        else:
            for (top, _), one in zip(parts, dq_all):
                dj_ref[0, top, lanes] = one.astype(BF)
        for block in range(2):
            at = slice(block * half, (block + 1) * half)
            dj_ref[1, at, lanes] = dk[block].astype(BF)
            dj_ref[2, at, lanes] = dv[block].astype(BF)
    gn = dot_nt(dj_ref[0], weight(0))
    gn = gn + dot_nt(dj_ref[1], weight(1))
    gn = gn + dot_nt(dj_ref[2], weight(2))
    gn_ref[...] = gn.astype(BF)


def attend_backward(count, layer, peer, kept, gm, segments, slots, bufs, picked):
    q, k, v = kept
    seq, width = q.shape
    rows, d = gm.shape
    outs = [shape((seq, d), BF), shape((3, seq, width), BF), shape((2, width), F32)]
    scratch = [
        pltpu.VMEM((d // BLOCK, 4 * BLOCK, width), BF),
        pltpu.VMEM((rows, seq), F32),
        pltpu.VMEM((rows, width), BF),
    ]
    if picked:
        outs.append(shape((seq, d), BF))
        scratch.append(pltpu.VMEM((rows, width), BF))
    return pl.pallas_call(
        partial(attend_backward_kernel, count, layer, peer, picked, len(bufs)),
        name="attend_backward",
        out_shape=outs,
        in_specs=[VMEM] * (6 + len(bufs)),
        scratch_shapes=scratch,
        compiler_params=vmem(16),
        cost_estimate=cost(
            2 * rows * d * width + 6 * seq * d * width + 10 * rows * seq * width,
            8 * d * width + 4 * seq * d + 12 * seq * width,
            rows * seq * width // HEAD,
        ),
    )(q, k, v, gm, segments, slots, *bufs)


def attend_grads_kernel(n0_ref, n1_ref, d0_ref, d1_ref, g0_ref, g1_ref, m0_ref, m1_ref, *outs):
    d = n0_ref.shape[1]
    width = m0_ref.shape[1]
    groups = d // BLOCK
    nt = [n0_ref[...].T, n1_ref[...].T]
    for which in range(3):
        total = dot(nt[0], d0_ref[which]) + dot(nt[1], d1_ref[which])
        store_blocks(
            total.astype(BF).reshape(groups, BLOCK, width),
            outs,
            slice(which * BLOCK, (which + 1) * BLOCK),
        )
    total = dot(g0_ref[...].T, m0_ref[...]) + dot(g1_ref[...].T, m1_ref[...])
    store_blocks(
        total.astype(BF).reshape(groups, BLOCK, width), outs, slice(3 * BLOCK, 4 * BLOCK)
    )


def grad_shapes(count, groups, rows, width, split):
    if split:
        return [shape((count // 2, rows, width), BF)] * 2
    return [shape((groups, rows, width), BF)]


def attend_grads(count, split, n, dj, gm, mixed):
    seq, d = n[0].shape
    width = mixed[0].shape[1]
    outs = grad_shapes(count, d // BLOCK, 4 * BLOCK, width, split)
    return pl.pallas_call(
        attend_grads_kernel,
        name="attend_grads",
        out_shape=outs,
        in_specs=[VMEM] * 8,
        compiler_params=vmem(16),
        cost_estimate=cost(16 * seq * d * width, 16 * d * width + 8 * seq * d),
    )(*n, *dj, *gm, *mixed)


def chunk_of(hidden):
    return 512 if hidden % 512 == 0 else hidden


def mlp_forward_kernel(count, layer, arrays, n0_ref, n1_ref, be_ref, *refs):
    e_bufs, s_bufs = refs[:arrays], refs[arrays : 2 * arrays]
    out0_ref, out1_ref, n_ref, acc_ref, we_ref, ws_ref = refs[2 * arrays :]
    rows, d = n0_ref.shape
    hidden = e_bufs[0].shape[2]
    chunk = chunk_of(hidden)
    n_ref[:rows, :] = n0_ref[...]
    n_ref[rows:, :] = n1_ref[...]
    acc_ref[...] = jnp.zeros_like(acc_ref)

    @pl.loop(0, hidden // chunk)
    def _(index):
        cols = pl.ds(pl.multiple_of(index * chunk, chunk), chunk)
        load_blocks(e_bufs, we_ref, cols)
        load_blocks(s_bufs, ws_ref, cols)
        shift = be_ref[:, cols].astype(F32)[layer : layer + 1, :]
        u = dot(n_ref[...], we_ref[...].reshape(d, chunk)) + shift
        t = jnp.tanh(GELU_C * (u + GELU_A * (u * u * u)))
        active = (0.5 * u * (1.0 + t)).astype(BF)
        acc_ref[...] = acc_ref[...] + dot_nt(active, ws_ref[...].reshape(d, chunk))

    out0_ref[...] = acc_ref[:rows, :].astype(BF)
    out1_ref[...] = acc_ref[rows:, :].astype(BF)


def mlp_forward(count, layer, n, be, e_bufs, s_bufs):
    rows, d = n[0].shape
    hidden = e_bufs[0].shape[-1]
    return pl.pallas_call(
        partial(mlp_forward_kernel, count, layer, len(e_bufs)),
        name="mlp_forward",
        out_shape=[shape((rows, d), BF)] * 2,
        in_specs=[VMEM] * (3 + 2 * len(e_bufs)),
        scratch_shapes=[
            pltpu.VMEM((2 * rows, d), BF),
            pltpu.VMEM((2 * rows, d), F32),
            pltpu.VMEM((d // BLOCK, BLOCK, chunk_of(hidden)), BF),
            pltpu.VMEM((d // BLOCK, BLOCK, chunk_of(hidden)), BF),
        ],
        compiler_params=vmem(16),
        cost_estimate=cost(
            8 * rows * d * hidden, 4 * d * hidden + 8 * rows * d, 2 * rows * hidden
        ),
    )(*n, be, *e_bufs, *s_bufs)


def mlp_backward_kernel(count, layer, arrays, full, outputs, n0_ref, n1_ref, g0_ref, g1_ref, be_ref, *refs):
    e_bufs, s_bufs = refs[:arrays], refs[arrays : 2 * arrays]
    refs = refs[2 * arrays :]
    if full:
        out0_ref, out1_ref, refs = refs[0], refs[1], refs[2:]
    gn0_ref, gn1_ref, gb_ref = refs[:3]
    outs = refs[3 : 3 + outputs]
    refs = refs[3 + outputs :]
    n_ref, g_ref, nt_ref, gt_ref, gacc_ref, we_ref, ws_ref = refs[:7]
    if full:
        acc_ref = refs[7]
    rows, d = n0_ref.shape
    hidden = e_bufs[0].shape[2]
    chunk = chunk_of(hidden)
    groups = d // BLOCK
    n_ref[:rows, :] = n0_ref[...]
    n_ref[rows:, :] = n1_ref[...]
    g_ref[:rows, :] = g0_ref[...]
    g_ref[rows:, :] = g1_ref[...]
    nt_ref[...] = n_ref[...].T
    gt_ref[...] = g_ref[...].T
    gacc_ref[...] = jnp.zeros_like(gacc_ref)
    if full:
        acc_ref[...] = jnp.zeros_like(acc_ref)

    @pl.loop(0, hidden // chunk)
    def _(index):
        cols = pl.ds(pl.multiple_of(index * chunk, chunk), chunk)
        load_blocks(e_bufs, we_ref, cols)
        load_blocks(s_bufs, ws_ref, cols)
        we = we_ref[...].reshape(d, chunk)
        ws = ws_ref[...].reshape(d, chunk)
        shift = be_ref[:, cols].astype(F32)[layer : layer + 1, :]
        u = dot(n_ref[...], we) + shift
        square = u * u
        t = jnp.tanh(GELU_C * (u + GELU_A * (square * u)))
        lean = 0.5 * (1.0 + t)
        active = (u * lean).astype(BF)
        slope = lean + (0.5 * u) * (1.0 - t * t) * (GELU_C + (3.0 * GELU_C * GELU_A) * square)
        gh = dot(g_ref[...], ws) * slope
        gb_ref[:, cols] = jnp.sum(gh, axis=0, keepdims=True)
        gh = gh.astype(BF)
        ge = dot(nt_ref[...], gh).astype(BF)
        gs = dot(gt_ref[...], active).astype(BF)
        every = slice(0, BLOCK)
        store_blocks(ge.reshape(groups, BLOCK, chunk), outs[: outputs // 2], every, cols)
        store_blocks(gs.reshape(groups, BLOCK, chunk), outs[outputs // 2 :], every, cols)
        gacc_ref[...] = gacc_ref[...] + dot_nt(gh, we)
        if full:
            acc_ref[...] = acc_ref[...] + dot_nt(active, ws)

    gn0_ref[...] = gacc_ref[:rows, :].astype(BF)
    gn1_ref[...] = gacc_ref[rows:, :].astype(BF)
    if full:
        out0_ref[...] = acc_ref[:rows, :].astype(BF)
        out1_ref[...] = acc_ref[rows:, :].astype(BF)


def mlp_backward(count, layer, split, n, g, be, e_bufs, s_bufs, full):
    rows, d = n[0].shape
    hidden = e_bufs[0].shape[-1]
    groups = d // BLOCK
    half = shape((rows, d), BF)
    grads = 2 * grad_shapes(count, groups, BLOCK, hidden, split)
    blocks = pltpu.VMEM((groups, BLOCK, chunk_of(hidden)), BF)
    return pl.pallas_call(
        partial(mlp_backward_kernel, count, layer, len(e_bufs), full, len(grads)),
        name="mlp_backward",
        out_shape=[half] * (4 if full else 2) + [shape((1, hidden), F32)] + grads,
        in_specs=[VMEM] * (5 + 2 * len(e_bufs)),
        scratch_shapes=[
            pltpu.VMEM((2 * rows, d), BF),
            pltpu.VMEM((2 * rows, d), BF),
            pltpu.VMEM((d, 2 * rows), BF),
            pltpu.VMEM((d, 2 * rows), BF),
            pltpu.VMEM((2 * rows, d), F32),
            blocks,
            blocks,
        ]
        + ([pltpu.VMEM((2 * rows, d), F32)] if full else []),
        compiler_params=vmem(28),
        cost_estimate=cost(
            (24 if full else 20) * rows * d * hidden,
            8 * d * hidden + 16 * rows * d,
            2 * rows * hidden,
        ),
    )(*n, *g, be, *e_bufs, *s_bufs)


def middle_kernel(layer, x_ref, own_ref, got_ref, slots_ref, gain_ref, shift_ref, bias_ref, *outs):
    middle = (
        x_ref[...].astype(F32)
        + (own_ref[...].astype(F32) + got_ref[...].astype(F32))
        + row_of(bias_ref, layer, 0)
    )
    unit, _ = statistics(middle)
    normed = (unit * row_of(gain_ref, layer, 1) + row_of(shift_ref, layer, 1)).astype(BF)
    outs[0][...] = middle
    outs[1][...] = normed
    if layer == 0:
        hit = ones(place_rows(slots_ref, 1, x_ref.shape[0]))
        outs[2][...] = exact_pick(hit, middle)
        outs[3][...] = dot(hit, normed).astype(BF)


def second_kernel(
    x_ref, mid_ref, own_ref, got_ref, slots_ref, gain_ref, shift_ref, bias_ref, out_ref, n_ref
):
    seq = x_ref.shape[0]
    latent = (
        mid_ref[...]
        + (own_ref[...].astype(F32) + got_ref[...].astype(F32))
        + row_of(bias_ref, 0, 1)
    )
    known = column(slots_ref[...]) >= 1.0
    latent = jnp.where(known, latent, 0.0).astype(BF)
    hit = place_columns(slots_ref, 0, seq)
    occupied = jnp.sum(jnp.where(hit, 1.0, 0.0), axis=-1, keepdims=True)
    second = x_ref[...].astype(F32) * (1.0 - occupied) + dot(ones(hit), latent)
    unit, _ = statistics(second)
    out_ref[...] = second
    n_ref[...] = (unit * row_of(gain_ref, 1, 0) + row_of(shift_ref, 1, 0)).astype(BF)


def grad_middle_kernel(mid_ref, own_ref, got_ref, cot_ref, gain_ref, out_ref, low_ref, sum_ref):
    cot = cot_ref[...].astype(F32)
    grad = own_ref[...].astype(F32) + got_ref[...].astype(F32)
    back, gain, shift = norm_backward(mid_ref[...], grad, row_of(gain_ref, 1, 1))
    total = cot + back
    out_ref[...] = total
    low_ref[...] = total.astype(BF)
    sum_ref[0:1, :] = gain
    sum_ref[1:2, :] = shift
    sum_ref[2:3, :] = jnp.sum(total, axis=0, keepdims=True)
    sum_ref[3:4, :] = jnp.sum(cot, axis=0, keepdims=True)


def grad_second_kernel(
    x_ref, own_ref, got_ref, gm_ref, slots_ref, gain_ref, out_ref, pick_ref, low_ref, sum_ref
):
    grad = own_ref[...].astype(F32) + got_ref[...].astype(F32)
    back, gain, shift = norm_backward(x_ref[...], grad, row_of(gain_ref, 1, 0))
    total = gm_ref[...] + back
    out_ref[...] = total
    hit = place_rows(slots_ref, 0, x_ref.shape[0])
    known = column(slots_ref[...]) >= 1.0
    pick = jnp.where(known, exact_pick(ones(hit), total), 0.0)
    pick_ref[...] = pick
    low_ref[...] = pick.astype(BF)
    sum_ref[0:1, :] = gain
    sum_ref[1:2, :] = shift


def grad_picked_kernel(mid_ref, own_ref, got_ref, pick_ref, gain_ref, out_ref, low_ref, sum_ref):
    grad = own_ref[...].astype(F32) + got_ref[...].astype(F32)
    back, gain, shift = norm_backward(mid_ref[...], grad, row_of(gain_ref, 0, 1))
    pick = pick_ref[...]
    total = pick + back
    out_ref[...] = total
    low_ref[...] = total.astype(BF)
    sum_ref[0:1, :] = gain
    sum_ref[1:2, :] = shift
    sum_ref[2:3, :] = jnp.sum(total, axis=0, keepdims=True)
    sum_ref[3:4, :] = jnp.sum(pick, axis=0, keepdims=True)


def grad_first_kernel(
    x_ref, own_ref, got_ref, gm_ref, second_ref, slots_ref, gain_ref,
    s22_ref, s21_ref, s12_ref, pair1_ref, pair0_ref, peer1_ref, peer0_ref, be1_ref, be0_ref,
    out_ref, sum_ref,
):
    seq, d = x_ref.shape
    grad = own_ref[...].astype(F32) + got_ref[...].astype(F32)
    back, gain, shift = norm_backward(x_ref[...].astype(F32), grad, row_of(gain_ref, 0, 0))
    hit = place_columns(slots_ref, 0, seq)
    occupied = jnp.sum(jnp.where(hit, 1.0, 0.0), axis=-1, keepdims=True)
    source = ones(place_columns(slots_ref, 1, seq))
    out_ref[...] = second_ref[...] * (1.0 - occupied) + (exact_pick(source, gm_ref[...]) + back)
    width = pair0_ref.shape[1]
    for index, row in enumerate(
        (
            gain, s12_ref[0:1, :], s21_ref[0:1, :], s22_ref[0:1, :],
            shift, s12_ref[1:2, :], s21_ref[1:2, :], s22_ref[1:2, :],
            s12_ref[2:3, :], s12_ref[3:4, :], s22_ref[2:3, :], s22_ref[3:4, :],
        )
    ):
        for part in range(d // width):
            at = index * (d // width) + part
            sum_ref[at : at + 1, :] = row[:, part * width : (part + 1) * width]
    first = 12 * (d // width)
    sum_ref[first : first + 2, :] = pair0_ref[...] + peer0_ref[...]
    sum_ref[first + 2 : first + 4, :] = pair1_ref[...] + peer1_ref[...]
    hidden = be0_ref.shape[1]
    for layer, ref in enumerate((be0_ref, be1_ref)):
        for part in range(hidden // width):
            at = first + 4 + layer * (hidden // width) + part
            sum_ref[at : at + 1, :] = ref[0:1, part * width : (part + 1) * width]


def vectors_kernel(sum_ref, gains_ref, shifts_ref, branch_ref, pair_ref, hidden_ref):
    d = gains_ref.shape[2]
    width = sum_ref.shape[1]
    index = 0
    for ref in (gains_ref, shifts_ref, branch_ref):
        for layer in range(2):
            for which in range(2):
                for part in range(d // width):
                    ref[layer, which : which + 1, part * width : (part + 1) * width] = sum_ref[
                        index : index + 1, :
                    ]
                    index += 1
    for layer in range(2):
        pair_ref[layer] = sum_ref[index : index + 2, :]
        index += 2
    for layer in range(2):
        for part in range(hidden_ref.shape[1] // width):
            hidden_ref[layer : layer + 1, part * width : (part + 1) * width] = sum_ref[
                index : index + 1, :
            ]
            index += 1


def small(kernel, name, outs, *args):
    moved = sum(a.size * a.dtype.itemsize for a in args) + sum(
        o.size * o.dtype.itemsize for o in outs
    )
    return pl.pallas_call(
        kernel,
        name=name,
        out_shape=outs,
        in_specs=[VMEM] * len(args),
        compiler_params=vmem(24),
        cost_estimate=cost(4 * moved, moved),
    )(*args)


def split_kernel(stride, keep_ref, got_ref, kept_ref, sent_ref):
    bit = lax.rem(lax.axis_index("fsdp") // stride, 2)
    for index in range(kept_ref.shape[0]):
        for out, place in ((kept_ref, bit), (sent_ref, 1 - bit)):
            at = 2 * index + place
            out[index] = (keep_ref[at].astype(F32) + got_ref[at].astype(F32)).astype(BF)


def split(keep, got, stride):
    blocks, rows, width = keep.shape
    return pl.pallas_call(
        partial(split_kernel, stride),
        name="split",
        out_shape=[shape((blocks // 2, rows, width), BF)] * 2,
        in_specs=[VMEM] * 2,
        compiler_params=vmem(8),
        cost_estimate=cost(keep.size + SPLIT_WAIT[stride], 6 * keep.size),
    )(keep, got)


def finish_kernel(counts, *refs):
    joint_ref, merge_ref, expand_ref, shrink_ref = refs[-4:]
    totals = []
    first = 0
    for number in counts:
        total = refs[first][0].astype(F32)
        for ref in refs[first + 1 : first + number]:
            total = total + ref[0].astype(F32)
        totals.append(total)
        first += number
    rows = merge_ref.shape[1]
    for layer in range(2):
        attend, expand, shrink = totals[3 * layer : 3 * layer + 3]
        for which in range(3):
            joint_ref[layer, which] = attend[which * rows : (which + 1) * rows, :]
        merge_ref[layer] = attend[3 * rows :, :]
        expand_ref[layer] = expand
        shrink_ref[layer] = shrink


def finish(states):
    _, rows, width = states[0][0].shape
    hidden = states[1][0].shape[2]
    rows = rows // 4
    outs = [shape((2, 3, rows, width), F32), shape((2, rows, width), F32)]
    outs += [shape((2, rows, hidden), F32)] * 2
    counts = tuple(len(state) for state in states)
    return small(
        partial(finish_kernel, counts), "finish", outs, *[one for state in states for one in state]
    )


def regroup(array, count, kinds):
    rows = array.shape[0] * array.shape[1] // kinds // BLOCK
    each = array.shape[1] // kinds
    width = array.shape[2]
    split = array.reshape(array.shape[0], kinds, each, width).transpose(1, 0, 2, 3)
    return split.reshape(kinds, rows, BLOCK, width).transpose(1, 0, 2, 3).reshape(
        rows, kinds * BLOCK, width
    )


def ungroup(array, count, kinds):
    width = array.shape[2]
    split = array.reshape(array.shape[0], kinds, BLOCK, width).transpose(1, 0, 2, 3)
    each = array.shape[0] * BLOCK // count
    return split.reshape(kinds, count, each, width).transpose(1, 0, 2, 3).reshape(
        count, kinds * each, width
    )


def shards(
    count,
    embedded,
    segments,
    thoughts,
    cotangent,
    gains,
    shifts,
    joint_weight,
    joint_bias,
    merge_weight,
    expand_weight,
    expand_bias,
    shrink_weight,
    branch_biases,
):
    seq, d = embedded.shape
    rows_each = joint_weight.shape[1]
    width = joint_weight.shape[3]
    hidden = expand_weight.shape[2]
    slots = thoughts.shape[1]
    staged = rows_each == BLOCK and count == 16
    rows_f32, rows_bf = shape((seq, d), F32), shape((seq, d), BF)
    few_f32, few_bf = shape((slots, d), F32), shape((slots, d), BF)
    ins = (
        joint_weight.transpose(0, 2, 1, 3),
        merge_weight.transpose(0, 2, 1),
        expand_weight,
        shrink_weight.transpose(0, 2, 1),
    )
    bufs = {}

    def first_step(own, *others):
        return join(after(own, *others), across(own, count, 8))

    def next_step(own, *others):
        return join(after(own, *others), across(own, count, 4))

    def third_step(own):
        return (own, across(own, count, 2))

    def last_step(both):
        return [*both, across(both[0], count, 1), across(both[1], count, 1)]

    if staged:
        attend, plain = shape((4 * rows_each, width), BF), shape((rows_each, hidden), BF)
        (a0,) = small(pack_kernel, "pack", [attend], *ins[:2])
        normed, e0, s0, a1, e1, s1 = small(
            start_kernel, "start", [rows_bf, plain, plain, attend, plain, plain],
            *ins, embedded, gains, shifts,
        )
    else:
        first = embedded.astype(F32)
        center = first - jnp.mean(first, axis=-1, keepdims=True)
        scale = lax.rsqrt(jnp.mean(center * center, axis=-1, keepdims=True) + EPSILON)
        normed = (
            center * scale * gains[0, 0].astype(F32) + shifts[0, 0].astype(F32)
        ).astype(BF)
        for layer in range(2):
            attend = jnp.concatenate(
                (ins[0][layer].reshape(3 * rows_each, width), ins[1][layer]), axis=0
            )
            for name, one, kind in (("a", attend, 4), ("e", ins[2][layer], 1), ("s", ins[3][layer], 1)):
                whole = lax.all_gather(one, "fsdp", axis=0, tiled=False)
                bufs[f"{name}{layer}"] = [regroup(whole, count, kind)]

    slots_peer = swap(thoughts)
    normed_peer = swap(normed)

    if staged:
        a0, e0 = sync(first_step(a0), e0)
        a0, e0, s0 = sync(next_step(a0), first_step(e0), s0)
        a0, e0, s0, a1, normed_peer, slots_peer = sync(
            third_step(a0), next_step(e0), first_step(s0), a1, normed_peer, slots_peer
        )
        bufs["a0"] = last_step(a0)
    cot_peer = swap(after(cotangent, normed_peer))

    def attention(layer, own, peer):
        weights = bufs[f"a{layer}"]
        part_peer, *kept_peer = attend_forward(count, layer, True, peer, segments, joint_bias, weights)
        got = swap(part_peer)
        part_own, *kept_own = attend_forward(
            count, layer, False, after(own, part_peer), segments, joint_bias, weights
        )
        return (part_own, got, (own, peer), (kept_own, kept_peer))

    part, got, n_one, kept_one = attention(0, normed, normed_peer)
    if staged:
        e0, s0, a1, part, e1, cot_peer = sync(
            third_step(e0), next_step(s0, part), first_step(a1, part), part, e1, cot_peer
        )
        bufs["e0"] = last_step(e0)
    middle_one, n2_one, middle_few, n2_few = small(
        partial(middle_kernel, 0), "middle", [rows_f32, rows_bf, few_f32, few_bf],
        embedded, part, got, thoughts, gains, shifts, branch_biases,
    )
    n2_few = (n2_few, swap(n2_few))
    if staged:
        s0, a1, e1, s1, n2_few, bufs["e0"] = sync(
            third_step(s0), next_step(a1, n2_few[1]), first_step(e1, n2_few[1]), s1, n2_few,
            bufs["e0"],
        )
        bufs["s0"] = last_step(s0)
    own, peer = mlp_forward(count, 0, n2_few, expand_bias, bufs["e0"], bufs["s0"])
    second, normed = small(
        second_kernel, "second", [rows_f32, rows_bf],
        embedded, middle_few, own, swap(peer), thoughts, gains, shifts, branch_biases,
    )
    normed_peer = swap(normed)

    if staged:
        a1, e1, s1, normed, normed_peer = sync(
            third_step(a1), next_step(e1, normed), first_step(s1, normed), normed, normed_peer
        )
        bufs["a1"] = last_step(a1)
    part, got, n_two, kept_two = attention(1, normed, normed_peer)
    if staged:
        e1, s1, part = sync(third_step(e1), next_step(s1, part), part)
        bufs["e1"] = last_step(e1)
    middle_two, n2_two = small(
        partial(middle_kernel, 1), "middle", [rows_f32, rows_bf],
        second, part, got, thoughts, gains, shifts, branch_biases,
    )
    n2_peer = swap(n2_two)
    if staged:
        s1, n2_two, n2_peer, bufs["e1"] = sync(third_step(s1), n2_two, n2_peer, bufs["e1"])
        bufs["s1"] = last_step(s1)
    own_two, peer_two, gn_own, gn_peer, gb_two, *grads = mlp_backward(
        count, 1, staged, (n2_two, n2_peer), (cotangent, cot_peer),
        expand_bias, bufs["e1"], bufs["s1"], True,
    )

    def begin(grads, kind):
        if staged:
            return (grads[0], across(grads[1], count, 1))
        done = lax.psum_scatter(
            ungroup(grads[0], count, kind), "fsdp", scatter_dimension=0, tiled=False
        )
        return (done[None],)

    def settle(state, stride, *others):
        return tuple(split(*after(state, *others), stride)) if staged else state

    def move(state, stride):
        return (state[0], across(state[1], count, stride)) if staged else state

    def apart(grads):
        return (grads[: len(grads) // 2], grads[len(grads) // 2 :])

    e1, s1 = apart(grads)
    got = swap(gn_peer)
    s1, e1, got, gn_own = sync(settle(begin(s1, 1), 2), settle(begin(e1, 1), 2), got, gn_own)
    s1 = move(s1, 2)
    gm, gm_low, s22 = small(
        grad_middle_kernel, "grad_middle", [rows_f32, rows_bf, shape((4, d), F32)],
        middle_two, gn_own, got, cotangent, gains,
    )
    gm_peer = swap(gm_low)
    weights = bufs["a1"]
    back_peer = attend_backward(
        count, 1, True, kept_two[1][:3], gm_peer, segments, slots_peer, weights, False
    )
    s1, e1, back_peer, gm_low = sync(settle(s1, 4, back_peer[0]), e1, back_peer, gm_low)
    got = swap(back_peer[0])
    s1, e1 = move(s1, 4), move(e1, 2)
    back_own = attend_backward(
        count, 1, False, kept_two[0][:3], gm_low, segments, thoughts, weights, False
    )
    a1 = attend_grads(
        count, staged, n_two, (after(back_own[1], got), back_peer[1]), (gm_low, gm_peer),
        (kept_two[0][3], kept_two[1][3]),
    )
    s1, e1, a1, got, own = sync(
        settle(s1, 8, a1), settle(e1, 4, a1), settle(begin(a1, 4), 2), got, back_own[0]
    )
    s1, e1, a1 = move(s1, 8), move(e1, 4), move(a1, 2)
    grad_second, g_few, g_low, s21 = small(
        grad_second_kernel, "grad_second", [rows_f32, few_f32, few_bf, shape((2, d), F32)],
        second, own, got, gm, thoughts, gains,
    )
    pair_two = (back_own[2], back_peer[2])

    g_peer = swap(g_low)
    own, peer, gb_one, *grads = mlp_backward(
        count, 0, staged, n2_few, (g_low, g_peer), expand_bias,
        bufs["e0"], bufs["s0"], False,
    )
    e0, s0 = apart(grads)
    s0, e0 = settle(begin(s0, 1), 2), settle(begin(e0, 1), 2)
    gm_few, gm_low, s12 = small(
        grad_picked_kernel, "grad_picked", [few_f32, few_bf, shape((4, d), F32)],
        middle_few, own, swap(peer), g_few, gains,
    )
    gm_peer = swap(gm_low)
    s1, e1, a1, s0, e0, gm_peer, gm_low = sync(
        s1, settle(e1, 8, gm_low), settle(a1, 4, gm_low), s0, e0, gm_peer, gm_low
    )
    e1, a1, s0 = move(e1, 8), move(a1, 4), move(s0, 2)
    weights = bufs["a0"]
    back_peer = attend_backward(
        count, 0, True, kept_one[1][:3], gm_peer, segments, slots_peer, weights, True
    )
    got = swap(back_peer[0])
    back_own = attend_backward(
        count, 0, False, kept_one[0][:3], after(gm_low, back_peer[0]), segments, thoughts, weights, True
    )
    a0 = attend_grads(
        count, staged, n_one, (back_own[1], back_peer[1]), (back_own[3], back_peer[3]),
        (kept_one[0][3], kept_one[1][3]),
    )
    pair_one = (back_own[2], back_peer[2])
    e1, a1, s0, e0, a0, got, n2_one, peer_two = sync(
        e1, settle(a1, 8, a0), settle(s0, 4, a0), e0, settle(begin(a0, 4), 2), got,
        n2_one, peer_two,
    )
    a1, s0, e0 = move(a1, 8), move(s0, 4), move(e0, 2)
    embedded_grad, vectors = small(
        grad_first_kernel, "grad_first",
        [rows_f32, shape((12 * d // width + 4 + 2 * (hidden // width), width), F32)],
        embedded, back_own[0], got, gm_few, grad_second, thoughts, gains,
        s22, s21, s12, pair_two[0], pair_one[0], pair_two[1], pair_one[1], gb_two, gb_one,
    )
    shared = jnp.arange(vectors.shape[0])[:, None] < 12 * d // width
    vectors = vectors + jnp.where(shared, swap(vectors), 0.0)
    n2_peer = swap(after(n2_one, vectors))
    a1, s0, e0, a0, vectors = sync(
        a1, settle(s0, 8, vectors), settle(e0, 4, vectors), a0, vectors
    )
    s0, e0, a0 = move(s0, 8), move(e0, 4), move(a0, 2)
    if staged:
        vectors = vectors + across(vectors, count, 1)
        vectors = vectors + across(after(vectors, s0), count, 2)
        s0, e0, a0, vectors, n2_peer = sync(s0, settle(e0, 8), settle(a0, 4), vectors, n2_peer)
        e0, a0 = move(e0, 8), move(a0, 4)
        vectors = vectors + across(vectors, count, 4)
        e0, a0, vectors = sync(e0, settle(a0, 8), vectors)
        a0 = move(a0, 8)
        total = vectors + across(vectors, count, 8)
    else:
        total = lax.psum(vectors, "fsdp")

    latent_own, latent_peer = mlp_forward(
        count, 0, (n2_one, n2_peer), expand_bias, bufs["e0"], bufs["s0"]
    )
    biases = branch_biases.astype(F32)
    latent_peer, peer_two = swap(latent_peer), swap(after(peer_two, n2_peer))
    latent = middle_one + (latent_own.astype(F32) + latent_peer.astype(F32)) + biases[0, 1]
    language = middle_two + (own_two.astype(F32) + peer_two.astype(F32)) + biases[1, 1]

    joint_grad, merge_grad, expand_grad, shrink_grad = finish((a0, e0, s0, a1, e1, s1))
    vector = shape((2, 2, d), F32)
    gains_grad, shifts_grad, branch_grad, joint_bias_grad, expand_bias_grad = small(
        vectors_kernel, "vectors",
        [vector, vector, vector, shape((2, 2, width), F32), shape((2, hidden), F32)], total,
    )
    return (
        latent.astype(BF),
        language.astype(BF),
        embedded_grad,
        gains_grad,
        shifts_grad,
        joint_grad.transpose(0, 2, 1, 3),
        joint_bias_grad,
        merge_grad.transpose(0, 2, 1),
        expand_grad,
        expand_bias_grad,
        shrink_grad.transpose(0, 2, 1),
        branch_grad,
    )


def solution(mesh):
    placed = (
        P(("fsdp", "tensor"), None),
        P("fsdp", None),
        P(("fsdp", "tensor"), None),
        P(("fsdp", "tensor"), None),
        P(),
        P(),
        P(None, "fsdp", None, "tensor"),
        P(None, None, "tensor"),
        P(None, "tensor", "fsdp"),
        P(None, "fsdp", "tensor"),
        P(None, "tensor"),
        P(None, "tensor", "fsdp"),
        P(),
    )
    return jax.shard_map(
        partial(shards, mesh.shape["fsdp"]),
        mesh=mesh,
        in_specs=placed,
        out_specs=(
            P(("fsdp", "tensor"), None),
            P(("fsdp", "tensor"), None),
            P(("fsdp", "tensor"), None),
            P(),
            P(),
            P(None, "fsdp", None, "tensor"),
            P(None, None, "tensor"),
            P(None, "tensor", "fsdp"),
            P(None, "fsdp", "tensor"),
            P(None, "tensor"),
            P(None, "tensor", "fsdp"),
            P(),
        ),
        check_vma=False,
    )
```

```python
from functools import partial

import jax
import jax.numpy as jnp
from jax import lax
from jax.experimental import pallas as pl
from jax.experimental.pallas import tpu as pltpu
from jax.sharding import PartitionSpec as P

HEAD = 64
LANES = 128
BLOCK = 48
EPSILON = 1e-05
BF = jnp.bfloat16
F32 = jnp.float32
GELU_C = 0.7978845608028654
GELU_A = 0.044715
MIB = 1 << 20


def dot(a, b):
    return lax.dot_general(a, b, (((1,), (0,)), ((), ())), preferred_element_type=F32)


def dot_nt(a, b):
    return lax.dot_general(a, b, (((1,), (1,)), ((), ())), preferred_element_type=F32)


def dot_tn(a, b):
    return lax.dot_general(a, b, (((0,), (0,)), ((), ())), preferred_element_type=F32)


def vmem(mib):
    return pltpu.CompilerParams(vmem_limit_bytes=mib * MIB)


def cost(flops, moved, exps=0):
    return pl.CostEstimate(flops=flops, transcendentals=exps, bytes_accessed=moved)


VMEM = pl.BlockSpec(memory_space=pltpu.VMEM)


def shape(dims, kind):
    return jax.ShapeDtypeStruct(tuple(dims), kind)


def across(value, count, stride):
    return lax.ppermute(value, "fsdp", [(place, place ^ stride) for place in range(count)])


def swap(value):
    return lax.ppermute(value, "tensor", [(0, 1), (1, 0)])


def after(value, *others):
    leaves, tree = jax.tree.flatten(value)
    held = lax.optimization_barrier(tuple(leaves) + tuple(jax.tree.leaves(others)))
    return jax.tree.unflatten(tree, held[: len(leaves)])


def sync(*values):
    leaves, tree = jax.tree.flatten(values)
    return jax.tree.unflatten(tree, lax.optimization_barrier(tuple(leaves)))


def hold_kernel(value_ref, token_ref):
    del value_ref
    token_ref[...] = jnp.zeros_like(token_ref)


def hold(value, wait=2 * 10**9):
    token = pl.pallas_call(
        hold_kernel,
        name="hold",
        out_shape=shape((8, LANES), F32),
        in_specs=[pl.BlockSpec(memory_space=pl.ANY)],
        compiler_params=vmem(1),
        cost_estimate=cost(wait, 4096),
    )(value)
    return after(value, token)


def join_kernel(own_ref, got_ref, out_ref):
    half = out_ref.shape[0] // 2
    for index in range(half):
        out_ref[index] = own_ref[index] if own_ref.ndim == 3 else own_ref[...]
        out_ref[half + index] = got_ref[index] if got_ref.ndim == 3 else got_ref[...]


JOIN_WAIT = 2 * 10**9
PIECES = 1
SPLIT_WAIT = {2: 0, 4: 25 * 10**9, 8: 2 * 10**9}


def join(own, got):
    dims = own.shape[-2:]
    blocks = 2 if own.ndim == 2 else 2 * own.shape[0]
    return pl.pallas_call(
        join_kernel,
        name="join",
        out_shape=shape((blocks,) + dims, BF),
        in_specs=[VMEM] * 2,
        compiler_params=vmem(4),
        cost_estimate=cost(JOIN_WAIT, 4 * blocks * dims[0] * dims[1]),
    )(own, got)


def load_blocks(bufs, target, columns=None):
    if len(bufs) == 1:
        target[...] = bufs[0][...] if columns is None else bufs[0][:, :, columns]
        return
    me = lax.axis_index("fsdp")
    for number, buf in enumerate(bufs):
        for block in range(buf.shape[0]):
            away = (number // 2) + 2 * (number % 2) + 4 * (block // 2) + 8 * (block % 2)
            at = jnp.bitwise_xor(me, away)
            target[at] = buf[block] if columns is None else buf[block, :, columns]


def store_blocks(value, outs, rows, columns=slice(None)):
    if len(outs) == 1:
        outs[0][:, rows, columns] = value
        return
    pairs = value.reshape((value.shape[0] // 2, 2) + value.shape[1:])
    first = lax.rem(lax.axis_index("fsdp"), 2) == 0
    outs[0][:, rows, columns] = jnp.where(first, pairs[:, 0], pairs[:, 1])
    sent = jnp.where(first, pairs[:, 1], pairs[:, 0])
    each = outs[1].shape[0]
    for index, out in enumerate(outs[1:]):
        out[:, rows, columns] = sent[index * each : (index + 1) * each]


def row_of(ref, layer, which):
    return ref[layer].astype(F32)[which : which + 1, :]


def statistics(rows):
    mean = jnp.mean(rows, axis=-1, keepdims=True)
    center = rows - mean
    scale = lax.rsqrt(jnp.mean(center * center, axis=-1, keepdims=True) + EPSILON)
    return (center * scale, scale)


def norm_backward(rows, grad, gain):
    unit, scale = statistics(rows)
    e = grad * gain
    back = scale * (
        e
        - jnp.mean(e, axis=-1, keepdims=True)
        - unit * jnp.mean(e * unit, axis=-1, keepdims=True)
    )
    return (
        back,
        jnp.sum(grad * unit, axis=0, keepdims=True),
        jnp.sum(grad, axis=0, keepdims=True),
    )


def column(row):
    wide = jnp.broadcast_to(row.astype(F32), (8, row.shape[1]))
    return wide.T[:, 0:1]


def place_rows(slots_ref, less, seq):
    slots = slots_ref.shape[1]
    wanted = column(slots_ref[...]) - float(less)
    places = lax.broadcasted_iota(jnp.int32, (slots, seq), 1).astype(F32)
    return wanted == places


def place_columns(slots_ref, less, seq):
    slots = slots_ref.shape[1]
    wanted = slots_ref[...] - less
    places = lax.broadcasted_iota(jnp.int32, (seq, slots), 0)
    return wanted == places


def ones(hit):
    return jnp.where(hit, 1.0, 0.0).astype(BF)


def exact_pick(hit, value):
    high = value.astype(BF)
    rest = value - high.astype(F32)
    middle = rest.astype(BF)
    low = (rest - middle.astype(F32)).astype(BF)
    return dot(hit, high) + dot(hit, middle) + dot(hit, low)


def pack_kernel(jt_ref, mt_ref, a_ref):
    rows = mt_ref.shape[1]
    for which in range(3):
        a_ref[which * rows : (which + 1) * rows, :] = jt_ref[0, which]
    a_ref[3 * rows :, :] = mt_ref[0]


def start_kernel(
    jt_ref, mt_ref, ex_ref, sh_ref, x_ref, gain_ref, shift_ref,
    n_ref, e0_ref, s0_ref, a1_ref, e1_ref, s1_ref,
):
    unit, _ = statistics(x_ref[...].astype(F32))
    n_ref[...] = (unit * row_of(gain_ref, 0, 0) + row_of(shift_ref, 0, 0)).astype(BF)
    rows = mt_ref.shape[1]
    for which in range(3):
        a1_ref[which * rows : (which + 1) * rows, :] = jt_ref[1, which]
    a1_ref[3 * rows :, :] = mt_ref[1]
    for layer, (e_ref, s_ref) in enumerate(((e0_ref, s0_ref), (e1_ref, s1_ref))):
        e_ref[...] = ex_ref[layer]
        s_ref[...] = sh_ref[layer]


def segment_row(seg_ref, peer):
    mine = lax.axis_index("tensor")
    which = (1 - mine) if peer else mine
    both = seg_ref[...].astype(F32)
    row = jnp.where(which == 0, both[0:1, :], both[1:2, :])
    return row


def lane_masks(rows):
    lane = lax.broadcasted_iota(jnp.int32, (rows, LANES), 1)
    return (lane < HEAD, lane >= HEAD)


def attend_forward_kernel(count, layer, peer, arrays, n_ref, seg_ref, bias_ref, *refs):
    bufs = refs[:arrays]
    part_ref, q_ref, k_ref, v_ref, mixed_ref, w_ref, neg_ref = refs[arrays:]
    load_blocks(bufs, w_ref)
    seq, d = n_ref.shape
    width = q_ref.shape[1]
    half = seq // 2
    row = segment_row(seg_ref, peer)
    rows = lax.broadcasted_iota(jnp.int32, (seq, seq), 0)
    cols = lax.broadcasted_iota(jnp.int32, (seq, seq), 1)
    allowed = (column(row) == row) & (cols <= rows)
    neg_ref[...] = jnp.where(allowed, 0.0, -1e30)
    n = n_ref[...]

    def weight(which):
        return w_ref[:, which * BLOCK : (which + 1) * BLOCK, :].reshape(d, width)

    q_ref[...] = (dot(n, weight(0)) + row_of(bias_ref, layer, 0)).astype(BF)
    k_ref[...] = dot(n, weight(1)).astype(BF)
    v_ref[...] = (dot(n, weight(2)) + row_of(bias_ref, layer, 1)).astype(BF)
    masks = lane_masks(half)
    for pair in range(width // LANES):
        lanes = slice(pair * LANES, (pair + 1) * LANES)
        for part in range(2):
            top = slice(part * half, (part + 1) * half)
            keys = slice(0, (part + 1) * half)
            qp = q_ref[top, lanes] * BF(HEAD ** (-0.5))
            kp = k_ref[keys, lanes]
            vp = v_ref[keys, lanes]
            found = []
            for mask in masks:
                s = dot_nt(jnp.where(mask, qp, BF(0)), kp) + neg_ref[top, keys]
                e = jnp.exp(s - jnp.max(s, axis=-1, keepdims=True))
                scale = 1.0 / jnp.sum(e, axis=-1, keepdims=True)
                found.append(dot((e * scale).astype(BF), vp))
            mixed_ref[top, lanes] = jnp.where(masks[0], found[0], found[1]).astype(BF)
    part_ref[...] = dot_nt(mixed_ref[...], weight(3)).astype(BF)


def attend_forward(count, layer, peer, n, segments, bias, bufs):
    seq, d = n.shape
    width = bufs[0].shape[-1]
    rows = shape((seq, width), BF)
    return pl.pallas_call(
        partial(attend_forward_kernel, count, layer, peer, len(bufs)),
        name="attend_forward",
        out_shape=[shape((seq, d), BF), rows, rows, rows, rows],
        in_specs=[VMEM] * (3 + len(bufs)),
        scratch_shapes=[
            pltpu.VMEM((d // BLOCK, 4 * BLOCK, width), BF),
            pltpu.VMEM((seq, seq), F32),
        ],
        compiler_params=vmem(16),
        cost_estimate=cost(
            8 * seq * d * width + 4 * seq * seq * width,
            8 * d * width + 4 * seq * d + 8 * seq * width,
            seq * seq * width // HEAD,
        ),
    )(n, segments, bias, *bufs)


def attend_backward_kernel(
    count, layer, peer, picked, arrays,
    q_ref, k_ref, v_ref, gm_ref, seg_ref, slots_ref, *refs,
):
    bufs = refs[:arrays]
    refs = refs[arrays:]
    if picked:
        gn_ref, dj_ref, gb_ref, wide_ref, w_ref, neg_ref, gx_ref, qx_ref = refs
    else:
        gn_ref, dj_ref, gb_ref, w_ref, neg_ref, gx_ref = refs
    load_blocks(bufs, w_ref)
    seq, width = q_ref.shape
    d = gm_ref.shape[1]
    half = seq // 2
    row = segment_row(seg_ref, peer)
    if picked:
        slots = gm_ref.shape[0]
        hit = place_rows(slots_ref, 1, seq)
        at = column(slots_ref[...]) - 1.0
        own = jnp.sum(jnp.where(hit, row, 0.0), axis=-1, keepdims=True)
        cols = lax.broadcasted_iota(jnp.int32, (slots, seq), 1).astype(F32)
        neg_ref[...] = jnp.where((own == row) & (cols <= at), 0.0, -1e30)
        qx_ref[...] = dot(ones(hit), q_ref[...]).astype(BF)
        parts = [(slice(0, slots), slice(0, seq))]
        queries = qx_ref
    else:
        rows = lax.broadcasted_iota(jnp.int32, (seq, seq), 0)
        cols = lax.broadcasted_iota(jnp.int32, (seq, seq), 1)
        allowed = (column(row) == row) & (cols <= rows)
        neg_ref[...] = jnp.where(allowed, 0.0, -1e30)
        parts = [
            (slice(part * half, (part + 1) * half), slice(0, (part + 1) * half))
            for part in range(2)
        ]
        queries = q_ref

    def weight(which):
        return w_ref[:, which * BLOCK : (which + 1) * BLOCK, :].reshape(d, width)

    gx_ref[...] = dot(gm_ref[...], weight(3)).astype(BF)
    if picked:
        back = ones(place_columns(slots_ref, 1, seq))
        wide_ref[...] = dot(back, gm_ref[...]).astype(BF)
    masks = lane_masks(parts[0][0].stop)
    for pair in range(width // LANES):
        lanes = slice(pair * LANES, (pair + 1) * LANES)
        dk = [None, None]
        dv = [None, None]
        dq_all = []
        for top, keys in parts:
            qp = queries[top, lanes]
            kp = k_ref[keys, lanes]
            vp = v_ref[keys, lanes]
            gp = gx_ref[top, lanes]
            dq, dk_now, dv_now = [], [], []
            for mask in masks:
                qm = jnp.where(mask, qp, BF(0)) * BF(HEAD ** (-0.5))
                s = dot_nt(qm, kp) + neg_ref[top, keys]
                e = jnp.exp(s - jnp.max(s, axis=-1, keepdims=True))
                p = e * (1.0 / jnp.sum(e, axis=-1, keepdims=True))
                gprobs = dot_nt(jnp.where(mask, gp, BF(0)), vp)
                inner = jnp.sum(gprobs * p, axis=-1, keepdims=True)
                ds = (p * (gprobs - inner) * HEAD ** (-0.5)).astype(BF)
                dq.append(dot(ds, kp))
                dk_now.append(dot_tn(ds, qp))
                dv_now.append(dot_tn(p.astype(BF), gp))
            dq_all.append(jnp.where(masks[0], dq[0], dq[1]))
            key_mask = lane_masks(half)[0]
            for block in range(keys.stop // half):
                at = slice(block * half, (block + 1) * half)
                k_new = jnp.where(key_mask, dk_now[0][at], dk_now[1][at])
                v_new = jnp.where(key_mask, dv_now[0][at], dv_now[1][at])
                dk[block] = k_new if dk[block] is None else dk[block] + k_new
                dv[block] = v_new if dv[block] is None else dv[block] + v_new
        gb_ref[0:1, lanes] = sum(jnp.sum(one, axis=0, keepdims=True) for one in dq_all)
        gb_ref[1:2, lanes] = sum(jnp.sum(one, axis=0, keepdims=True) for one in dv)
        if picked:
            dj_ref[0, :, lanes] = dot(back, dq_all[0].astype(BF)).astype(BF)
        else:
            for (top, _), one in zip(parts, dq_all):
                dj_ref[0, top, lanes] = one.astype(BF)
        for block in range(2):
            at = slice(block * half, (block + 1) * half)
            dj_ref[1, at, lanes] = dk[block].astype(BF)
            dj_ref[2, at, lanes] = dv[block].astype(BF)
    gn = dot_nt(dj_ref[0], weight(0))
    gn = gn + dot_nt(dj_ref[1], weight(1))
    gn = gn + dot_nt(dj_ref[2], weight(2))
    gn_ref[...] = gn.astype(BF)


def attend_backward(count, layer, peer, kept, gm, segments, slots, bufs, picked):
    q, k, v = kept
    seq, width = q.shape
    rows, d = gm.shape
    outs = [shape((seq, d), BF), shape((3, seq, width), BF), shape((2, width), F32)]
    scratch = [
        pltpu.VMEM((d // BLOCK, 4 * BLOCK, width), BF),
        pltpu.VMEM((rows, seq), F32),
        pltpu.VMEM((rows, width), BF),
    ]
    if picked:
        outs.append(shape((seq, d), BF))
        scratch.append(pltpu.VMEM((rows, width), BF))
    return pl.pallas_call(
        partial(attend_backward_kernel, count, layer, peer, picked, len(bufs)),
        name="attend_backward",
        out_shape=outs,
        in_specs=[VMEM] * (6 + len(bufs)),
        scratch_shapes=scratch,
        compiler_params=vmem(16),
        cost_estimate=cost(
            2 * rows * d * width + 6 * seq * d * width + 10 * rows * seq * width,
            8 * d * width + 4 * seq * d + 12 * seq * width,
            rows * seq * width // HEAD,
        ),
    )(q, k, v, gm, segments, slots, *bufs)


def attend_grads_kernel(n0_ref, n1_ref, d0_ref, d1_ref, g0_ref, g1_ref, m0_ref, m1_ref, *outs):
    d = n0_ref.shape[1]
    width = m0_ref.shape[1]
    groups = d // BLOCK
    nt = [n0_ref[...].T, n1_ref[...].T]
    for which in range(3):
        total = dot(nt[0], d0_ref[which]) + dot(nt[1], d1_ref[which])
        store_blocks(
            total.astype(BF).reshape(groups, BLOCK, width),
            outs,
            slice(which * BLOCK, (which + 1) * BLOCK),
        )
    total = dot(g0_ref[...].T, m0_ref[...]) + dot(g1_ref[...].T, m1_ref[...])
    store_blocks(
        total.astype(BF).reshape(groups, BLOCK, width), outs, slice(3 * BLOCK, 4 * BLOCK)
    )


def grad_shapes(count, groups, rows, width, split, pieces=1):
    if split:
        blocks = count // 2
        return [shape((blocks, rows, width), BF)] + [
            shape((blocks // pieces, rows, width), BF)
        ] * pieces
    return [shape((groups, rows, width), BF)]


def attend_grads(count, split, n, dj, gm, mixed):
    seq, d = n[0].shape
    width = mixed[0].shape[1]
    outs = grad_shapes(count, d // BLOCK, 4 * BLOCK, width, split, PIECES)
    return pl.pallas_call(
        attend_grads_kernel,
        name="attend_grads",
        out_shape=outs,
        in_specs=[VMEM] * 8,
        compiler_params=vmem(16),
        cost_estimate=cost(16 * seq * d * width, 16 * d * width + 8 * seq * d),
    )(*n, *dj, *gm, *mixed)


def chunk_of(hidden):
    return 512 if hidden % 512 == 0 else hidden


def mlp_forward_kernel(count, layer, arrays, n0_ref, n1_ref, be_ref, *refs):
    e_bufs, s_bufs = refs[:arrays], refs[arrays : 2 * arrays]
    out0_ref, out1_ref, n_ref, acc_ref, we_ref, ws_ref = refs[2 * arrays :]
    rows, d = n0_ref.shape
    hidden = e_bufs[0].shape[2]
    chunk = chunk_of(hidden)
    n_ref[:rows, :] = n0_ref[...]
    n_ref[rows:, :] = n1_ref[...]
    acc_ref[...] = jnp.zeros_like(acc_ref)

    @pl.loop(0, hidden // chunk)
    def _(index):
        cols = pl.ds(pl.multiple_of(index * chunk, chunk), chunk)
        load_blocks(e_bufs, we_ref, cols)
        load_blocks(s_bufs, ws_ref, cols)
        shift = be_ref[:, cols].astype(F32)[layer : layer + 1, :]
        u = dot(n_ref[...], we_ref[...].reshape(d, chunk)) + shift
        t = jnp.tanh(GELU_C * (u + GELU_A * (u * u * u)))
        active = (0.5 * u * (1.0 + t)).astype(BF)
        acc_ref[...] = acc_ref[...] + dot_nt(active, ws_ref[...].reshape(d, chunk))

    out0_ref[...] = acc_ref[:rows, :].astype(BF)
    out1_ref[...] = acc_ref[rows:, :].astype(BF)


def mlp_forward(count, layer, n, be, e_bufs, s_bufs):
    rows, d = n[0].shape
    hidden = e_bufs[0].shape[-1]
    return pl.pallas_call(
        partial(mlp_forward_kernel, count, layer, len(e_bufs)),
        name="mlp_forward",
        out_shape=[shape((rows, d), BF)] * 2,
        in_specs=[VMEM] * (3 + 2 * len(e_bufs)),
        scratch_shapes=[
            pltpu.VMEM((2 * rows, d), BF),
            pltpu.VMEM((2 * rows, d), F32),
            pltpu.VMEM((d // BLOCK, BLOCK, chunk_of(hidden)), BF),
            pltpu.VMEM((d // BLOCK, BLOCK, chunk_of(hidden)), BF),
        ],
        compiler_params=vmem(16),
        cost_estimate=cost(
            8 * rows * d * hidden, 4 * d * hidden + 8 * rows * d, 2 * rows * hidden
        ),
    )(*n, be, *e_bufs, *s_bufs)


def mlp_backward_kernel(count, layer, arrays, full, outputs, n0_ref, n1_ref, g0_ref, g1_ref, be_ref, *refs):
    e_bufs, s_bufs = refs[:arrays], refs[arrays : 2 * arrays]
    refs = refs[2 * arrays :]
    if full:
        out0_ref, out1_ref, refs = refs[0], refs[1], refs[2:]
    gn0_ref, gn1_ref, gb_ref = refs[:3]
    outs = refs[3 : 3 + outputs]
    refs = refs[3 + outputs :]
    n_ref, g_ref, nt_ref, gt_ref, gacc_ref, we_ref, ws_ref = refs[:7]
    if full:
        acc_ref = refs[7]
    rows, d = n0_ref.shape
    hidden = e_bufs[0].shape[2]
    chunk = chunk_of(hidden)
    groups = d // BLOCK
    n_ref[:rows, :] = n0_ref[...]
    n_ref[rows:, :] = n1_ref[...]
    g_ref[:rows, :] = g0_ref[...]
    g_ref[rows:, :] = g1_ref[...]
    nt_ref[...] = n_ref[...].T
    gt_ref[...] = g_ref[...].T
    gacc_ref[...] = jnp.zeros_like(gacc_ref)
    if full:
        acc_ref[...] = jnp.zeros_like(acc_ref)

    @pl.loop(0, hidden // chunk)
    def _(index):
        cols = pl.ds(pl.multiple_of(index * chunk, chunk), chunk)
        load_blocks(e_bufs, we_ref, cols)
        load_blocks(s_bufs, ws_ref, cols)
        we = we_ref[...].reshape(d, chunk)
        ws = ws_ref[...].reshape(d, chunk)
        shift = be_ref[:, cols].astype(F32)[layer : layer + 1, :]
        u = dot(n_ref[...], we) + shift
        square = u * u
        t = jnp.tanh(GELU_C * (u + GELU_A * (square * u)))
        lean = 0.5 * (1.0 + t)
        active = (u * lean).astype(BF)
        slope = lean + (0.5 * u) * (1.0 - t * t) * (GELU_C + (3.0 * GELU_C * GELU_A) * square)
        gh = dot(g_ref[...], ws) * slope
        gb_ref[:, cols] = jnp.sum(gh, axis=0, keepdims=True)
        gh = gh.astype(BF)
        ge = dot(nt_ref[...], gh).astype(BF)
        gs = dot(gt_ref[...], active).astype(BF)
        ge, gs = ge.reshape(groups, BLOCK, chunk), gs.reshape(groups, BLOCK, chunk)
        if full:
            store_blocks(ge, outs[: outputs // 2], slice(0, BLOCK), cols)
            store_blocks(gs, outs[outputs // 2 :], slice(0, BLOCK), cols)
        else:
            store_blocks(ge, outs, slice(0, BLOCK), cols)
            store_blocks(gs, outs, slice(BLOCK, 2 * BLOCK), cols)
        gacc_ref[...] = gacc_ref[...] + dot_nt(gh, we)
        if full:
            acc_ref[...] = acc_ref[...] + dot_nt(active, ws)

    gn0_ref[...] = gacc_ref[:rows, :].astype(BF)
    gn1_ref[...] = gacc_ref[rows:, :].astype(BF)
    if full:
        out0_ref[...] = acc_ref[:rows, :].astype(BF)
        out1_ref[...] = acc_ref[rows:, :].astype(BF)


def mlp_backward(count, layer, split, n, g, be, e_bufs, s_bufs, full):
    rows, d = n[0].shape
    hidden = e_bufs[0].shape[-1]
    groups = d // BLOCK
    half = shape((rows, d), BF)
    if full:
        grads = 2 * grad_shapes(count, groups, BLOCK, hidden, split)
    else:
        grads = grad_shapes(count, groups, 2 * BLOCK, hidden, split)
    blocks = pltpu.VMEM((groups, BLOCK, chunk_of(hidden)), BF)
    return pl.pallas_call(
        partial(mlp_backward_kernel, count, layer, len(e_bufs), full, len(grads)),
        name="mlp_backward",
        out_shape=[half] * (4 if full else 2) + [shape((1, hidden), F32)] + grads,
        in_specs=[VMEM] * (5 + 2 * len(e_bufs)),
        scratch_shapes=[
            pltpu.VMEM((2 * rows, d), BF),
            pltpu.VMEM((2 * rows, d), BF),
            pltpu.VMEM((d, 2 * rows), BF),
            pltpu.VMEM((d, 2 * rows), BF),
            pltpu.VMEM((2 * rows, d), F32),
            blocks,
            blocks,
        ]
        + ([pltpu.VMEM((2 * rows, d), F32)] if full else []),
        compiler_params=vmem(28),
        cost_estimate=cost(
            (24 if full else 20) * rows * d * hidden,
            8 * d * hidden + 16 * rows * d,
            2 * rows * hidden,
        ),
    )(*n, *g, be, *e_bufs, *s_bufs)


def middle_kernel(layer, x_ref, own_ref, got_ref, slots_ref, gain_ref, shift_ref, bias_ref, *outs):
    middle = (
        x_ref[...].astype(F32)
        + (own_ref[...].astype(F32) + got_ref[...].astype(F32))
        + row_of(bias_ref, layer, 0)
    )
    unit, _ = statistics(middle)
    normed = (unit * row_of(gain_ref, layer, 1) + row_of(shift_ref, layer, 1)).astype(BF)
    outs[0][...] = middle
    outs[1][...] = normed
    if layer == 0:
        hit = ones(place_rows(slots_ref, 1, x_ref.shape[0]))
        outs[2][...] = exact_pick(hit, middle)
        outs[3][...] = dot(hit, normed).astype(BF)


def second_kernel(
    x_ref, mid_ref, own_ref, got_ref, slots_ref, gain_ref, shift_ref, bias_ref, out_ref, n_ref
):
    seq = x_ref.shape[0]
    latent = (
        mid_ref[...]
        + (own_ref[...].astype(F32) + got_ref[...].astype(F32))
        + row_of(bias_ref, 0, 1)
    )
    known = column(slots_ref[...]) >= 1.0
    latent = jnp.where(known, latent, 0.0).astype(BF)
    hit = place_columns(slots_ref, 0, seq)
    occupied = jnp.sum(jnp.where(hit, 1.0, 0.0), axis=-1, keepdims=True)
    second = x_ref[...].astype(F32) * (1.0 - occupied) + dot(ones(hit), latent)
    unit, _ = statistics(second)
    out_ref[...] = second
    n_ref[...] = (unit * row_of(gain_ref, 1, 0) + row_of(shift_ref, 1, 0)).astype(BF)


def grad_middle_kernel(mid_ref, own_ref, got_ref, cot_ref, gain_ref, out_ref, low_ref, sum_ref):
    cot = cot_ref[...].astype(F32)
    grad = own_ref[...].astype(F32) + got_ref[...].astype(F32)
    back, gain, shift = norm_backward(mid_ref[...], grad, row_of(gain_ref, 1, 1))
    total = cot + back
    out_ref[...] = total
    low_ref[...] = total.astype(BF)
    sum_ref[0:1, :] = gain
    sum_ref[1:2, :] = shift
    sum_ref[2:3, :] = jnp.sum(total, axis=0, keepdims=True)
    sum_ref[3:4, :] = jnp.sum(cot, axis=0, keepdims=True)


def grad_second_kernel(
    x_ref, own_ref, got_ref, gm_ref, slots_ref, gain_ref, out_ref, pick_ref, low_ref, sum_ref
):
    grad = own_ref[...].astype(F32) + got_ref[...].astype(F32)
    back, gain, shift = norm_backward(x_ref[...], grad, row_of(gain_ref, 1, 0))
    total = gm_ref[...] + back
    out_ref[...] = total
    hit = place_rows(slots_ref, 0, x_ref.shape[0])
    known = column(slots_ref[...]) >= 1.0
    pick = jnp.where(known, exact_pick(ones(hit), total), 0.0)
    pick_ref[...] = pick
    low_ref[...] = pick.astype(BF)
    sum_ref[0:1, :] = gain
    sum_ref[1:2, :] = shift


def grad_picked_kernel(mid_ref, own_ref, got_ref, pick_ref, gain_ref, out_ref, low_ref, sum_ref):
    grad = own_ref[...].astype(F32) + got_ref[...].astype(F32)
    back, gain, shift = norm_backward(mid_ref[...], grad, row_of(gain_ref, 0, 1))
    pick = pick_ref[...]
    total = pick + back
    out_ref[...] = total
    low_ref[...] = total.astype(BF)
    sum_ref[0:1, :] = gain
    sum_ref[1:2, :] = shift
    sum_ref[2:3, :] = jnp.sum(total, axis=0, keepdims=True)
    sum_ref[3:4, :] = jnp.sum(pick, axis=0, keepdims=True)


def grad_first_kernel(
    x_ref, own_ref, got_ref, gm_ref, second_ref, slots_ref, gain_ref,
    s22_ref, s21_ref, s12_ref, pair1_ref, pair0_ref, peer1_ref, peer0_ref, be1_ref, be0_ref,
    out_ref, sum_ref,
):
    seq, d = x_ref.shape
    grad = own_ref[...].astype(F32) + got_ref[...].astype(F32)
    back, gain, shift = norm_backward(x_ref[...].astype(F32), grad, row_of(gain_ref, 0, 0))
    hit = place_columns(slots_ref, 0, seq)
    occupied = jnp.sum(jnp.where(hit, 1.0, 0.0), axis=-1, keepdims=True)
    source = ones(place_columns(slots_ref, 1, seq))
    out_ref[...] = second_ref[...] * (1.0 - occupied) + (exact_pick(source, gm_ref[...]) + back)
    width = pair0_ref.shape[1]
    for index, row in enumerate(
        (
            gain, s12_ref[0:1, :], s21_ref[0:1, :], s22_ref[0:1, :],
            shift, s12_ref[1:2, :], s21_ref[1:2, :], s22_ref[1:2, :],
            s12_ref[2:3, :], s12_ref[3:4, :], s22_ref[2:3, :], s22_ref[3:4, :],
        )
    ):
        for part in range(d // width):
            at = index * (d // width) + part
            sum_ref[at : at + 1, :] = row[:, part * width : (part + 1) * width]
    first = 12 * (d // width)
    sum_ref[first : first + 2, :] = pair0_ref[...] + peer0_ref[...]
    sum_ref[first + 2 : first + 4, :] = pair1_ref[...] + peer1_ref[...]
    hidden = be0_ref.shape[1]
    for layer, ref in enumerate((be0_ref, be1_ref)):
        for part in range(hidden // width):
            at = first + 4 + layer * (hidden // width) + part
            sum_ref[at : at + 1, :] = ref[0:1, part * width : (part + 1) * width]


def vectors_kernel(sum_ref, gains_ref, shifts_ref, branch_ref, pair_ref, hidden_ref):
    d = gains_ref.shape[2]
    width = sum_ref.shape[1]
    index = 0
    for ref in (gains_ref, shifts_ref, branch_ref):
        for layer in range(2):
            for which in range(2):
                for part in range(d // width):
                    ref[layer, which : which + 1, part * width : (part + 1) * width] = sum_ref[
                        index : index + 1, :
                    ]
                    index += 1
    for layer in range(2):
        pair_ref[layer] = sum_ref[index : index + 2, :]
        index += 2
    for layer in range(2):
        for part in range(hidden_ref.shape[1] // width):
            hidden_ref[layer : layer + 1, part * width : (part + 1) * width] = sum_ref[
                index : index + 1, :
            ]
            index += 1


def small(kernel, name, outs, *args):
    moved = sum(a.size * a.dtype.itemsize for a in args) + sum(
        o.size * o.dtype.itemsize for o in outs
    )
    return pl.pallas_call(
        kernel,
        name=name,
        out_shape=outs,
        in_specs=[VMEM] * len(args),
        compiler_params=vmem(24),
        cost_estimate=cost(4 * moved, moved),
    )(*args)


def split_kernel(stride, keep_ref, *refs):
    *got_refs, kept_ref, sent_ref = refs
    each = got_refs[0].shape[0]
    bit = lax.rem(lax.axis_index("fsdp") // stride, 2)
    for index in range(kept_ref.shape[0]):
        got_ref, first = got_refs[2 * index // each], 2 * index // each * each
        for out, place in ((kept_ref, bit), (sent_ref, 1 - bit)):
            at = 2 * index + place
            got = got_ref[at - first].astype(F32)
            out[index] = (keep_ref[at].astype(F32) + got).astype(BF)


def split(stride, keep, *got):
    blocks, rows, width = keep.shape
    return pl.pallas_call(
        partial(split_kernel, stride),
        name="split",
        out_shape=[shape((blocks // 2, rows, width), BF)] * 2,
        in_specs=[VMEM] * (1 + len(got)),
        compiler_params=vmem(8),
        cost_estimate=cost(keep.size + SPLIT_WAIT[stride], 6 * keep.size),
    )(keep, *got)


def finish_kernel(counts, *refs):
    joint_ref, merge_ref, expand_ref, shrink_ref = refs[-4:]
    totals = []
    first = 0
    for number in counts:
        total = refs[first][0].astype(F32)
        for ref in refs[first + 1 : first + number]:
            total = total + ref[0].astype(F32)
        totals.append(total)
        first += number
    rows = merge_ref.shape[1]
    attend, both = totals[:2]
    half = both.shape[0] // 2
    sums = ((attend, both[:half, :], both[half:, :]), totals[2:])
    for layer, (attend, expand, shrink) in enumerate(sums):
        for which in range(3):
            joint_ref[layer, which] = attend[which * rows : (which + 1) * rows, :]
        merge_ref[layer] = attend[3 * rows :, :]
        expand_ref[layer] = expand
        shrink_ref[layer] = shrink


def finish(states):
    _, rows, width = states[0][0].shape
    hidden = states[1][0].shape[2]
    rows = rows // 4
    outs = [shape((2, 3, rows, width), F32), shape((2, rows, width), F32)]
    outs += [shape((2, rows, hidden), F32)] * 2
    counts = tuple(len(state) for state in states)
    return small(
        partial(finish_kernel, counts), "finish", outs, *[one for state in states for one in state]
    )


def regroup(array, count, kinds):
    rows = array.shape[0] * array.shape[1] // kinds // BLOCK
    each = array.shape[1] // kinds
    width = array.shape[2]
    split = array.reshape(array.shape[0], kinds, each, width).transpose(1, 0, 2, 3)
    return split.reshape(kinds, rows, BLOCK, width).transpose(1, 0, 2, 3).reshape(
        rows, kinds * BLOCK, width
    )


def ungroup(array, count, kinds):
    width = array.shape[2]
    split = array.reshape(array.shape[0], kinds, BLOCK, width).transpose(1, 0, 2, 3)
    each = array.shape[0] * BLOCK // count
    return split.reshape(kinds, count, each, width).transpose(1, 0, 2, 3).reshape(
        count, kinds * each, width
    )


def shards(
    count,
    embedded,
    segments,
    thoughts,
    cotangent,
    gains,
    shifts,
    joint_weight,
    joint_bias,
    merge_weight,
    expand_weight,
    expand_bias,
    shrink_weight,
    branch_biases,
):
    seq, d = embedded.shape
    rows_each = joint_weight.shape[1]
    width = joint_weight.shape[3]
    hidden = expand_weight.shape[2]
    slots = thoughts.shape[1]
    staged = rows_each == BLOCK and count == 16
    rows_f32, rows_bf = shape((seq, d), F32), shape((seq, d), BF)
    few_f32, few_bf = shape((slots, d), F32), shape((slots, d), BF)
    ins = (
        joint_weight.transpose(0, 2, 1, 3),
        merge_weight.transpose(0, 2, 1),
        expand_weight,
        shrink_weight.transpose(0, 2, 1),
    )
    bufs = {}

    def first_step(own, *others):
        return join(after(own, *others), across(own, count, 8))

    def next_step(own, *others):
        return join(after(own, *others), across(own, count, 4))

    def third_step(own):
        return (own, across(own, count, 2))

    def last_step(both):
        return [*both, across(both[0], count, 1), across(both[1], count, 1)]

    if staged:
        attend, plain = shape((4 * rows_each, width), BF), shape((rows_each, hidden), BF)
        (a0,) = small(pack_kernel, "pack", [attend], *ins[:2])
        normed, e0, s0, a1, e1, s1 = small(
            start_kernel, "start", [rows_bf, plain, plain, attend, plain, plain],
            *ins, embedded, gains, shifts,
        )
    else:
        first = embedded.astype(F32)
        center = first - jnp.mean(first, axis=-1, keepdims=True)
        scale = lax.rsqrt(jnp.mean(center * center, axis=-1, keepdims=True) + EPSILON)
        normed = (
            center * scale * gains[0, 0].astype(F32) + shifts[0, 0].astype(F32)
        ).astype(BF)
        for layer in range(2):
            attend = jnp.concatenate(
                (ins[0][layer].reshape(3 * rows_each, width), ins[1][layer]), axis=0
            )
            for name, one, kind in (("a", attend, 4), ("e", ins[2][layer], 1), ("s", ins[3][layer], 1)):
                whole = lax.all_gather(one, "fsdp", axis=0, tiled=False)
                bufs[f"{name}{layer}"] = [regroup(whole, count, kind)]

    slots_peer = swap(thoughts)
    normed_peer = swap(normed)

    if staged:
        a0, e0 = sync(first_step(a0), e0)
        cot_peer = hold(swap(cotangent), 4 * 10**9)
        a0, e0, s0, cot_peer = sync(next_step(a0, cot_peer), first_step(e0), s0, cot_peer)
        a0, e0, s0, a1, normed_peer, slots_peer = sync(
            third_step(a0), next_step(e0), first_step(s0), a1, normed_peer, slots_peer
        )
        bufs["a0"] = last_step(a0)
    else:
        cot_peer = swap(cotangent)

    def attention(layer, own, peer):
        weights = bufs[f"a{layer}"]
        part_peer, *kept_peer = attend_forward(count, layer, True, peer, segments, joint_bias, weights)
        got = swap(part_peer)
        part_own, *kept_own = attend_forward(
            count, layer, False, after(own, part_peer), segments, joint_bias, weights
        )
        return (part_own, got, (own, peer), (kept_own, kept_peer))

    part, got, n_one, kept_one = attention(0, normed, normed_peer)
    if staged:
        e0, s0, a1, part, e1 = sync(
            third_step(e0), next_step(s0, part), first_step(a1, part), part, e1
        )
        bufs["e0"] = last_step(e0)
    middle_one, n2_one, middle_few, n2_few = small(
        partial(middle_kernel, 0), "middle", [rows_f32, rows_bf, few_f32, few_bf],
        embedded, part, got, thoughts, gains, shifts, branch_biases,
    )
    n2_few = (n2_few, swap(n2_few))
    if staged:
        s0, a1, e1, s1, bufs["e0"] = sync(
            third_step(s0), next_step(a1, n2_few[0]), first_step(e1, n2_few[0]), s1, bufs["e0"]
        )
        bufs["s0"] = last_step(s0)
    own, peer = mlp_forward(count, 0, n2_few, expand_bias, bufs["e0"], bufs["s0"])
    second, normed = small(
        second_kernel, "second", [rows_f32, rows_bf],
        embedded, middle_few, own, swap(peer), thoughts, gains, shifts, branch_biases,
    )
    normed_peer = swap(normed)

    if staged:
        a1, e1, s1, normed, normed_peer = sync(
            third_step(a1), next_step(e1, normed), first_step(s1, normed), normed, normed_peer
        )
        bufs["a1"] = last_step(a1)
    part, got, n_two, kept_two = attention(1, normed, normed_peer)
    if staged:
        e1, s1, part = sync(third_step(e1), next_step(s1, part), part)
        bufs["e1"] = last_step(e1)
    middle_two, n2_two = small(
        partial(middle_kernel, 1), "middle", [rows_f32, rows_bf],
        second, part, got, thoughts, gains, shifts, branch_biases,
    )
    n2_peer = swap(n2_two)
    if staged:
        s1, n2_two, n2_peer, bufs["e1"] = sync(third_step(s1), n2_two, n2_peer, bufs["e1"])
        bufs["s1"] = last_step(s1)
    own_two, peer_two, gn_own, gn_peer, gb_two, *grads = mlp_backward(
        count, 1, staged, (n2_two, n2_peer), (cotangent, cot_peer),
        expand_bias, bufs["e1"], bufs["s1"], True,
    )

    def begin(grads, kind):
        if staged:
            return (grads[0], *[across(sent, count, 1) for sent in grads[1:]])
        done = lax.psum_scatter(
            ungroup(grads[0], count, kind), "fsdp", scatter_dimension=0, tiled=False
        )
        return (done[None],)

    def settle(state, stride, *others):
        return tuple(split(stride, *after(state, *others))) if staged else state

    def move(state, stride):
        return (state[0], across(state[1], count, stride)) if staged else state

    def apart(grads):
        return (grads[: len(grads) // 2], grads[len(grads) // 2 :])

    e1, s1 = apart(grads)
    got = swap(gn_peer)
    s1, e1, got, gn_own = sync(settle(begin(s1, 1), 2), settle(begin(e1, 1), 2), got, gn_own)
    s1 = move(s1, 2)
    gm, gm_low, s22 = small(
        grad_middle_kernel, "grad_middle", [rows_f32, rows_bf, shape((4, d), F32)],
        middle_two, gn_own, got, cotangent, gains,
    )
    gm_peer = swap(gm_low)
    weights = bufs["a1"]
    back_peer = attend_backward(
        count, 1, True, kept_two[1][:3], gm_peer, segments, slots_peer, weights, False
    )
    s1, e1, back_peer, gm_low = sync(settle(s1, 4, back_peer[0]), e1, back_peer, gm_low)
    got = swap(back_peer[0])
    s1, e1 = move(s1, 4), move(e1, 2)
    back_own = attend_backward(
        count, 1, False, kept_two[0][:3], gm_low, segments, thoughts, weights, False
    )
    a1 = attend_grads(
        count, staged, n_two, (after(back_own[1], got), back_peer[1]), (gm_low, gm_peer),
        (kept_two[0][3], kept_two[1][3]),
    )
    s1 = settle(s1, 8, a1)
    e1 = settle(e1, 4, s1)
    s1, e1, a1, got, own = sync(s1, e1, settle(begin(a1, 4), 2, e1), got, back_own[0])
    s1, e1, a1 = move(s1, 8), move(e1, 4), move(a1, 2)
    grad_second, g_few, g_low, s21 = small(
        grad_second_kernel, "grad_second", [rows_f32, few_f32, few_bf, shape((2, d), F32)],
        second, own, got, gm, thoughts, gains,
    )
    pair_two = (back_own[2], back_peer[2])

    g_peer = swap(g_low)
    own, peer, gb_one, *m0 = mlp_backward(
        count, 0, staged, n2_few, (g_low, g_peer), expand_bias,
        bufs["e0"], bufs["s0"], False,
    )
    m0 = settle(begin(m0, 2), 2)
    gm_few, gm_low, s12 = small(
        grad_picked_kernel, "grad_picked", [few_f32, few_bf, shape((4, d), F32)],
        middle_few, own, swap(peer), g_few, gains,
    )
    gm_peer = swap(gm_low)
    e1 = settle(e1, 8, gm_low)
    a1 = settle(a1, 4, e1)
    s1, e1, a1, m0, gm_peer, gm_low = sync(s1, e1, a1, m0, gm_peer, gm_low)
    e1, a1, m0 = move(e1, 8), move(a1, 4), move(m0, 2)
    weights = bufs["a0"]
    back_peer = attend_backward(
        count, 0, True, kept_one[1][:3], gm_peer, segments, slots_peer, weights, True
    )
    got = swap(back_peer[0])
    back_own = attend_backward(
        count, 0, False, kept_one[0][:3], after(gm_low, back_peer[0], e1), segments, thoughts,
        weights, True,
    )
    a0 = attend_grads(
        count, staged, n_one, (back_own[1], back_peer[1]), (back_own[3], back_peer[3]),
        (kept_one[0][3], kept_one[1][3]),
    )
    pair_one = (back_own[2], back_peer[2])
    a1 = settle(a1, 8, a0)
    m0 = settle(m0, 4, a1)
    a1, m0, a0, got, n2_one, peer_two = sync(
        a1, m0, settle(begin(a0, 4), 2, m0), got, n2_one, peer_two
    )
    a1, m0, a0 = move(a1, 8), move(m0, 4), move(a0, 2)
    embedded_grad, vectors = small(
        grad_first_kernel, "grad_first",
        [rows_f32, shape((12 * d // width + 4 + 2 * (hidden // width), width), F32)],
        embedded, back_own[0], got, gm_few, grad_second, thoughts, gains,
        s22, s21, s12, pair_two[0], pair_one[0], pair_two[1], pair_one[1], gb_two, gb_one,
    )
    shared = jnp.arange(vectors.shape[0])[:, None] < 12 * d // width
    vectors = vectors + jnp.where(shared, swap(vectors), 0.0)
    n2_peer = swap(after(n2_one, vectors))
    if staged:
        vectors = vectors + across(vectors, count, 1)
        m0 = settle(m0, 8, embedded_grad)
        a1, m0, a0, vectors = sync(a1, m0, settle(a0, 4, m0), vectors)
        m0, a0 = move(m0, 8), move(a0, 4)
    latent_own, latent_peer = mlp_forward(
        count, 0, (n2_one, n2_peer), expand_bias, bufs["e0"], bufs["s0"]
    )
    if staged:
        vectors = vectors + across(vectors, count, 2)
        m0 = (m0[0], hold(after(m0[1], latent_own)))
        m0, a0, vectors = sync(m0, settle(a0, 8, m0), vectors)
        a0 = move(a0, 8)
        total = (vectors + across(vectors, count, 4)) + (
            across(vectors, count, 8) + across(vectors, count, 12)
        )
    else:
        total = lax.psum(vectors, "fsdp")

    biases = branch_biases.astype(F32)
    latent_peer, peer_two = swap(latent_peer), swap(peer_two)
    latent = middle_one + (latent_own.astype(F32) + latent_peer.astype(F32)) + biases[0, 1]
    language = middle_two + (own_two.astype(F32) + peer_two.astype(F32)) + biases[1, 1]

    joint_grad, merge_grad, expand_grad, shrink_grad = finish((a0, m0, a1, e1, s1))
    vector = shape((2, 2, d), F32)
    gains_grad, shifts_grad, branch_grad, joint_bias_grad, expand_bias_grad = small(
        vectors_kernel, "vectors",
        [vector, vector, vector, shape((2, 2, width), F32), shape((2, hidden), F32)],
        total,
    )
    return (
        latent.astype(BF),
        language.astype(BF),
        embedded_grad,
        gains_grad,
        shifts_grad,
        joint_grad.transpose(0, 2, 1, 3),
        joint_bias_grad,
        merge_grad.transpose(0, 2, 1),
        expand_grad,
        expand_bias_grad,
        shrink_grad.transpose(0, 2, 1),
        branch_grad,
    )


def solution(mesh):
    placed = (
        P(("fsdp", "tensor"), None),
        P("fsdp", None),
        P(("fsdp", "tensor"), None),
        P(("fsdp", "tensor"), None),
        P(),
        P(),
        P(None, "fsdp", None, "tensor"),
        P(None, None, "tensor"),
        P(None, "tensor", "fsdp"),
        P(None, "fsdp", "tensor"),
        P(None, "tensor"),
        P(None, "tensor", "fsdp"),
        P(),
    )
    return jax.shard_map(
        partial(shards, mesh.shape["fsdp"]),
        mesh=mesh,
        in_specs=placed,
        out_specs=(
            P(("fsdp", "tensor"), None),
            P(("fsdp", "tensor"), None),
            P(("fsdp", "tensor"), None),
            P(),
            P(),
            P(None, "fsdp", None, "tensor"),
            P(None, None, "tensor"),
            P(None, "tensor", "fsdp"),
            P(None, "fsdp", "tensor"),
            P(None, "tensor"),
            P(None, "tensor", "fsdp"),
            P(),
        ),
        check_vma=False,
    )
```

```python
from functools import partial

import jax
import jax.numpy as jnp
from jax import lax
from jax.experimental import pallas as pl
from jax.experimental.pallas import tpu as pltpu
from jax.sharding import PartitionSpec as P

HEAD = 64
LANES = 128
BLOCK = 48
EPSILON = 1e-05
BF = jnp.bfloat16
F32 = jnp.float32
GELU_C = 0.7978845608028654
GELU_A = 0.044715
MIB = 1 << 20


def dot(a, b):
    return lax.dot_general(a, b, (((1,), (0,)), ((), ())), preferred_element_type=F32)


def dot_nt(a, b):
    return lax.dot_general(a, b, (((1,), (1,)), ((), ())), preferred_element_type=F32)


def dot_tn(a, b):
    return lax.dot_general(a, b, (((0,), (0,)), ((), ())), preferred_element_type=F32)


def vmem(mib):
    return pltpu.CompilerParams(vmem_limit_bytes=mib * MIB)


def cost(flops, moved, exps=0):
    return pl.CostEstimate(flops=flops, transcendentals=exps, bytes_accessed=moved)


VMEM = pl.BlockSpec(memory_space=pltpu.VMEM)
ANY = pl.BlockSpec(memory_space=pl.ANY)


def shape(dims, kind):
    return jax.ShapeDtypeStruct(tuple(dims), kind)


def across(value, count, stride):
    return lax.ppermute(value, "fsdp", [(place, place ^ stride) for place in range(count)])


def swap(value):
    return lax.ppermute(value, "tensor", [(0, 1), (1, 0)])


def after(value, *others):
    leaves, tree = jax.tree.flatten(value)
    held = lax.optimization_barrier(tuple(leaves) + tuple(jax.tree.leaves(others)))
    return jax.tree.unflatten(tree, held[: len(leaves)])


def sync(*values):
    leaves, tree = jax.tree.flatten(values)
    return jax.tree.unflatten(tree, lax.optimization_barrier(tuple(leaves)))


def hold_kernel(value_ref, token_ref):
    del value_ref
    token_ref[...] = jnp.zeros_like(token_ref)


def hold(value, wait=2 * 10**9):
    token = pl.pallas_call(
        hold_kernel,
        name="hold",
        out_shape=shape((8, LANES), F32),
        in_specs=[pl.BlockSpec(memory_space=pl.ANY)],
        compiler_params=vmem(1),
        cost_estimate=cost(wait, 4096),
    )(value)
    return after(value, token)


def join_kernel(own_ref, got_ref, out_ref):
    half = out_ref.shape[0] // 2
    for index in range(half):
        out_ref[index] = own_ref[index] if own_ref.ndim == 3 else own_ref[...]
        out_ref[half + index] = got_ref[index] if got_ref.ndim == 3 else got_ref[...]


JOIN_WAIT = 2 * 10**9
PIECES = 1
SPLIT_WAIT = {2: 0, 4: 25 * 10**9, 8: 2 * 10**9}


def join(own, got):
    dims = own.shape[-2:]
    blocks = 2 if own.ndim == 2 else 2 * own.shape[0]
    return pl.pallas_call(
        join_kernel,
        name="join",
        out_shape=shape((blocks,) + dims, BF),
        in_specs=[VMEM] * 2,
        compiler_params=vmem(4),
        cost_estimate=cost(JOIN_WAIT, 4 * blocks * dims[0] * dims[1]),
    )(own, got)


def load_blocks(bufs, target, columns=None):
    if len(bufs) == 1:
        target[...] = bufs[0][...] if columns is None else bufs[0][:, :, columns]
        return
    me = lax.axis_index("fsdp")
    for number, buf in enumerate(bufs):
        for block in range(buf.shape[0]):
            away = (number // 2) + 2 * (number % 2) + 4 * (block // 2) + 8 * (block % 2)
            at = jnp.bitwise_xor(me, away)
            target[at] = buf[block] if columns is None else buf[block, :, columns]


def store_blocks(value, outs, rows, columns=slice(None)):
    if len(outs) == 1:
        outs[0][:, rows, columns] = value
        return
    pairs = value.reshape((value.shape[0] // 2, 2) + value.shape[1:])
    first = lax.rem(lax.axis_index("fsdp"), 2) == 0
    outs[0][:, rows, columns] = jnp.where(first, pairs[:, 0], pairs[:, 1])
    sent = jnp.where(first, pairs[:, 1], pairs[:, 0])
    each = outs[1].shape[0]
    for index, out in enumerate(outs[1:]):
        out[:, rows, columns] = sent[index * each : (index + 1) * each]


def row_of(ref, layer, which):
    return ref[layer].astype(F32)[which : which + 1, :]


def statistics(rows):
    mean = jnp.mean(rows, axis=-1, keepdims=True)
    center = rows - mean
    scale = lax.rsqrt(jnp.mean(center * center, axis=-1, keepdims=True) + EPSILON)
    return (center * scale, scale)


def norm_backward(rows, grad, gain):
    unit, scale = statistics(rows)
    e = grad * gain
    back = scale * (
        e
        - jnp.mean(e, axis=-1, keepdims=True)
        - unit * jnp.mean(e * unit, axis=-1, keepdims=True)
    )
    return (
        back,
        jnp.sum(grad * unit, axis=0, keepdims=True),
        jnp.sum(grad, axis=0, keepdims=True),
    )


def column(row):
    wide = jnp.broadcast_to(row.astype(F32), (8, row.shape[1]))
    return wide.T[:, 0:1]


def place_rows(slots_ref, less, seq):
    slots = slots_ref.shape[1]
    wanted = column(slots_ref[...]) - float(less)
    places = lax.broadcasted_iota(jnp.int32, (slots, seq), 1).astype(F32)
    return wanted == places


def place_columns(slots_ref, less, seq):
    slots = slots_ref.shape[1]
    wanted = slots_ref[...] - less
    places = lax.broadcasted_iota(jnp.int32, (seq, slots), 0)
    return wanted == places


def ones(hit):
    return jnp.where(hit, 1.0, 0.0).astype(BF)


def exact_pick(hit, value):
    high = value.astype(BF)
    rest = value - high.astype(F32)
    middle = rest.astype(BF)
    low = (rest - middle.astype(F32)).astype(BF)
    return dot(hit, high) + dot(hit, middle) + dot(hit, low)


def pack_kernel(jt_ref, mt_ref, a_ref):
    rows = mt_ref.shape[1]
    for which in range(3):
        a_ref[which * rows : (which + 1) * rows, :] = jt_ref[0, which]
    a_ref[3 * rows :, :] = mt_ref[0]


def start_kernel(
    jt_ref, mt_ref, ex_ref, sh_ref, x_ref, gain_ref, shift_ref,
    n_ref, e0_ref, s0_ref, a1_ref, e1_ref, s1_ref,
):
    unit, _ = statistics(x_ref[...].astype(F32))
    n_ref[...] = (unit * row_of(gain_ref, 0, 0) + row_of(shift_ref, 0, 0)).astype(BF)
    rows = mt_ref.shape[1]
    for which in range(3):
        a1_ref[which * rows : (which + 1) * rows, :] = jt_ref[1, which]
    a1_ref[3 * rows :, :] = mt_ref[1]
    for layer, (e_ref, s_ref) in enumerate(((e0_ref, s0_ref), (e1_ref, s1_ref))):
        e_ref[...] = ex_ref[layer]
        s_ref[...] = sh_ref[layer]


def segment_row(seg_ref, peer):
    mine = lax.axis_index("tensor")
    which = (1 - mine) if peer else mine
    both = seg_ref[...].astype(F32)
    row = jnp.where(which == 0, both[0:1, :], both[1:2, :])
    return row


def lane_masks(rows):
    lane = lax.broadcasted_iota(jnp.int32, (rows, LANES), 1)
    return (lane < HEAD, lane >= HEAD)


def attend_forward_kernel(count, layer, peer, arrays, n_ref, seg_ref, bias_ref, *refs):
    bufs = refs[:arrays]
    part_ref, q_ref, k_ref, v_ref, mixed_ref, w_ref, neg_ref = refs[arrays:]
    load_blocks(bufs, w_ref)
    seq, d = n_ref.shape
    width = q_ref.shape[1]
    half = seq // 2
    row = segment_row(seg_ref, peer)
    rows = lax.broadcasted_iota(jnp.int32, (seq, seq), 0)
    cols = lax.broadcasted_iota(jnp.int32, (seq, seq), 1)
    allowed = (column(row) == row) & (cols <= rows)
    neg_ref[...] = jnp.where(allowed, 0.0, -1e30)
    n = n_ref[...]

    def weight(which):
        return w_ref[:, which * BLOCK : (which + 1) * BLOCK, :].reshape(d, width)

    q_ref[...] = (dot(n, weight(0)) + row_of(bias_ref, layer, 0)).astype(BF)
    k_ref[...] = dot(n, weight(1)).astype(BF)
    v_ref[...] = (dot(n, weight(2)) + row_of(bias_ref, layer, 1)).astype(BF)
    masks = lane_masks(half)
    for pair in range(width // LANES):
        lanes = slice(pair * LANES, (pair + 1) * LANES)
        for part in range(2):
            top = slice(part * half, (part + 1) * half)
            keys = slice(0, (part + 1) * half)
            qp = q_ref[top, lanes] * BF(HEAD ** (-0.5))
            kp = k_ref[keys, lanes]
            vp = v_ref[keys, lanes]
            found = []
            for mask in masks:
                s = dot_nt(jnp.where(mask, qp, BF(0)), kp) + neg_ref[top, keys]
                e = jnp.exp(s - jnp.max(s, axis=-1, keepdims=True))
                scale = 1.0 / jnp.sum(e, axis=-1, keepdims=True)
                found.append(dot((e * scale).astype(BF), vp))
            mixed_ref[top, lanes] = jnp.where(masks[0], found[0], found[1]).astype(BF)
    part_ref[...] = dot_nt(mixed_ref[...], weight(3)).astype(BF)


def attend_forward(count, layer, peer, n, segments, bias, bufs):
    seq, d = n.shape
    width = bufs[0].shape[-1]
    rows = shape((seq, width), BF)
    return pl.pallas_call(
        partial(attend_forward_kernel, count, layer, peer, len(bufs)),
        name="attend_forward",
        out_shape=[shape((seq, d), BF), rows, rows, rows, rows],
        in_specs=[VMEM] * (3 + len(bufs)),
        scratch_shapes=[
            pltpu.VMEM((d // BLOCK, 4 * BLOCK, width), BF),
            pltpu.VMEM((seq, seq), F32),
        ],
        compiler_params=vmem(16),
        cost_estimate=cost(
            8 * seq * d * width + 4 * seq * seq * width,
            8 * d * width + 4 * seq * d + 8 * seq * width,
            seq * seq * width // HEAD,
        ),
    )(n, segments, bias, *bufs)


def attend_backward_kernel(
    count, layer, peer, picked, arrays,
    q_ref, k_ref, v_ref, gm_ref, seg_ref, slots_ref, *refs,
):
    bufs = refs[:arrays]
    refs = refs[arrays:]
    if picked:
        gn_ref, dj_ref, gb_ref, wide_ref, w_ref, neg_ref, gx_ref, qx_ref = refs
    else:
        gn_ref, dj_ref, gb_ref, w_ref, neg_ref, gx_ref = refs
    load_blocks(bufs, w_ref)
    seq, width = q_ref.shape
    d = gm_ref.shape[1]
    half = seq // 2
    row = segment_row(seg_ref, peer)
    if picked:
        slots = gm_ref.shape[0]
        hit = place_rows(slots_ref, 1, seq)
        at = column(slots_ref[...]) - 1.0
        own = jnp.sum(jnp.where(hit, row, 0.0), axis=-1, keepdims=True)
        cols = lax.broadcasted_iota(jnp.int32, (slots, seq), 1).astype(F32)
        neg_ref[...] = jnp.where((own == row) & (cols <= at), 0.0, -1e30)
        qx_ref[...] = dot(ones(hit), q_ref[...]).astype(BF)
        parts = [(slice(0, slots), slice(0, seq))]
        queries = qx_ref
    else:
        rows = lax.broadcasted_iota(jnp.int32, (seq, seq), 0)
        cols = lax.broadcasted_iota(jnp.int32, (seq, seq), 1)
        allowed = (column(row) == row) & (cols <= rows)
        neg_ref[...] = jnp.where(allowed, 0.0, -1e30)
        parts = [
            (slice(part * half, (part + 1) * half), slice(0, (part + 1) * half))
            for part in range(2)
        ]
        queries = q_ref

    def weight(which):
        return w_ref[:, which * BLOCK : (which + 1) * BLOCK, :].reshape(d, width)

    gx_ref[...] = dot(gm_ref[...], weight(3)).astype(BF)
    if picked:
        back = ones(place_columns(slots_ref, 1, seq))
        wide_ref[...] = dot(back, gm_ref[...]).astype(BF)
    masks = lane_masks(parts[0][0].stop)
    for pair in range(width // LANES):
        lanes = slice(pair * LANES, (pair + 1) * LANES)
        dk = [None, None]
        dv = [None, None]
        dq_all = []
        for top, keys in parts:
            qp = queries[top, lanes]
            kp = k_ref[keys, lanes]
            vp = v_ref[keys, lanes]
            gp = gx_ref[top, lanes]
            dq, dk_now, dv_now = [], [], []
            for mask in masks:
                qm = jnp.where(mask, qp, BF(0)) * BF(HEAD ** (-0.5))
                s = dot_nt(qm, kp) + neg_ref[top, keys]
                e = jnp.exp(s - jnp.max(s, axis=-1, keepdims=True))
                p = e * (1.0 / jnp.sum(e, axis=-1, keepdims=True))
                gprobs = dot_nt(jnp.where(mask, gp, BF(0)), vp)
                inner = jnp.sum(gprobs * p, axis=-1, keepdims=True)
                ds = (p * (gprobs - inner) * HEAD ** (-0.5)).astype(BF)
                dq.append(dot(ds, kp))
                dk_now.append(dot_tn(ds, qp))
                dv_now.append(dot_tn(p.astype(BF), gp))
            dq_all.append(jnp.where(masks[0], dq[0], dq[1]))
            key_mask = lane_masks(half)[0]
            for block in range(keys.stop // half):
                at = slice(block * half, (block + 1) * half)
                k_new = jnp.where(key_mask, dk_now[0][at], dk_now[1][at])
                v_new = jnp.where(key_mask, dv_now[0][at], dv_now[1][at])
                dk[block] = k_new if dk[block] is None else dk[block] + k_new
                dv[block] = v_new if dv[block] is None else dv[block] + v_new
        gb_ref[0:1, lanes] = sum(jnp.sum(one, axis=0, keepdims=True) for one in dq_all)
        gb_ref[1:2, lanes] = sum(jnp.sum(one, axis=0, keepdims=True) for one in dv)
        if picked:
            dj_ref[0, :, lanes] = dot(back, dq_all[0].astype(BF)).astype(BF)
        else:
            for (top, _), one in zip(parts, dq_all):
                dj_ref[0, top, lanes] = one.astype(BF)
        for block in range(2):
            at = slice(block * half, (block + 1) * half)
            dj_ref[1, at, lanes] = dk[block].astype(BF)
            dj_ref[2, at, lanes] = dv[block].astype(BF)
    gn = dot_nt(dj_ref[0], weight(0))
    gn = gn + dot_nt(dj_ref[1], weight(1))
    gn = gn + dot_nt(dj_ref[2], weight(2))
    gn_ref[...] = gn.astype(BF)


def attend_backward(count, layer, peer, kept, gm, segments, slots, bufs, picked):
    q, k, v = kept
    seq, width = q.shape
    rows, d = gm.shape
    outs = [shape((seq, d), BF), shape((3, seq, width), BF), shape((2, width), F32)]
    scratch = [
        pltpu.VMEM((d // BLOCK, 4 * BLOCK, width), BF),
        pltpu.VMEM((rows, seq), F32),
        pltpu.VMEM((rows, width), BF),
    ]
    if picked:
        outs.append(shape((seq, d), BF))
        scratch.append(pltpu.VMEM((rows, width), BF))
    return pl.pallas_call(
        partial(attend_backward_kernel, count, layer, peer, picked, len(bufs)),
        name="attend_backward",
        out_shape=outs,
        in_specs=[VMEM] * (6 + len(bufs)),
        scratch_shapes=scratch,
        compiler_params=vmem(16),
        cost_estimate=cost(
            2 * rows * d * width + 6 * seq * d * width + 10 * rows * seq * width,
            8 * d * width + 4 * seq * d + 12 * seq * width,
            rows * seq * width // HEAD,
        ),
    )(q, k, v, gm, segments, slots, *bufs)


def attend_grads_kernel(n0_ref, n1_ref, d0_ref, d1_ref, g0_ref, g1_ref, m0_ref, m1_ref, *outs):
    d = n0_ref.shape[1]
    width = m0_ref.shape[1]
    groups = d // BLOCK
    nt = [n0_ref[...].T, n1_ref[...].T]
    for which in range(3):
        total = dot(nt[0], d0_ref[which]) + dot(nt[1], d1_ref[which])
        store_blocks(
            total.astype(BF).reshape(groups, BLOCK, width),
            outs,
            slice(which * BLOCK, (which + 1) * BLOCK),
        )
    total = dot(g0_ref[...].T, m0_ref[...]) + dot(g1_ref[...].T, m1_ref[...])
    store_blocks(
        total.astype(BF).reshape(groups, BLOCK, width), outs, slice(3 * BLOCK, 4 * BLOCK)
    )


def grad_shapes(count, groups, rows, width, split, pieces=1):
    if split:
        blocks = count // 2
        return [shape((blocks, rows, width), BF)] + [
            shape((blocks // pieces, rows, width), BF)
        ] * pieces
    return [shape((groups, rows, width), BF)]


def attend_grads(count, split, n, dj, gm, mixed):
    seq, d = n[0].shape
    width = mixed[0].shape[1]
    outs = grad_shapes(count, d // BLOCK, 4 * BLOCK, width, split, PIECES)
    return pl.pallas_call(
        attend_grads_kernel,
        name="attend_grads",
        out_shape=outs,
        in_specs=[VMEM] * 8,
        compiler_params=vmem(16),
        cost_estimate=cost(16 * seq * d * width, 16 * d * width + 8 * seq * d),
    )(*n, *dj, *gm, *mixed)


def chunk_of(hidden):
    return 512 if hidden % 512 == 0 else hidden


def mlp_forward_kernel(count, layer, arrays, n0_ref, n1_ref, be_ref, *refs):
    e_bufs, s_bufs = refs[:arrays], refs[arrays : 2 * arrays]
    out0_ref, out1_ref, n_ref, acc_ref, we_ref, ws_ref = refs[2 * arrays :]
    rows, d = n0_ref.shape
    hidden = e_bufs[0].shape[2]
    chunk = chunk_of(hidden)
    n_ref[:rows, :] = n0_ref[...]
    n_ref[rows:, :] = n1_ref[...]
    acc_ref[...] = jnp.zeros_like(acc_ref)

    @pl.loop(0, hidden // chunk)
    def _(index):
        cols = pl.ds(pl.multiple_of(index * chunk, chunk), chunk)
        load_blocks(e_bufs, we_ref, cols)
        load_blocks(s_bufs, ws_ref, cols)
        shift = be_ref[:, cols].astype(F32)[layer : layer + 1, :]
        u = dot(n_ref[...], we_ref[...].reshape(d, chunk)) + shift
        t = jnp.tanh(GELU_C * (u + GELU_A * (u * u * u)))
        active = (0.5 * u * (1.0 + t)).astype(BF)
        acc_ref[...] = acc_ref[...] + dot_nt(active, ws_ref[...].reshape(d, chunk))

    out0_ref[...] = acc_ref[:rows, :].astype(BF)
    out1_ref[...] = acc_ref[rows:, :].astype(BF)


def mlp_forward(count, layer, n, be, e_bufs, s_bufs):
    rows, d = n[0].shape
    hidden = e_bufs[0].shape[-1]
    return pl.pallas_call(
        partial(mlp_forward_kernel, count, layer, len(e_bufs)),
        name="mlp_forward",
        out_shape=[shape((rows, d), BF)] * 2,
        in_specs=[VMEM] * (3 + 2 * len(e_bufs)),
        scratch_shapes=[
            pltpu.VMEM((2 * rows, d), BF),
            pltpu.VMEM((2 * rows, d), F32),
            pltpu.VMEM((d // BLOCK, BLOCK, chunk_of(hidden)), BF),
            pltpu.VMEM((d // BLOCK, BLOCK, chunk_of(hidden)), BF),
        ],
        compiler_params=vmem(16),
        cost_estimate=cost(
            8 * rows * d * hidden, 4 * d * hidden + 8 * rows * d, 2 * rows * hidden
        ),
    )(*n, be, *e_bufs, *s_bufs)


def gelu_parts(u):
    square = u * u
    t = jnp.tanh(GELU_C * (u + GELU_A * (square * u)))
    lean = 0.5 * (1.0 + t)
    slope = lean + (0.5 * u) * (1.0 - t * t) * (GELU_C + (3.0 * GELU_C * GELU_A) * square)
    return (u * lean, slope)


def mlp_rows_kernel(layer, arrays, whole, n_ref, g_ref, be_ref, *refs):
    bufs, refs = refs[:arrays], refs[arrays:]
    if whole:
        n1_ref, g1_ref, a1_ref, h1_ref, out_ref, gn_ref, gb_ref, *outs = refs[:-7]
        acc_ref, gacc_ref, we_ref, ws_ref, nt_ref, gt_ref, hold_ref = refs[-7:]
    else:
        out_ref, gn_ref, gb_ref, a_ref, h_ref, acc_ref, gacc_ref, we_ref, ws_ref = refs
    rows, d = n_ref.shape
    hidden = bufs[0].shape[2]
    chunk = chunk_of(hidden)
    groups = d // BLOCK
    if whole:
        nt_ref[:, :rows] = n_ref[...].T
        nt_ref[:, rows:] = n1_ref[...].T
        gt_ref[:, :rows] = g_ref[...].T
        gt_ref[:, rows:] = g1_ref[...].T
    acc_ref[...] = jnp.zeros_like(acc_ref)
    gacc_ref[...] = jnp.zeros_like(gacc_ref)

    @pl.loop(0, hidden // chunk)
    def _(index):
        cols = pl.ds(pl.multiple_of(index * chunk, chunk), chunk)
        load_blocks(bufs[: arrays // 2], we_ref, cols)
        load_blocks(bufs[arrays // 2 :], ws_ref, cols)
        we = we_ref[...].reshape(d, chunk)
        ws = ws_ref[...].reshape(d, chunk)
        shift = be_ref[:, cols].astype(F32)[layer : layer + 1, :]
        active, slope = gelu_parts(dot(n_ref[...], we) + shift)
        active = active.astype(BF)
        gh = dot(g_ref[...], ws) * slope
        gb_ref[:, cols] = jnp.sum(gh, axis=0, keepdims=True)
        gh = gh.astype(BF)
        gacc_ref[...] = gacc_ref[...] + dot_nt(gh, we)
        acc_ref[...] = acc_ref[...] + dot_nt(active, ws)
        if whole:
            hold_ref[:rows, :] = gh
            hold_ref[rows:, :] = h1_ref[:, cols]
            ge = dot(nt_ref[...], hold_ref[...]).astype(BF)
            hold_ref[:rows, :] = active
            hold_ref[rows:, :] = a1_ref[:, cols]
            gs = dot(gt_ref[...], hold_ref[...]).astype(BF)
            half = len(outs) // 2
            every = slice(0, BLOCK)
            store_blocks(ge.reshape(groups, BLOCK, chunk), outs[:half], every, cols)
            store_blocks(gs.reshape(groups, BLOCK, chunk), outs[half:], every, cols)
        else:
            a_ref[:, cols] = active
            h_ref[:, cols] = gh

    gn_ref[...] = gacc_ref[...].astype(BF)
    out_ref[...] = acc_ref[...].astype(BF)


def mlp_rows(count, layer, split, n, g, be, e_bufs, s_bufs, other=()):
    rows, d = n.shape
    bufs = (*e_bufs, *s_bufs)
    hidden = bufs[0].shape[-1]
    chunk = chunk_of(hidden)
    groups = d // BLOCK
    whole = bool(other)
    half = shape((rows, d), BF)
    outs = [half, half, shape((1, hidden), F32)]
    blocks = pltpu.VMEM((groups, BLOCK, chunk), BF)
    scratch = [pltpu.VMEM((rows, d), F32)] * 2 + [blocks] * 2
    if whole:
        outs += 2 * grad_shapes(count, groups, BLOCK, hidden, split)
        scratch += [pltpu.VMEM((d, 2 * rows), BF)] * 2 + [pltpu.VMEM((2 * rows, chunk), BF)]
    else:
        outs += [shape((rows, hidden), BF)] * 2
    return pl.pallas_call(
        partial(mlp_rows_kernel, layer, len(bufs), whole),
        name="mlp_whole" if whole else "mlp_rows",
        out_shape=outs,
        in_specs=[VMEM] * (3 + len(bufs) + len(other)),
        scratch_shapes=scratch,
        compiler_params=vmem(24),
        cost_estimate=cost(
            (16 if whole else 8) * rows * d * hidden,
            8 * d * hidden + 16 * rows * d,
            rows * hidden,
        ),
    )(n, g, be, *bufs, *other)


def mlp_backward_kernel(count, layer, arrays, full, outputs, n0_ref, n1_ref, g0_ref, g1_ref, be_ref, *refs):
    e_bufs, s_bufs = refs[:arrays], refs[arrays : 2 * arrays]
    refs = refs[2 * arrays :]
    if full:
        out0_ref, out1_ref, refs = refs[0], refs[1], refs[2:]
    gn0_ref, gn1_ref, gb_ref = refs[:3]
    outs = refs[3 : 3 + outputs]
    refs = refs[3 + outputs :]
    n_ref, g_ref, nt_ref, gt_ref, gacc_ref, we_ref, ws_ref = refs[:7]
    if full:
        acc_ref = refs[7]
    rows, d = n0_ref.shape
    hidden = e_bufs[0].shape[2]
    chunk = chunk_of(hidden)
    groups = d // BLOCK
    n_ref[:rows, :] = n0_ref[...]
    n_ref[rows:, :] = n1_ref[...]
    g_ref[:rows, :] = g0_ref[...]
    g_ref[rows:, :] = g1_ref[...]
    nt_ref[...] = n_ref[...].T
    gt_ref[...] = g_ref[...].T
    gacc_ref[...] = jnp.zeros_like(gacc_ref)
    if full:
        acc_ref[...] = jnp.zeros_like(acc_ref)

    @pl.loop(0, hidden // chunk)
    def _(index):
        cols = pl.ds(pl.multiple_of(index * chunk, chunk), chunk)
        load_blocks(e_bufs, we_ref, cols)
        load_blocks(s_bufs, ws_ref, cols)
        we = we_ref[...].reshape(d, chunk)
        ws = ws_ref[...].reshape(d, chunk)
        shift = be_ref[:, cols].astype(F32)[layer : layer + 1, :]
        u = dot(n_ref[...], we) + shift
        square = u * u
        t = jnp.tanh(GELU_C * (u + GELU_A * (square * u)))
        lean = 0.5 * (1.0 + t)
        active = (u * lean).astype(BF)
        slope = lean + (0.5 * u) * (1.0 - t * t) * (GELU_C + (3.0 * GELU_C * GELU_A) * square)
        gh = dot(g_ref[...], ws) * slope
        gb_ref[:, cols] = jnp.sum(gh, axis=0, keepdims=True)
        gh = gh.astype(BF)
        ge = dot(nt_ref[...], gh).astype(BF)
        gs = dot(gt_ref[...], active).astype(BF)
        ge, gs = ge.reshape(groups, BLOCK, chunk), gs.reshape(groups, BLOCK, chunk)
        if full:
            store_blocks(ge, outs[: outputs // 2], slice(0, BLOCK), cols)
            store_blocks(gs, outs[outputs // 2 :], slice(0, BLOCK), cols)
        else:
            store_blocks(ge, outs, slice(0, BLOCK), cols)
            store_blocks(gs, outs, slice(BLOCK, 2 * BLOCK), cols)
        gacc_ref[...] = gacc_ref[...] + dot_nt(gh, we)
        if full:
            acc_ref[...] = acc_ref[...] + dot_nt(active, ws)

    gn0_ref[...] = gacc_ref[:rows, :].astype(BF)
    gn1_ref[...] = gacc_ref[rows:, :].astype(BF)
    if full:
        out0_ref[...] = acc_ref[:rows, :].astype(BF)
        out1_ref[...] = acc_ref[rows:, :].astype(BF)


def mlp_backward(count, layer, split, n, g, be, e_bufs, s_bufs, full):
    rows, d = n[0].shape
    hidden = e_bufs[0].shape[-1]
    groups = d // BLOCK
    half = shape((rows, d), BF)
    if full:
        grads = 2 * grad_shapes(count, groups, BLOCK, hidden, split)
    else:
        grads = grad_shapes(count, groups, 2 * BLOCK, hidden, split)
    blocks = pltpu.VMEM((groups, BLOCK, chunk_of(hidden)), BF)
    return pl.pallas_call(
        partial(mlp_backward_kernel, count, layer, len(e_bufs), full, len(grads)),
        name="mlp_backward",
        out_shape=[half] * (4 if full else 2) + [shape((1, hidden), F32)] + grads,
        in_specs=[VMEM] * (5 + 2 * len(e_bufs)),
        scratch_shapes=[
            pltpu.VMEM((2 * rows, d), BF),
            pltpu.VMEM((2 * rows, d), BF),
            pltpu.VMEM((d, 2 * rows), BF),
            pltpu.VMEM((d, 2 * rows), BF),
            pltpu.VMEM((2 * rows, d), F32),
            blocks,
            blocks,
        ]
        + ([pltpu.VMEM((2 * rows, d), F32)] if full else []),
        compiler_params=vmem(28),
        cost_estimate=cost(
            (24 if full else 20) * rows * d * hidden,
            8 * d * hidden + 16 * rows * d,
            2 * rows * hidden,
        ),
    )(*n, *g, be, *e_bufs, *s_bufs)


def middle_kernel(layer, x_ref, own_ref, got_ref, slots_ref, gain_ref, shift_ref, bias_ref, *outs):
    middle = (
        x_ref[...].astype(F32)
        + (own_ref[...].astype(F32) + got_ref[...].astype(F32))
        + row_of(bias_ref, layer, 0)
    )
    unit, _ = statistics(middle)
    normed = (unit * row_of(gain_ref, layer, 1) + row_of(shift_ref, layer, 1)).astype(BF)
    outs[0][...] = middle
    outs[1][...] = normed
    if layer == 0:
        hit = ones(place_rows(slots_ref, 1, x_ref.shape[0]))
        outs[2][...] = exact_pick(hit, middle)
        outs[3][...] = dot(hit, normed).astype(BF)


def second_kernel(
    x_ref, mid_ref, own_ref, got_ref, slots_ref, gain_ref, shift_ref, bias_ref, out_ref, n_ref
):
    seq = x_ref.shape[0]
    latent = (
        mid_ref[...]
        + (own_ref[...].astype(F32) + got_ref[...].astype(F32))
        + row_of(bias_ref, 0, 1)
    )
    known = column(slots_ref[...]) >= 1.0
    latent = jnp.where(known, latent, 0.0).astype(BF)
    hit = place_columns(slots_ref, 0, seq)
    occupied = jnp.sum(jnp.where(hit, 1.0, 0.0), axis=-1, keepdims=True)
    second = x_ref[...].astype(F32) * (1.0 - occupied) + dot(ones(hit), latent)
    unit, _ = statistics(second)
    out_ref[...] = second
    n_ref[...] = (unit * row_of(gain_ref, 1, 0) + row_of(shift_ref, 1, 0)).astype(BF)


def grad_middle_kernel(mid_ref, own_ref, got_ref, cot_ref, gain_ref, out_ref, low_ref, sum_ref):
    cot = cot_ref[...].astype(F32)
    grad = own_ref[...].astype(F32) + got_ref[...].astype(F32)
    back, gain, shift = norm_backward(mid_ref[...], grad, row_of(gain_ref, 1, 1))
    total = cot + back
    out_ref[...] = total
    low_ref[...] = total.astype(BF)
    sum_ref[0:1, :] = gain
    sum_ref[1:2, :] = shift
    sum_ref[2:3, :] = jnp.sum(total, axis=0, keepdims=True)
    sum_ref[3:4, :] = jnp.sum(cot, axis=0, keepdims=True)


def grad_second_kernel(
    x_ref, own_ref, got_ref, gm_ref, slots_ref, gain_ref, out_ref, pick_ref, low_ref, sum_ref
):
    grad = own_ref[...].astype(F32) + got_ref[...].astype(F32)
    back, gain, shift = norm_backward(x_ref[...], grad, row_of(gain_ref, 1, 0))
    total = gm_ref[...] + back
    out_ref[...] = total
    hit = place_rows(slots_ref, 0, x_ref.shape[0])
    known = column(slots_ref[...]) >= 1.0
    pick = jnp.where(known, exact_pick(ones(hit), total), 0.0)
    pick_ref[...] = pick
    low_ref[...] = pick.astype(BF)
    sum_ref[0:1, :] = gain
    sum_ref[1:2, :] = shift


def grad_picked_kernel(mid_ref, own_ref, got_ref, pick_ref, gain_ref, out_ref, low_ref, sum_ref):
    grad = own_ref[...].astype(F32) + got_ref[...].astype(F32)
    back, gain, shift = norm_backward(mid_ref[...], grad, row_of(gain_ref, 0, 1))
    pick = pick_ref[...]
    total = pick + back
    out_ref[...] = total
    low_ref[...] = total.astype(BF)
    sum_ref[0:1, :] = gain
    sum_ref[1:2, :] = shift
    sum_ref[2:3, :] = jnp.sum(total, axis=0, keepdims=True)
    sum_ref[3:4, :] = jnp.sum(pick, axis=0, keepdims=True)


def grad_first_kernel(
    x_ref, own_ref, got_ref, gm_ref, second_ref, slots_ref, gain_ref,
    s22_ref, s21_ref, s12_ref, pair1_ref, pair0_ref, peer1_ref, peer0_ref, be1_ref, more1_ref, be0_ref,
    out_ref, sum_ref,
):
    seq, d = x_ref.shape
    grad = own_ref[...].astype(F32) + got_ref[...].astype(F32)
    back, gain, shift = norm_backward(x_ref[...].astype(F32), grad, row_of(gain_ref, 0, 0))
    hit = place_columns(slots_ref, 0, seq)
    occupied = jnp.sum(jnp.where(hit, 1.0, 0.0), axis=-1, keepdims=True)
    source = ones(place_columns(slots_ref, 1, seq))
    out_ref[...] = second_ref[...] * (1.0 - occupied) + (exact_pick(source, gm_ref[...]) + back)
    width = pair0_ref.shape[1]
    for index, row in enumerate(
        (
            gain, s12_ref[0:1, :], s21_ref[0:1, :], s22_ref[0:1, :],
            shift, s12_ref[1:2, :], s21_ref[1:2, :], s22_ref[1:2, :],
            s12_ref[2:3, :], s12_ref[3:4, :], s22_ref[2:3, :], s22_ref[3:4, :],
        )
    ):
        for part in range(d // width):
            at = index * (d // width) + part
            sum_ref[at : at + 1, :] = row[:, part * width : (part + 1) * width]
    first = 12 * (d // width)
    sum_ref[first : first + 2, :] = pair0_ref[...] + peer0_ref[...]
    sum_ref[first + 2 : first + 4, :] = pair1_ref[...] + peer1_ref[...]
    hidden = be0_ref.shape[1]
    for layer, row in enumerate((be0_ref[...], be1_ref[...] + more1_ref[...])):
        for part in range(hidden // width):
            at = first + 4 + layer * (hidden // width) + part
            sum_ref[at : at + 1, :] = row[:, part * width : (part + 1) * width]


def vectors_kernel(sum_ref, gains_ref, shifts_ref, branch_ref, pair_ref, hidden_ref):
    d = gains_ref.shape[2]
    width = sum_ref.shape[1]
    index = 0
    for ref in (gains_ref, shifts_ref, branch_ref):
        for layer in range(2):
            for which in range(2):
                for part in range(d // width):
                    ref[layer, which : which + 1, part * width : (part + 1) * width] = sum_ref[
                        index : index + 1, :
                    ]
                    index += 1
    for layer in range(2):
        pair_ref[layer] = sum_ref[index : index + 2, :]
        index += 2
    for layer in range(2):
        for part in range(hidden_ref.shape[1] // width):
            hidden_ref[layer : layer + 1, part * width : (part + 1) * width] = sum_ref[
                index : index + 1, :
            ]
            index += 1


def small(kernel, name, outs, *args, wait=0):
    moved = sum(a.size * a.dtype.itemsize for a in args) + sum(
        o.size * o.dtype.itemsize for o in outs
    )
    return pl.pallas_call(
        kernel,
        name=name,
        out_shape=outs,
        in_specs=[VMEM] * len(args),
        compiler_params=vmem(24),
        cost_estimate=cost(4 * moved + wait, moved),
    )(*args)


def split_kernel(stride, keep_ref, *refs):
    *got_refs, kept_ref, sent_ref = refs
    each = got_refs[0].shape[0]
    bit = lax.rem(lax.axis_index("fsdp") // stride, 2)
    for index in range(kept_ref.shape[0]):
        got_ref, first = got_refs[2 * index // each], 2 * index // each * each
        for out, place in ((kept_ref, bit), (sent_ref, 1 - bit)):
            at = 2 * index + place
            got = got_ref[at - first].astype(F32)
            out[index] = (keep_ref[at].astype(F32) + got).astype(BF)


def split_kernel_of(stride, used, behind):
    def kernel(*refs):
        split_kernel(stride, *refs[:used], *refs[used + behind :])

    return kernel


def split(stride, keep, *got, behind=None):
    blocks, rows, width = keep.shape
    return pl.pallas_call(
        split_kernel_of(stride, 1 + len(got), behind is not None),
        name="split",
        out_shape=[shape((blocks // 2, rows, width), BF)] * 2,
        in_specs=[VMEM] * (1 + len(got)) + [ANY] * (behind is not None),
        compiler_params=vmem(8),
        cost_estimate=cost(keep.size + SPLIT_WAIT[stride], 6 * keep.size),
    )(keep, *got, *(() if behind is None else (behind,)))


def finish_kernel(counts, *refs):
    joint_ref, merge_ref, expand_ref, shrink_ref = refs[-4:]
    totals = []
    first = 0
    for number in counts:
        total = refs[first][0].astype(F32)
        for ref in refs[first + 1 : first + number]:
            total = total + ref[0].astype(F32)
        totals.append(total)
        first += number
    rows = merge_ref.shape[1]
    attend, both = totals[:2]
    half = both.shape[0] // 2
    sums = ((attend, both[:half, :], both[half:, :]), totals[2:])
    for layer, (attend, expand, shrink) in enumerate(sums):
        for which in range(3):
            joint_ref[layer, which] = attend[which * rows : (which + 1) * rows, :]
        merge_ref[layer] = attend[3 * rows :, :]
        expand_ref[layer] = expand
        shrink_ref[layer] = shrink


def finish(states):
    _, rows, width = states[0][0].shape
    hidden = states[1][0].shape[2]
    rows = rows // 4
    outs = [shape((2, 3, rows, width), F32), shape((2, rows, width), F32)]
    outs += [shape((2, rows, hidden), F32)] * 2
    counts = tuple(len(state) for state in states)
    return small(
        partial(finish_kernel, counts), "finish", outs, *[one for state in states for one in state]
    )


def regroup(array, count, kinds):
    rows = array.shape[0] * array.shape[1] // kinds // BLOCK
    each = array.shape[1] // kinds
    width = array.shape[2]
    split = array.reshape(array.shape[0], kinds, each, width).transpose(1, 0, 2, 3)
    return split.reshape(kinds, rows, BLOCK, width).transpose(1, 0, 2, 3).reshape(
        rows, kinds * BLOCK, width
    )


def ungroup(array, count, kinds):
    width = array.shape[2]
    split = array.reshape(array.shape[0], kinds, BLOCK, width).transpose(1, 0, 2, 3)
    each = array.shape[0] * BLOCK // count
    return split.reshape(kinds, count, each, width).transpose(1, 0, 2, 3).reshape(
        count, kinds * each, width
    )


def shards(
    count,
    embedded,
    segments,
    thoughts,
    cotangent,
    gains,
    shifts,
    joint_weight,
    joint_bias,
    merge_weight,
    expand_weight,
    expand_bias,
    shrink_weight,
    branch_biases,
):
    seq, d = embedded.shape
    rows_each = joint_weight.shape[1]
    width = joint_weight.shape[3]
    hidden = expand_weight.shape[2]
    slots = thoughts.shape[1]
    staged = rows_each == BLOCK and count == 16
    rows_f32, rows_bf = shape((seq, d), F32), shape((seq, d), BF)
    few_f32, few_bf = shape((slots, d), F32), shape((slots, d), BF)
    ins = (
        joint_weight.transpose(0, 2, 1, 3),
        merge_weight.transpose(0, 2, 1),
        expand_weight,
        shrink_weight.transpose(0, 2, 1),
    )
    bufs = {}

    def first_step(own, *others):
        return join(after(own, *others), across(own, count, 8))

    def next_step(own, *others):
        return join(after(own, *others), across(own, count, 4))

    def third_step(own):
        return (own, across(own, count, 2))

    def last_step(both):
        return [*both, across(both[0], count, 1), across(both[1], count, 1)]

    if staged:
        attend, plain = shape((4 * rows_each, width), BF), shape((rows_each, hidden), BF)
        (a0,) = small(pack_kernel, "pack", [attend], *ins[:2])
        normed, e0, s0, a1, e1, s1 = small(
            start_kernel, "start", [rows_bf, plain, plain, attend, plain, plain],
            *ins, embedded, gains, shifts,
        )
    else:
        first = embedded.astype(F32)
        center = first - jnp.mean(first, axis=-1, keepdims=True)
        scale = lax.rsqrt(jnp.mean(center * center, axis=-1, keepdims=True) + EPSILON)
        normed = (
            center * scale * gains[0, 0].astype(F32) + shifts[0, 0].astype(F32)
        ).astype(BF)
        for layer in range(2):
            attend = jnp.concatenate(
                (ins[0][layer].reshape(3 * rows_each, width), ins[1][layer]), axis=0
            )
            for name, one, kind in (("a", attend, 4), ("e", ins[2][layer], 1), ("s", ins[3][layer], 1)):
                whole = lax.all_gather(one, "fsdp", axis=0, tiled=False)
                bufs[f"{name}{layer}"] = [regroup(whole, count, kind)]

    slots_peer = swap(thoughts)
    normed_peer = swap(normed)

    if staged:
        a0, e0 = sync(first_step(a0), e0)
        cot_peer = hold(swap(cotangent), 4 * 10**9)
        a0, e0, s0, cot_peer = sync(next_step(a0, cot_peer), first_step(e0), s0, cot_peer)
        a0, e0, s0, a1, normed_peer, slots_peer = sync(
            third_step(a0), next_step(e0), first_step(s0), a1, normed_peer, slots_peer
        )
        bufs["a0"] = last_step(a0)
    else:
        cot_peer = swap(cotangent)

    def attention(layer, own, peer):
        weights = bufs[f"a{layer}"]
        part_peer, *kept_peer = attend_forward(count, layer, True, peer, segments, joint_bias, weights)
        got = swap(part_peer)
        part_own, *kept_own = attend_forward(
            count, layer, False, after(own, part_peer), segments, joint_bias, weights
        )
        return (part_own, got, (own, peer), (kept_own, kept_peer))

    part, got, n_one, kept_one = attention(0, normed, normed_peer)
    if staged:
        e0, s0, a1, part, e1 = sync(
            third_step(e0), next_step(s0, part), first_step(a1, part), part, e1
        )
        bufs["e0"] = last_step(e0)
    middle_one, n2_one, middle_few, n2_few = small(
        partial(middle_kernel, 0), "middle", [rows_f32, rows_bf, few_f32, few_bf],
        embedded, part, got, thoughts, gains, shifts, branch_biases, wait=10**10,
    )
    n2_few = (n2_few, swap(n2_few))
    if staged:
        s0, a1, e1, s1, n2_few, bufs["e0"] = sync(
            third_step(s0), next_step(a1), first_step(e1), s1, n2_few, bufs["e0"]
        )
        bufs["s0"] = last_step(s0)
    own, peer = mlp_forward(count, 0, n2_few, expand_bias, bufs["e0"], bufs["s0"])
    second, normed = small(
        second_kernel, "second", [rows_f32, rows_bf],
        embedded, middle_few, own, swap(peer), thoughts, gains, shifts, branch_biases,
    )
    normed_peer = swap(normed)

    if staged:
        a1, e1, s1, normed, normed_peer = sync(
            third_step(a1), next_step(e1, normed), first_step(s1, normed), normed, normed_peer
        )
        bufs["a1"] = last_step(a1)
    part, got, n_two, kept_two = attention(1, normed, normed_peer)
    if staged:
        e1, s1, part = sync(third_step(e1), next_step(s1, part), part)
        bufs["e1"] = last_step(e1)
    middle_two, n2_two = small(
        partial(middle_kernel, 1), "middle", [rows_f32, rows_bf],
        second, part, got, thoughts, gains, shifts, branch_biases,
    )
    n2_peer = swap(n2_two)
    if staged:
        s1, n2_two, n2_peer, bufs["e1"] = sync(third_step(s1), n2_two, n2_peer, bufs["e1"])
        bufs["s1"] = last_step(s1)
    peer_two, gn_peer, gb_peer, *more = mlp_rows(
        count, 1, staged, n2_peer, cot_peer, expand_bias, bufs["e1"], bufs["s1"]
    )
    got = swap(gn_peer)
    own_two, gn_own, gb_own, *grads = mlp_rows(
        count, 1, staged, after(n2_two, gn_peer), cotangent, expand_bias, bufs["e1"], bufs["s1"],
        (n2_peer, cot_peer, *more),
    )
    gb_two = (gb_own, gb_peer)

    def begin(grads, kind):
        if staged:
            return (grads[0], *[across(sent, count, 1) for sent in grads[1:]])
        done = lax.psum_scatter(
            ungroup(grads[0], count, kind), "fsdp", scatter_dimension=0, tiled=False
        )
        return (done[None],)

    def settle(state, stride, *others, behind=None):
        if not staged:
            return state
        return tuple(split(stride, *after(state, *others), behind=behind))

    def move(state, stride):
        return (state[0], across(state[1], count, stride)) if staged else state

    def apart(grads):
        return (grads[: len(grads) // 2], grads[len(grads) // 2 :])

    e1, s1 = apart(grads)
    s1, e1 = begin(s1, 1), begin(e1, 1)
    gm, gm_low, s22 = small(
        grad_middle_kernel, "grad_middle", [rows_f32, rows_bf, shape((4, d), F32)],
        middle_two, gn_own, got, cotangent, gains, wait=25 * 10**9,
    )
    s1, e1, gm, gm_low = sync(
        settle(s1, 2, behind=s22), settle(e1, 2, behind=s22), gm, gm_low
    )
    s1, e1 = move(s1, 2), move(e1, 2)
    gm_peer = swap(gm_low)
    weights = bufs["a1"]
    back_own = attend_backward(
        count, 1, False, kept_two[0][:3], gm_low, segments, thoughts, weights, False
    )
    back_peer = attend_backward(
        count, 1, True, kept_two[1][:3], after(gm_peer, back_own[0]), segments, slots_peer,
        weights, False,
    )
    s1, back_peer, back_own = sync(settle(s1, 4, back_peer[0]), back_peer, back_own)
    got = swap(back_peer[0])
    s1 = move(s1, 4)
    a1 = attend_grads(
        count, staged, n_two, (back_own[1], back_peer[1]), (gm_low, gm_peer),
        (kept_two[0][3], kept_two[1][3]),
    )
    a1 = begin(a1, 4)
    s1 = settle(s1, 8, got)
    e1 = settle(e1, 4, s1)
    s1, e1, a1, got, own = sync(s1, e1, settle(a1, 2, e1), got, back_own[0])
    s1, e1, a1 = move(s1, 8), move(e1, 4), move(a1, 2)
    grad_second, g_few, g_low, s21 = small(
        grad_second_kernel, "grad_second", [rows_f32, few_f32, few_bf, shape((2, d), F32)],
        second, own, got, gm, thoughts, gains,
    )
    pair_two = (back_own[2], back_peer[2])

    g_peer = swap(g_low)
    own, peer, gb_one, *m0 = mlp_backward(
        count, 0, staged, n2_few, (g_low, g_peer), expand_bias,
        bufs["e0"], bufs["s0"], False,
    )
    m0 = settle(begin(m0, 2), 2)
    gm_few, gm_low, s12 = small(
        grad_picked_kernel, "grad_picked", [few_f32, few_bf, shape((4, d), F32)],
        middle_few, own, swap(peer), g_few, gains,
    )
    gm_peer = swap(gm_low)
    weights = bufs["a0"]
    back_own = attend_backward(
        count, 0, False, kept_one[0][:3], gm_low, segments, thoughts, weights, True
    )
    e1 = settle(e1, 8, back_own[0])
    a1 = settle(a1, 4, e1)
    s1, e1, a1, m0, gm_peer, back_own = sync(s1, e1, a1, m0, gm_peer, back_own)
    e1, a1, m0 = move(e1, 8), move(a1, 4), move(m0, 2)
    back_peer = attend_backward(
        count, 0, True, kept_one[1][:3], gm_peer, segments, slots_peer, weights, True
    )
    got = swap(back_peer[0])
    a0 = attend_grads(
        count, staged, n_one, (back_own[1], back_peer[1]), (back_own[3], back_peer[3]),
        (kept_one[0][3], kept_one[1][3]),
    )
    pair_one = (back_own[2], back_peer[2])
    a1 = move(settle(a1, 8, got), 8)
    m0 = settle(m0, 4, a1, e1)
    a1, m0, a0, got, n2_one, peer_two = sync(
        a1, m0, settle(begin(a0, 4), 2, m0), got, n2_one, peer_two
    )
    m0, a0 = move(m0, 4), move(a0, 2)
    embedded_grad, vectors = small(
        grad_first_kernel, "grad_first",
        [rows_f32, shape((12 * d // width + 4 + 2 * (hidden // width), width), F32)],
        embedded, back_own[0], got, gm_few, grad_second, thoughts, gains,
        s22, s21, s12, pair_two[0], pair_one[0], pair_two[1], pair_one[1], *gb_two, gb_one,
    )
    shared = jnp.arange(vectors.shape[0])[:, None] < 12 * d // width
    vectors = vectors + jnp.where(shared, swap(vectors), 0.0)
    n2_peer = swap(after(n2_one, vectors))
    if staged:
        vectors = vectors + across(vectors, count, 1)
        m0 = settle(m0, 8, embedded_grad)
        m0, a0, vectors = sync(m0, settle(a0, 4, m0), vectors)
        m0, a0 = move(m0, 8), move(a0, 4)
    latent_own, latent_peer = mlp_forward(
        count, 0, (n2_one, n2_peer), expand_bias, bufs["e0"], bufs["s0"]
    )
    if staged:
        vectors = vectors + across(vectors, count, 2)
        m0 = (m0[0], hold(after(m0[1], latent_own)))
        m0, a0, vectors = sync(m0, settle(a0, 8, m0), vectors)
        a0 = move(a0, 8)
        total = (vectors + across(vectors, count, 4)) + (
            across(vectors, count, 8) + across(vectors, count, 12)
        )
    else:
        total = lax.psum(vectors, "fsdp")

    biases = branch_biases.astype(F32)
    latent_peer, peer_two = swap(latent_peer), swap(peer_two)
    latent = middle_one + (latent_own.astype(F32) + latent_peer.astype(F32)) + biases[0, 1]
    language = middle_two + (own_two.astype(F32) + peer_two.astype(F32)) + biases[1, 1]

    joint_grad, merge_grad, expand_grad, shrink_grad = finish((a0, m0, a1, e1, s1))
    vector = shape((2, 2, d), F32)
    gains_grad, shifts_grad, branch_grad, joint_bias_grad, expand_bias_grad = small(
        vectors_kernel, "vectors",
        [vector, vector, vector, shape((2, 2, width), F32), shape((2, hidden), F32)],
        total,
    )
    return (
        latent.astype(BF),
        language.astype(BF),
        embedded_grad,
        gains_grad,
        shifts_grad,
        joint_grad.transpose(0, 2, 1, 3),
        joint_bias_grad,
        merge_grad.transpose(0, 2, 1),
        expand_grad,
        expand_bias_grad,
        shrink_grad.transpose(0, 2, 1),
        branch_grad,
    )


def solution(mesh):
    placed = (
        P(("fsdp", "tensor"), None),
        P("fsdp", None),
        P(("fsdp", "tensor"), None),
        P(("fsdp", "tensor"), None),
        P(),
        P(),
        P(None, "fsdp", None, "tensor"),
        P(None, None, "tensor"),
        P(None, "tensor", "fsdp"),
        P(None, "fsdp", "tensor"),
        P(None, "tensor"),
        P(None, "tensor", "fsdp"),
        P(),
    )
    return jax.shard_map(
        partial(shards, mesh.shape["fsdp"]),
        mesh=mesh,
        in_specs=placed,
        out_specs=(
            P(("fsdp", "tensor"), None),
            P(("fsdp", "tensor"), None),
            P(("fsdp", "tensor"), None),
            P(),
            P(),
            P(None, "fsdp", None, "tensor"),
            P(None, None, "tensor"),
            P(None, "tensor", "fsdp"),
            P(None, "fsdp", "tensor"),
            P(None, "tensor"),
            P(None, "tensor", "fsdp"),
            P(),
        ),
        check_vma=False,
    )
```

```python
from functools import partial

import jax
import jax.numpy as jnp
from jax import lax
from jax.experimental import pallas as pl
from jax.experimental.pallas import tpu as pltpu
from jax.sharding import PartitionSpec as P

HEAD = 64
LANES = 128
BLOCK = 48
EPSILON = 1e-05
BF = jnp.bfloat16
F32 = jnp.float32
GELU_C = 0.7978845608028654
GELU_A = 0.044715
MIB = 1 << 20


def dot(a, b):
    return lax.dot_general(a, b, (((1,), (0,)), ((), ())), preferred_element_type=F32)


def dot_nt(a, b):
    return lax.dot_general(a, b, (((1,), (1,)), ((), ())), preferred_element_type=F32)


def dot_tn(a, b):
    return lax.dot_general(a, b, (((0,), (0,)), ((), ())), preferred_element_type=F32)


def vmem(mib):
    return pltpu.CompilerParams(vmem_limit_bytes=mib * MIB)


def cost(flops, moved, exps=0):
    return pl.CostEstimate(flops=flops, transcendentals=exps, bytes_accessed=moved)


VMEM = pl.BlockSpec(memory_space=pltpu.VMEM)
ANY = pl.BlockSpec(memory_space=pl.ANY)


def shape(dims, kind):
    return jax.ShapeDtypeStruct(tuple(dims), kind)


def across(value, count, stride):
    return lax.ppermute(value, "fsdp", [(place, place ^ stride) for place in range(count)])


def swap(value):
    return lax.ppermute(value, "tensor", [(0, 1), (1, 0)])


def after(value, *others):
    leaves, tree = jax.tree.flatten(value)
    held = lax.optimization_barrier(tuple(leaves) + tuple(jax.tree.leaves(others)))
    return jax.tree.unflatten(tree, held[: len(leaves)])


def sync(*values):
    leaves, tree = jax.tree.flatten(values)
    return jax.tree.unflatten(tree, lax.optimization_barrier(tuple(leaves)))


def hold_kernel(value_ref, token_ref):
    del value_ref
    token_ref[...] = jnp.zeros_like(token_ref)


def hold(value, wait=2 * 10**9):
    token = pl.pallas_call(
        hold_kernel,
        name="hold",
        out_shape=shape((8, LANES), F32),
        in_specs=[pl.BlockSpec(memory_space=pl.ANY)],
        compiler_params=vmem(1),
        cost_estimate=cost(wait, 4096),
    )(value)
    return after(value, token)


def join_kernel(own_ref, got_ref, out_ref):
    half = out_ref.shape[0] // 2
    for index in range(half):
        out_ref[index] = own_ref[index] if own_ref.ndim == 3 else own_ref[...]
        out_ref[half + index] = got_ref[index] if got_ref.ndim == 3 else got_ref[...]


JOIN_WAIT = 2 * 10**9
PIECES = 1
SPLIT_WAIT = {2: 0, 4: 25 * 10**9, 8: 2 * 10**9}


def join(own, got, wait=JOIN_WAIT):
    dims = own.shape[-2:]
    blocks = 2 if own.ndim == 2 else 2 * own.shape[0]
    return pl.pallas_call(
        join_kernel,
        name="join",
        out_shape=shape((blocks,) + dims, BF),
        in_specs=[VMEM] * 2,
        compiler_params=vmem(4),
        cost_estimate=cost(wait, 4 * blocks * dims[0] * dims[1]),
    )(own, got)


def load_blocks(bufs, target, columns=None):
    if len(bufs) == 1:
        target[...] = bufs[0][...] if columns is None else bufs[0][:, :, columns]
        return
    me = lax.axis_index("fsdp")
    for number, buf in enumerate(bufs):
        for block in range(buf.shape[0]):
            away = (number // 2) + 2 * (number % 2) + 4 * (block // 2) + 8 * (block % 2)
            at = jnp.bitwise_xor(me, away)
            target[at] = buf[block] if columns is None else buf[block, :, columns]


def store_blocks(value, outs, rows, columns=slice(None)):
    if len(outs) == 1:
        outs[0][:, rows, columns] = value
        return
    pairs = value.reshape((value.shape[0] // 2, 2) + value.shape[1:])
    first = lax.rem(lax.axis_index("fsdp"), 2) == 0
    outs[0][:, rows, columns] = jnp.where(first, pairs[:, 0], pairs[:, 1])
    sent = jnp.where(first, pairs[:, 1], pairs[:, 0])
    each = outs[1].shape[0]
    for index, out in enumerate(outs[1:]):
        out[:, rows, columns] = sent[index * each : (index + 1) * each]


def row_of(ref, layer, which):
    return ref[layer].astype(F32)[which : which + 1, :]


def statistics(rows):
    mean = jnp.mean(rows, axis=-1, keepdims=True)
    center = rows - mean
    scale = lax.rsqrt(jnp.mean(center * center, axis=-1, keepdims=True) + EPSILON)
    return (center * scale, scale)


def norm_backward(rows, grad, gain):
    unit, scale = statistics(rows)
    e = grad * gain
    back = scale * (
        e
        - jnp.mean(e, axis=-1, keepdims=True)
        - unit * jnp.mean(e * unit, axis=-1, keepdims=True)
    )
    return (
        back,
        jnp.sum(grad * unit, axis=0, keepdims=True),
        jnp.sum(grad, axis=0, keepdims=True),
    )


def column(row):
    wide = jnp.broadcast_to(row.astype(F32), (8, row.shape[1]))
    return wide.T[:, 0:1]


def place_rows(slots_ref, less, seq):
    slots = slots_ref.shape[1]
    wanted = column(slots_ref[...]) - float(less)
    places = lax.broadcasted_iota(jnp.int32, (slots, seq), 1).astype(F32)
    return wanted == places


def place_columns(slots_ref, less, seq):
    slots = slots_ref.shape[1]
    wanted = slots_ref[...] - less
    places = lax.broadcasted_iota(jnp.int32, (seq, slots), 0)
    return wanted == places


def ones(hit):
    return jnp.where(hit, 1.0, 0.0).astype(BF)


def exact_pick(hit, value):
    high = value.astype(BF)
    rest = value - high.astype(F32)
    middle = rest.astype(BF)
    low = (rest - middle.astype(F32)).astype(BF)
    return dot(hit, high) + dot(hit, middle) + dot(hit, low)


def pack_kernel(jt_ref, mt_ref, a_ref):
    rows = mt_ref.shape[1]
    for which in range(3):
        a_ref[which * rows : (which + 1) * rows, :] = jt_ref[0, which]
    a_ref[3 * rows :, :] = mt_ref[0]


def start_kernel(
    jt_ref, mt_ref, ex_ref, sh_ref, x_ref, gain_ref, shift_ref,
    n_ref, next_ref, e0_ref, s0_ref, a1_ref, e1_ref, s1_ref,
):
    unit, _ = statistics(x_ref[...].astype(F32))
    n_ref[...] = (unit * row_of(gain_ref, 0, 0) + row_of(shift_ref, 0, 0)).astype(BF)
    next_ref[...] = (unit * row_of(gain_ref, 1, 0) + row_of(shift_ref, 1, 0)).astype(BF)
    rows = mt_ref.shape[1]
    for which in range(3):
        a1_ref[which * rows : (which + 1) * rows, :] = jt_ref[1, which]
    a1_ref[3 * rows :, :] = mt_ref[1]
    for layer, (e_ref, s_ref) in enumerate(((e0_ref, s0_ref), (e1_ref, s1_ref))):
        e_ref[...] = ex_ref[layer]
        s_ref[...] = sh_ref[layer]


def segment_row(seg_ref, peer):
    mine = lax.axis_index("tensor")
    which = (1 - mine) if peer else mine
    both = seg_ref[...].astype(F32)
    row = jnp.where(which == 0, both[0:1, :], both[1:2, :])
    return row


def lane_masks(rows):
    lane = lax.broadcasted_iota(jnp.int32, (rows, LANES), 1)
    return (lane < HEAD, lane >= HEAD)


def attend_forward_kernel(count, layer, peer, arrays, n_ref, seg_ref, bias_ref, *refs):
    bufs = refs[:arrays]
    part_ref, q_ref, k_ref, v_ref, mixed_ref, w_ref, neg_ref = refs[arrays:]
    load_blocks(bufs, w_ref)
    seq, d = n_ref.shape
    width = q_ref.shape[1]
    half = seq // 2
    row = segment_row(seg_ref, peer)
    rows = lax.broadcasted_iota(jnp.int32, (seq, seq), 0)
    cols = lax.broadcasted_iota(jnp.int32, (seq, seq), 1)
    allowed = (column(row) == row) & (cols <= rows)
    neg_ref[...] = jnp.where(allowed, 0.0, -1e30)
    n = n_ref[...]

    def weight(which):
        return w_ref[:, which * BLOCK : (which + 1) * BLOCK, :].reshape(d, width)

    q_ref[...] = (dot(n, weight(0)) + row_of(bias_ref, layer, 0)).astype(BF)
    k_ref[...] = dot(n, weight(1)).astype(BF)
    v_ref[...] = (dot(n, weight(2)) + row_of(bias_ref, layer, 1)).astype(BF)
    masks = lane_masks(half)
    for pair in range(width // LANES):
        lanes = slice(pair * LANES, (pair + 1) * LANES)
        for part in range(2):
            top = slice(part * half, (part + 1) * half)
            keys = slice(0, (part + 1) * half)
            qp = q_ref[top, lanes] * BF(HEAD ** (-0.5))
            kp = k_ref[keys, lanes]
            vp = v_ref[keys, lanes]
            found = []
            for mask in masks:
                s = dot_nt(jnp.where(mask, qp, BF(0)), kp) + neg_ref[top, keys]
                e = jnp.exp(s - jnp.max(s, axis=-1, keepdims=True))
                scale = 1.0 / jnp.sum(e, axis=-1, keepdims=True)
                found.append(dot((e * scale).astype(BF), vp))
            mixed_ref[top, lanes] = jnp.where(masks[0], found[0], found[1]).astype(BF)
    part_ref[...] = dot_nt(mixed_ref[...], weight(3)).astype(BF)


def attend_forward(count, layer, peer, n, segments, bias, bufs):
    seq, d = n.shape
    width = bufs[0].shape[-1]
    rows = shape((seq, width), BF)
    return pl.pallas_call(
        partial(attend_forward_kernel, count, layer, peer, len(bufs)),
        name="attend_forward",
        out_shape=[shape((seq, d), BF), rows, rows, rows, rows],
        in_specs=[VMEM] * (3 + len(bufs)),
        scratch_shapes=[
            pltpu.VMEM((d // BLOCK, 4 * BLOCK, width), BF),
            pltpu.VMEM((seq, seq), F32),
        ],
        compiler_params=vmem(16),
        cost_estimate=cost(
            8 * seq * d * width + 4 * seq * seq * width,
            8 * d * width + 4 * seq * d + 8 * seq * width,
            seq * seq * width // HEAD,
        ),
    )(n, segments, bias, *bufs)


def attend_backward_kernel(
    count, layer, peer, picked, arrays,
    q_ref, k_ref, v_ref, gm_ref, seg_ref, slots_ref, *refs,
):
    bufs = refs[:arrays]
    refs = refs[arrays:]
    if picked:
        gn_ref, dj_ref, gb_ref, wide_ref, w_ref, neg_ref, gx_ref, qx_ref = refs
    else:
        gn_ref, dj_ref, gb_ref, w_ref, neg_ref, gx_ref = refs
    load_blocks(bufs, w_ref)
    seq, width = q_ref.shape
    d = gm_ref.shape[1]
    half = seq // 2
    row = segment_row(seg_ref, peer)
    if picked:
        slots = gm_ref.shape[0]
        hit = place_rows(slots_ref, 1, seq)
        at = column(slots_ref[...]) - 1.0
        own = jnp.sum(jnp.where(hit, row, 0.0), axis=-1, keepdims=True)
        cols = lax.broadcasted_iota(jnp.int32, (slots, seq), 1).astype(F32)
        neg_ref[...] = jnp.where((own == row) & (cols <= at), 0.0, -1e30)
        qx_ref[...] = dot(ones(hit), q_ref[...]).astype(BF)
        parts = [(slice(0, slots), slice(0, seq))]
        queries = qx_ref
    else:
        rows = lax.broadcasted_iota(jnp.int32, (seq, seq), 0)
        cols = lax.broadcasted_iota(jnp.int32, (seq, seq), 1)
        allowed = (column(row) == row) & (cols <= rows)
        neg_ref[...] = jnp.where(allowed, 0.0, -1e30)
        parts = [
            (slice(part * half, (part + 1) * half), slice(0, (part + 1) * half))
            for part in range(2)
        ]
        queries = q_ref

    def weight(which):
        return w_ref[:, which * BLOCK : (which + 1) * BLOCK, :].reshape(d, width)

    gx_ref[...] = dot(gm_ref[...], weight(3)).astype(BF)
    if picked:
        back = ones(place_columns(slots_ref, 1, seq))
        wide_ref[...] = dot(back, gm_ref[...]).astype(BF)
    masks = lane_masks(parts[0][0].stop)
    for pair in range(width // LANES):
        lanes = slice(pair * LANES, (pair + 1) * LANES)
        dk = [None, None]
        dv = [None, None]
        dq_all = []
        for top, keys in parts:
            qp = queries[top, lanes]
            kp = k_ref[keys, lanes]
            vp = v_ref[keys, lanes]
            gp = gx_ref[top, lanes]
            dq, dk_now, dv_now = [], [], []
            for mask in masks:
                qm = jnp.where(mask, qp, BF(0)) * BF(HEAD ** (-0.5))
                s = dot_nt(qm, kp) + neg_ref[top, keys]
                e = jnp.exp(s - jnp.max(s, axis=-1, keepdims=True))
                p = e * (1.0 / jnp.sum(e, axis=-1, keepdims=True))
                gprobs = dot_nt(jnp.where(mask, gp, BF(0)), vp)
                inner = jnp.sum(gprobs * p, axis=-1, keepdims=True)
                ds = (p * (gprobs - inner) * HEAD ** (-0.5)).astype(BF)
                dq.append(dot(ds, kp))
                dk_now.append(dot_tn(ds, qp))
                dv_now.append(dot_tn(p.astype(BF), gp))
            dq_all.append(jnp.where(masks[0], dq[0], dq[1]))
            key_mask = lane_masks(half)[0]
            for block in range(keys.stop // half):
                at = slice(block * half, (block + 1) * half)
                k_new = jnp.where(key_mask, dk_now[0][at], dk_now[1][at])
                v_new = jnp.where(key_mask, dv_now[0][at], dv_now[1][at])
                dk[block] = k_new if dk[block] is None else dk[block] + k_new
                dv[block] = v_new if dv[block] is None else dv[block] + v_new
        gb_ref[0:1, lanes] = sum(jnp.sum(one, axis=0, keepdims=True) for one in dq_all)
        gb_ref[1:2, lanes] = sum(jnp.sum(one, axis=0, keepdims=True) for one in dv)
        if picked:
            dj_ref[0, :, lanes] = dot(back, dq_all[0].astype(BF)).astype(BF)
        else:
            for (top, _), one in zip(parts, dq_all):
                dj_ref[0, top, lanes] = one.astype(BF)
        for block in range(2):
            at = slice(block * half, (block + 1) * half)
            dj_ref[1, at, lanes] = dk[block].astype(BF)
            dj_ref[2, at, lanes] = dv[block].astype(BF)
    gn = dot_nt(dj_ref[0], weight(0))
    gn = gn + dot_nt(dj_ref[1], weight(1))
    gn = gn + dot_nt(dj_ref[2], weight(2))
    gn_ref[...] = gn.astype(BF)


def attend_backward(count, layer, peer, kept, gm, segments, slots, bufs, picked):
    q, k, v = kept
    seq, width = q.shape
    rows, d = gm.shape
    outs = [shape((seq, d), BF), shape((3, seq, width), BF), shape((2, width), F32)]
    scratch = [
        pltpu.VMEM((d // BLOCK, 4 * BLOCK, width), BF),
        pltpu.VMEM((rows, seq), F32),
        pltpu.VMEM((rows, width), BF),
    ]
    if picked:
        outs.append(shape((seq, d), BF))
        scratch.append(pltpu.VMEM((rows, width), BF))
    return pl.pallas_call(
        partial(attend_backward_kernel, count, layer, peer, picked, len(bufs)),
        name="attend_backward",
        out_shape=outs,
        in_specs=[VMEM] * (6 + len(bufs)),
        scratch_shapes=scratch,
        compiler_params=vmem(16),
        cost_estimate=cost(
            2 * rows * d * width + 6 * seq * d * width + 10 * rows * seq * width,
            8 * d * width + 4 * seq * d + 12 * seq * width,
            rows * seq * width // HEAD,
        ),
    )(q, k, v, gm, segments, slots, *bufs)


def attend_grads_kernel(n0_ref, n1_ref, d0_ref, d1_ref, g0_ref, g1_ref, m0_ref, m1_ref, *outs):
    d = n0_ref.shape[1]
    width = m0_ref.shape[1]
    groups = d // BLOCK
    nt = [n0_ref[...].T, n1_ref[...].T]
    for which in range(3):
        total = dot(nt[0], d0_ref[which]) + dot(nt[1], d1_ref[which])
        store_blocks(
            total.astype(BF).reshape(groups, BLOCK, width),
            outs,
            slice(which * BLOCK, (which + 1) * BLOCK),
        )
    total = dot(g0_ref[...].T, m0_ref[...]) + dot(g1_ref[...].T, m1_ref[...])
    store_blocks(
        total.astype(BF).reshape(groups, BLOCK, width), outs, slice(3 * BLOCK, 4 * BLOCK)
    )


def grad_shapes(count, groups, rows, width, split, pieces=1):
    if split:
        blocks = count // 2
        return [shape((blocks, rows, width), BF)] + [
            shape((blocks // pieces, rows, width), BF)
        ] * pieces
    return [shape((groups, rows, width), BF)]


def attend_grads(count, split, n, dj, gm, mixed):
    seq, d = n[0].shape
    width = mixed[0].shape[1]
    outs = grad_shapes(count, d // BLOCK, 4 * BLOCK, width, split, PIECES)
    return pl.pallas_call(
        attend_grads_kernel,
        name="attend_grads",
        out_shape=outs,
        in_specs=[VMEM] * 8,
        compiler_params=vmem(16),
        cost_estimate=cost(16 * seq * d * width, 16 * d * width + 8 * seq * d),
    )(*n, *dj, *gm, *mixed)


def chunk_of(hidden):
    return 512 if hidden % 512 == 0 else hidden


def mlp_forward_kernel(count, layer, arrays, n0_ref, n1_ref, be_ref, *refs):
    e_bufs, s_bufs = refs[:arrays], refs[arrays : 2 * arrays]
    out0_ref, out1_ref, n_ref, acc_ref, we_ref, ws_ref = refs[2 * arrays :]
    rows, d = n0_ref.shape
    hidden = e_bufs[0].shape[2]
    chunk = chunk_of(hidden)
    n_ref[:rows, :] = n0_ref[...]
    n_ref[rows:, :] = n1_ref[...]
    acc_ref[...] = jnp.zeros_like(acc_ref)

    @pl.loop(0, hidden // chunk)
    def _(index):
        cols = pl.ds(pl.multiple_of(index * chunk, chunk), chunk)
        load_blocks(e_bufs, we_ref, cols)
        load_blocks(s_bufs, ws_ref, cols)
        shift = be_ref[:, cols].astype(F32)[layer : layer + 1, :]
        u = dot(n_ref[...], we_ref[...].reshape(d, chunk)) + shift
        t = jnp.tanh(GELU_C * (u + GELU_A * (u * u * u)))
        active = (0.5 * u * (1.0 + t)).astype(BF)
        acc_ref[...] = acc_ref[...] + dot_nt(active, ws_ref[...].reshape(d, chunk))

    out0_ref[...] = acc_ref[:rows, :].astype(BF)
    out1_ref[...] = acc_ref[rows:, :].astype(BF)


def mlp_forward(count, layer, n, be, e_bufs, s_bufs):
    rows, d = n[0].shape
    hidden = e_bufs[0].shape[-1]
    return pl.pallas_call(
        partial(mlp_forward_kernel, count, layer, len(e_bufs)),
        name="mlp_forward",
        out_shape=[shape((rows, d), BF)] * 2,
        in_specs=[VMEM] * (3 + 2 * len(e_bufs)),
        scratch_shapes=[
            pltpu.VMEM((2 * rows, d), BF),
            pltpu.VMEM((2 * rows, d), F32),
            pltpu.VMEM((d // BLOCK, BLOCK, chunk_of(hidden)), BF),
            pltpu.VMEM((d // BLOCK, BLOCK, chunk_of(hidden)), BF),
        ],
        compiler_params=vmem(16),
        cost_estimate=cost(
            8 * rows * d * hidden, 4 * d * hidden + 8 * rows * d, 2 * rows * hidden
        ),
    )(*n, be, *e_bufs, *s_bufs)


def gelu_parts(u):
    square = u * u
    t = jnp.tanh(GELU_C * (u + GELU_A * (square * u)))
    lean = 0.5 * (1.0 + t)
    slope = lean + (0.5 * u) * (1.0 - t * t) * (GELU_C + (3.0 * GELU_C * GELU_A) * square)
    return (u * lean, slope)


def mlp_rows_kernel(layer, arrays, whole, n_ref, g_ref, be_ref, *refs):
    bufs, refs = refs[:arrays], refs[arrays:]
    if whole:
        n1_ref, g1_ref, a1_ref, h1_ref, out_ref, gn_ref, gb_ref, *outs = refs[:-7]
        acc_ref, gacc_ref, we_ref, ws_ref, nt_ref, gt_ref, hold_ref = refs[-7:]
    else:
        out_ref, gn_ref, gb_ref, a_ref, h_ref, acc_ref, gacc_ref, we_ref, ws_ref = refs
    rows, d = n_ref.shape
    hidden = bufs[0].shape[2]
    chunk = chunk_of(hidden)
    groups = d // BLOCK
    if whole:
        nt_ref[:, :rows] = n_ref[...].T
        nt_ref[:, rows:] = n1_ref[...].T
        gt_ref[:, :rows] = g_ref[...].T
        gt_ref[:, rows:] = g1_ref[...].T
    acc_ref[...] = jnp.zeros_like(acc_ref)
    gacc_ref[...] = jnp.zeros_like(gacc_ref)

    @pl.loop(0, hidden // chunk)
    def _(index):
        cols = pl.ds(pl.multiple_of(index * chunk, chunk), chunk)
        load_blocks(bufs[: arrays // 2], we_ref, cols)
        load_blocks(bufs[arrays // 2 :], ws_ref, cols)
        we = we_ref[...].reshape(d, chunk)
        ws = ws_ref[...].reshape(d, chunk)
        shift = be_ref[:, cols].astype(F32)[layer : layer + 1, :]
        active, slope = gelu_parts(dot(n_ref[...], we) + shift)
        active = active.astype(BF)
        gh = dot(g_ref[...], ws) * slope
        gb_ref[:, cols] = jnp.sum(gh, axis=0, keepdims=True)
        gh = gh.astype(BF)
        gacc_ref[...] = gacc_ref[...] + dot_nt(gh, we)
        acc_ref[...] = acc_ref[...] + dot_nt(active, ws)
        if whole:
            hold_ref[:rows, :] = gh
            hold_ref[rows:, :] = h1_ref[:, cols]
            ge = dot(nt_ref[...], hold_ref[...]).astype(BF)
            hold_ref[:rows, :] = active
            hold_ref[rows:, :] = a1_ref[:, cols]
            gs = dot(gt_ref[...], hold_ref[...]).astype(BF)
            half = len(outs) // 2
            every = slice(0, BLOCK)
            store_blocks(ge.reshape(groups, BLOCK, chunk), outs[:half], every, cols)
            store_blocks(gs.reshape(groups, BLOCK, chunk), outs[half:], every, cols)
        else:
            a_ref[:, cols] = active
            h_ref[:, cols] = gh

    gn_ref[...] = gacc_ref[...].astype(BF)
    out_ref[...] = acc_ref[...].astype(BF)


def mlp_rows(count, layer, split, n, g, be, e_bufs, s_bufs, other=()):
    rows, d = n.shape
    bufs = (*e_bufs, *s_bufs)
    hidden = bufs[0].shape[-1]
    chunk = chunk_of(hidden)
    groups = d // BLOCK
    whole = bool(other)
    half = shape((rows, d), BF)
    outs = [half, half, shape((1, hidden), F32)]
    blocks = pltpu.VMEM((groups, BLOCK, chunk), BF)
    scratch = [pltpu.VMEM((rows, d), F32)] * 2 + [blocks] * 2
    if whole:
        outs += 2 * grad_shapes(count, groups, BLOCK, hidden, split)
        scratch += [pltpu.VMEM((d, 2 * rows), BF)] * 2 + [pltpu.VMEM((2 * rows, chunk), BF)]
    else:
        outs += [shape((rows, hidden), BF)] * 2
    return pl.pallas_call(
        partial(mlp_rows_kernel, layer, len(bufs), whole),
        name="mlp_whole" if whole else "mlp_rows",
        out_shape=outs,
        in_specs=[VMEM] * (3 + len(bufs) + len(other)),
        scratch_shapes=scratch,
        compiler_params=vmem(24),
        cost_estimate=cost(
            (16 if whole else 8) * rows * d * hidden,
            8 * d * hidden + 16 * rows * d,
            rows * hidden,
        ),
    )(n, g, be, *bufs, *other)


def mlp_backward_kernel(count, layer, arrays, full, outputs, n0_ref, n1_ref, g0_ref, g1_ref, be_ref, *refs):
    e_bufs, s_bufs = refs[:arrays], refs[arrays : 2 * arrays]
    refs = refs[2 * arrays :]
    if full:
        out0_ref, out1_ref, refs = refs[0], refs[1], refs[2:]
    gn0_ref, gn1_ref, gb_ref = refs[:3]
    outs = refs[3 : 3 + outputs]
    refs = refs[3 + outputs :]
    n_ref, g_ref, nt_ref, gt_ref, gacc_ref, we_ref, ws_ref = refs[:7]
    if full:
        acc_ref = refs[7]
    rows, d = n0_ref.shape
    hidden = e_bufs[0].shape[2]
    chunk = chunk_of(hidden)
    groups = d // BLOCK
    n_ref[:rows, :] = n0_ref[...]
    n_ref[rows:, :] = n1_ref[...]
    g_ref[:rows, :] = g0_ref[...]
    g_ref[rows:, :] = g1_ref[...]
    nt_ref[...] = n_ref[...].T
    gt_ref[...] = g_ref[...].T
    gacc_ref[...] = jnp.zeros_like(gacc_ref)
    if full:
        acc_ref[...] = jnp.zeros_like(acc_ref)

    @pl.loop(0, hidden // chunk)
    def _(index):
        cols = pl.ds(pl.multiple_of(index * chunk, chunk), chunk)
        load_blocks(e_bufs, we_ref, cols)
        load_blocks(s_bufs, ws_ref, cols)
        we = we_ref[...].reshape(d, chunk)
        ws = ws_ref[...].reshape(d, chunk)
        shift = be_ref[:, cols].astype(F32)[layer : layer + 1, :]
        u = dot(n_ref[...], we) + shift
        square = u * u
        t = jnp.tanh(GELU_C * (u + GELU_A * (square * u)))
        lean = 0.5 * (1.0 + t)
        active = (u * lean).astype(BF)
        slope = lean + (0.5 * u) * (1.0 - t * t) * (GELU_C + (3.0 * GELU_C * GELU_A) * square)
        gh = dot(g_ref[...], ws) * slope
        gb_ref[:, cols] = jnp.sum(gh, axis=0, keepdims=True)
        gh = gh.astype(BF)
        ge = dot(nt_ref[...], gh).astype(BF)
        gs = dot(gt_ref[...], active).astype(BF)
        ge, gs = ge.reshape(groups, BLOCK, chunk), gs.reshape(groups, BLOCK, chunk)
        if full:
            store_blocks(ge, outs[: outputs // 2], slice(0, BLOCK), cols)
            store_blocks(gs, outs[outputs // 2 :], slice(0, BLOCK), cols)
        else:
            store_blocks(ge, outs, slice(0, BLOCK), cols)
            store_blocks(gs, outs, slice(BLOCK, 2 * BLOCK), cols)
        gacc_ref[...] = gacc_ref[...] + dot_nt(gh, we)
        if full:
            acc_ref[...] = acc_ref[...] + dot_nt(active, ws)

    gn0_ref[...] = gacc_ref[:rows, :].astype(BF)
    gn1_ref[...] = gacc_ref[rows:, :].astype(BF)
    if full:
        out0_ref[...] = acc_ref[:rows, :].astype(BF)
        out1_ref[...] = acc_ref[rows:, :].astype(BF)


def mlp_backward(count, layer, split, n, g, be, e_bufs, s_bufs, full):
    rows, d = n[0].shape
    hidden = e_bufs[0].shape[-1]
    groups = d // BLOCK
    half = shape((rows, d), BF)
    if full:
        grads = 2 * grad_shapes(count, groups, BLOCK, hidden, split)
    else:
        grads = grad_shapes(count, groups, 2 * BLOCK, hidden, split)
    blocks = pltpu.VMEM((groups, BLOCK, chunk_of(hidden)), BF)
    return pl.pallas_call(
        partial(mlp_backward_kernel, count, layer, len(e_bufs), full, len(grads)),
        name="mlp_backward",
        out_shape=[half] * (4 if full else 2) + [shape((1, hidden), F32)] + grads,
        in_specs=[VMEM] * (5 + 2 * len(e_bufs)),
        scratch_shapes=[
            pltpu.VMEM((2 * rows, d), BF),
            pltpu.VMEM((2 * rows, d), BF),
            pltpu.VMEM((d, 2 * rows), BF),
            pltpu.VMEM((d, 2 * rows), BF),
            pltpu.VMEM((2 * rows, d), F32),
            blocks,
            blocks,
        ]
        + ([pltpu.VMEM((2 * rows, d), F32)] if full else []),
        compiler_params=vmem(28),
        cost_estimate=cost(
            (24 if full else 20) * rows * d * hidden,
            8 * d * hidden + 16 * rows * d,
            2 * rows * hidden,
        ),
    )(*n, *g, be, *e_bufs, *s_bufs)


def middle_kernel(layer, x_ref, own_ref, got_ref, slots_ref, gain_ref, shift_ref, bias_ref, *outs):
    middle = (
        x_ref[...].astype(F32)
        + (own_ref[...].astype(F32) + got_ref[...].astype(F32))
        + row_of(bias_ref, layer, 0)
    )
    unit, _ = statistics(middle)
    normed = (unit * row_of(gain_ref, layer, 1) + row_of(shift_ref, layer, 1)).astype(BF)
    outs[0][...] = middle
    outs[1][...] = normed
    if layer == 0:
        hit = ones(place_rows(slots_ref, 1, x_ref.shape[0]))
        outs[2][...] = exact_pick(hit, middle)
        outs[3][...] = dot(hit, normed).astype(BF)


def second_kernel(
    x_ref, mid_ref, own_ref, got_ref, slots_ref, gain_ref, shift_ref, bias_ref,
    out_ref, n_ref, few_ref,
):
    seq = x_ref.shape[0]
    latent = (
        mid_ref[...]
        + (own_ref[...].astype(F32) + got_ref[...].astype(F32))
        + row_of(bias_ref, 0, 1)
    )
    known = column(slots_ref[...]) >= 1.0
    latent = jnp.where(known, latent, 0.0).astype(BF)
    hit = place_columns(slots_ref, 0, seq)
    occupied = jnp.sum(jnp.where(hit, 1.0, 0.0), axis=-1, keepdims=True)
    second = x_ref[...].astype(F32) * (1.0 - occupied) + dot(ones(hit), latent)
    unit, _ = statistics(second)
    out_ref[...] = second
    few, _ = statistics(latent.astype(F32))
    few_ref[...] = (few * row_of(gain_ref, 1, 0) + row_of(shift_ref, 1, 0)).astype(BF)
    n_ref[...] = (unit * row_of(gain_ref, 1, 0) + row_of(shift_ref, 1, 0)).astype(BF)


def blend_kernel(early_ref, few_ref, slots_ref, out_ref):
    hit = ones(place_columns(slots_ref, 0, early_ref.shape[0]))
    placed = dot(hit, few_ref[...])
    taken = jnp.sum(hit.astype(F32), axis=-1, keepdims=True) > 0.5
    out_ref[...] = jnp.where(taken, placed, early_ref[...].astype(F32)).astype(BF)


def grad_middle_kernel(mid_ref, own_ref, got_ref, cot_ref, gain_ref, out_ref, low_ref, sum_ref):
    cot = cot_ref[...].astype(F32)
    grad = own_ref[...].astype(F32) + got_ref[...].astype(F32)
    back, gain, shift = norm_backward(mid_ref[...], grad, row_of(gain_ref, 1, 1))
    total = cot + back
    out_ref[...] = total
    low_ref[...] = total.astype(BF)
    sum_ref[0:1, :] = gain
    sum_ref[1:2, :] = shift
    sum_ref[2:3, :] = jnp.sum(total, axis=0, keepdims=True)
    sum_ref[3:4, :] = jnp.sum(cot, axis=0, keepdims=True)


def grad_second_kernel(
    x_ref, own_ref, got_ref, gm_ref, slots_ref, gain_ref, out_ref, pick_ref, low_ref, sum_ref
):
    grad = own_ref[...].astype(F32) + got_ref[...].astype(F32)
    back, gain, shift = norm_backward(x_ref[...], grad, row_of(gain_ref, 1, 0))
    total = gm_ref[...] + back
    out_ref[...] = total
    hit = place_rows(slots_ref, 0, x_ref.shape[0])
    known = column(slots_ref[...]) >= 1.0
    pick = jnp.where(known, exact_pick(ones(hit), total), 0.0)
    pick_ref[...] = pick
    low_ref[...] = pick.astype(BF)
    sum_ref[0:1, :] = gain
    sum_ref[1:2, :] = shift


def grad_picked_kernel(mid_ref, own_ref, got_ref, pick_ref, gain_ref, out_ref, low_ref, sum_ref):
    grad = own_ref[...].astype(F32) + got_ref[...].astype(F32)
    back, gain, shift = norm_backward(mid_ref[...], grad, row_of(gain_ref, 0, 1))
    pick = pick_ref[...]
    total = pick + back
    out_ref[...] = total
    low_ref[...] = total.astype(BF)
    sum_ref[0:1, :] = gain
    sum_ref[1:2, :] = shift
    sum_ref[2:3, :] = jnp.sum(total, axis=0, keepdims=True)
    sum_ref[3:4, :] = jnp.sum(pick, axis=0, keepdims=True)


def grad_first_kernel(
    x_ref, own_ref, got_ref, gm_ref, second_ref, slots_ref, gain_ref,
    s22_ref, s21_ref, s12_ref, pair1_ref, pair0_ref, peer1_ref, peer0_ref, be1_ref, more1_ref, be0_ref,
    out_ref, sum_ref,
):
    seq, d = x_ref.shape
    grad = own_ref[...].astype(F32) + got_ref[...].astype(F32)
    back, gain, shift = norm_backward(x_ref[...].astype(F32), grad, row_of(gain_ref, 0, 0))
    hit = place_columns(slots_ref, 0, seq)
    occupied = jnp.sum(jnp.where(hit, 1.0, 0.0), axis=-1, keepdims=True)
    source = ones(place_columns(slots_ref, 1, seq))
    out_ref[...] = second_ref[...] * (1.0 - occupied) + (exact_pick(source, gm_ref[...]) + back)
    width = pair0_ref.shape[1]
    for index, row in enumerate(
        (
            gain, s12_ref[0:1, :], s21_ref[0:1, :], s22_ref[0:1, :],
            shift, s12_ref[1:2, :], s21_ref[1:2, :], s22_ref[1:2, :],
            s12_ref[2:3, :], s12_ref[3:4, :], s22_ref[2:3, :], s22_ref[3:4, :],
        )
    ):
        for part in range(d // width):
            at = index * (d // width) + part
            sum_ref[at : at + 1, :] = row[:, part * width : (part + 1) * width]
    first = 12 * (d // width)
    sum_ref[first : first + 2, :] = pair0_ref[...] + peer0_ref[...]
    sum_ref[first + 2 : first + 4, :] = pair1_ref[...] + peer1_ref[...]
    hidden = be0_ref.shape[1]
    for layer, row in enumerate((be0_ref[...], be1_ref[...] + more1_ref[...])):
        for part in range(hidden // width):
            at = first + 4 + layer * (hidden // width) + part
            sum_ref[at : at + 1, :] = row[:, part * width : (part + 1) * width]


def vectors_kernel(sum_ref, gains_ref, shifts_ref, branch_ref, pair_ref, hidden_ref):
    d = gains_ref.shape[2]
    width = sum_ref.shape[1]
    index = 0
    for ref in (gains_ref, shifts_ref, branch_ref):
        for layer in range(2):
            for which in range(2):
                for part in range(d // width):
                    ref[layer, which : which + 1, part * width : (part + 1) * width] = sum_ref[
                        index : index + 1, :
                    ]
                    index += 1
    for layer in range(2):
        pair_ref[layer] = sum_ref[index : index + 2, :]
        index += 2
    for layer in range(2):
        for part in range(hidden_ref.shape[1] // width):
            hidden_ref[layer : layer + 1, part * width : (part + 1) * width] = sum_ref[
                index : index + 1, :
            ]
            index += 1


def small(kernel, name, outs, *args, wait=0):
    moved = sum(a.size * a.dtype.itemsize for a in args) + sum(
        o.size * o.dtype.itemsize for o in outs
    )
    return pl.pallas_call(
        kernel,
        name=name,
        out_shape=outs,
        in_specs=[VMEM] * len(args),
        compiler_params=vmem(24),
        cost_estimate=cost(4 * moved + wait, moved),
    )(*args)


def split_kernel(stride, keep_ref, *refs):
    *got_refs, kept_ref, sent_ref = refs
    each = got_refs[0].shape[0]
    bit = lax.rem(lax.axis_index("fsdp") // stride, 2)
    for index in range(kept_ref.shape[0]):
        got_ref, first = got_refs[2 * index // each], 2 * index // each * each
        for out, place in ((kept_ref, bit), (sent_ref, 1 - bit)):
            at = 2 * index + place
            got = got_ref[at - first].astype(F32)
            out[index] = (keep_ref[at].astype(F32) + got).astype(BF)


def split_kernel_of(stride, used, behind):
    def kernel(*refs):
        split_kernel(stride, *refs[:used], *refs[used + behind :])

    return kernel


def split(stride, keep, *got, behind=None):
    blocks, rows, width = keep.shape
    return pl.pallas_call(
        split_kernel_of(stride, 1 + len(got), behind is not None),
        name="split",
        out_shape=[shape((blocks // 2, rows, width), BF)] * 2,
        in_specs=[VMEM] * (1 + len(got)) + [ANY] * (behind is not None),
        compiler_params=vmem(8),
        cost_estimate=cost(keep.size + SPLIT_WAIT[stride], 6 * keep.size),
    )(keep, *got, *(() if behind is None else (behind,)))


def finish_kernel(counts, *refs):
    joint_ref, merge_ref, expand_ref, shrink_ref = refs[-4:]
    totals = []
    first = 0
    for number in counts:
        total = refs[first][0].astype(F32)
        for ref in refs[first + 1 : first + number]:
            total = total + ref[0].astype(F32)
        totals.append(total)
        first += number
    rows = merge_ref.shape[1]
    attend, both = totals[:2]
    half = both.shape[0] // 2
    sums = ((attend, both[:half, :], both[half:, :]), totals[2:])
    for layer, (attend, expand, shrink) in enumerate(sums):
        for which in range(3):
            joint_ref[layer, which] = attend[which * rows : (which + 1) * rows, :]
        merge_ref[layer] = attend[3 * rows :, :]
        expand_ref[layer] = expand
        shrink_ref[layer] = shrink


def finish(states):
    _, rows, width = states[0][0].shape
    hidden = states[1][0].shape[2]
    rows = rows // 4
    outs = [shape((2, 3, rows, width), F32), shape((2, rows, width), F32)]
    outs += [shape((2, rows, hidden), F32)] * 2
    counts = tuple(len(state) for state in states)
    return small(
        partial(finish_kernel, counts), "finish", outs, *[one for state in states for one in state]
    )


def regroup(array, count, kinds):
    rows = array.shape[0] * array.shape[1] // kinds // BLOCK
    each = array.shape[1] // kinds
    width = array.shape[2]
    split = array.reshape(array.shape[0], kinds, each, width).transpose(1, 0, 2, 3)
    return split.reshape(kinds, rows, BLOCK, width).transpose(1, 0, 2, 3).reshape(
        rows, kinds * BLOCK, width
    )


def ungroup(array, count, kinds):
    width = array.shape[2]
    split = array.reshape(array.shape[0], kinds, BLOCK, width).transpose(1, 0, 2, 3)
    each = array.shape[0] * BLOCK // count
    return split.reshape(kinds, count, each, width).transpose(1, 0, 2, 3).reshape(
        count, kinds * each, width
    )


def shards(
    count,
    embedded,
    segments,
    thoughts,
    cotangent,
    gains,
    shifts,
    joint_weight,
    joint_bias,
    merge_weight,
    expand_weight,
    expand_bias,
    shrink_weight,
    branch_biases,
):
    seq, d = embedded.shape
    rows_each = joint_weight.shape[1]
    width = joint_weight.shape[3]
    hidden = expand_weight.shape[2]
    slots = thoughts.shape[1]
    staged = rows_each == BLOCK and count == 16
    rows_f32, rows_bf = shape((seq, d), F32), shape((seq, d), BF)
    few_f32, few_bf = shape((slots, d), F32), shape((slots, d), BF)
    ins = (
        joint_weight.transpose(0, 2, 1, 3),
        merge_weight.transpose(0, 2, 1),
        expand_weight,
        shrink_weight.transpose(0, 2, 1),
    )
    bufs = {}

    def first_step(own, *others, wait=JOIN_WAIT):
        return join(after(own, *others), across(own, count, 8), wait)

    def next_step(own, *others, wait=JOIN_WAIT):
        return join(after(own, *others), across(own, count, 4), wait)

    def third_step(own):
        return (own, across(own, count, 2))

    def last_step(both):
        return [*both, across(both[0], count, 1), across(both[1], count, 1)]

    if staged:
        attend, plain = shape((4 * rows_each, width), BF), shape((rows_each, hidden), BF)
        (a0,) = small(pack_kernel, "pack", [attend], *ins[:2])
        normed, early, e0, s0, a1, e1, s1 = small(
            start_kernel, "start", [rows_bf, rows_bf, plain, plain, attend, plain, plain],
            *ins, embedded, gains, shifts,
        )
    else:
        first = embedded.astype(F32)
        center = first - jnp.mean(first, axis=-1, keepdims=True)
        scale = lax.rsqrt(jnp.mean(center * center, axis=-1, keepdims=True) + EPSILON)
        normed = (
            center * scale * gains[0, 0].astype(F32) + shifts[0, 0].astype(F32)
        ).astype(BF)
        for layer in range(2):
            attend = jnp.concatenate(
                (ins[0][layer].reshape(3 * rows_each, width), ins[1][layer]), axis=0
            )
            for name, one, kind in (("a", attend, 4), ("e", ins[2][layer], 1), ("s", ins[3][layer], 1)):
                whole = lax.all_gather(one, "fsdp", axis=0, tiled=False)
                bufs[f"{name}{layer}"] = [regroup(whole, count, kind)]

    slots_peer = swap(thoughts)
    normed_peer = swap(normed)

    if staged:
        a0, e0 = sync(first_step(a0), e0)
        cot_peer = hold(swap(cotangent), 4 * 10**9)
        a0, e0, s0, cot_peer, early_peer = sync(
            next_step(a0, cot_peer, wait=10**10), first_step(e0), s0, cot_peer, swap(early)
        )
        a0, e0, s0, a1, normed_peer, slots_peer = sync(
            third_step(a0), next_step(e0), first_step(s0), a1, normed_peer, slots_peer
        )
        bufs["a0"] = last_step(a0)
    else:
        cot_peer = swap(cotangent)

    def attention(layer, own, peer):
        weights = bufs[f"a{layer}"]
        part_peer, *kept_peer = attend_forward(count, layer, True, peer, segments, joint_bias, weights)
        got = swap(part_peer)
        part_own, *kept_own = attend_forward(
            count, layer, False, after(own, part_peer), segments, joint_bias, weights
        )
        return (part_own, got, (own, peer), (kept_own, kept_peer))

    part, got, n_one, kept_one = attention(0, normed, normed_peer)
    if staged:
        e0, s0, a1, part, e1 = sync(
            third_step(e0), next_step(s0, part), first_step(a1, part), part, e1
        )
        bufs["e0"] = last_step(e0)
    middle_one, n2_one, middle_few, n2_few = small(
        partial(middle_kernel, 0), "middle", [rows_f32, rows_bf, few_f32, few_bf],
        embedded, part, got, thoughts, gains, shifts, branch_biases, wait=10**10,
    )
    n2_few = (n2_few, swap(n2_few))
    if staged:
        s0, a1, e1, s1, n2_few, bufs["e0"] = sync(
            third_step(s0), next_step(a1), first_step(e1), s1, n2_few, bufs["e0"]
        )
        bufs["s0"] = last_step(s0)
    own, peer = mlp_forward(count, 0, n2_few, expand_bias, bufs["e0"], bufs["s0"])
    second, normed, few = small(
        second_kernel, "second", [rows_f32, rows_bf, few_bf],
        embedded, middle_few, own, swap(peer), thoughts, gains, shifts, branch_biases,
    )
    if staged:
        (normed_peer,) = small(blend_kernel, "blend", [rows_bf], early_peer, swap(few), slots_peer)
    else:
        normed_peer = swap(normed)

    if staged:
        a1, e1, s1, normed, normed_peer = sync(
            third_step(a1), next_step(e1, normed), first_step(s1, normed), normed, normed_peer
        )
        bufs["a1"] = last_step(a1)
    part, got, n_two, kept_two = attention(1, normed, normed_peer)
    if staged:
        e1, s1, part = sync(third_step(e1), next_step(s1, part), part)
        bufs["e1"] = last_step(e1)
    middle_two, n2_two = small(
        partial(middle_kernel, 1), "middle", [rows_f32, rows_bf],
        second, part, got, thoughts, gains, shifts, branch_biases,
    )
    n2_peer = swap(n2_two)
    if staged:
        s1, n2_two, n2_peer, bufs["e1"] = sync(third_step(s1), n2_two, n2_peer, bufs["e1"])
        bufs["s1"] = last_step(s1)
    peer_two, gn_peer, gb_peer, *more = mlp_rows(
        count, 1, staged, n2_peer, cot_peer, expand_bias, bufs["e1"], bufs["s1"]
    )
    got = swap(gn_peer)
    own_two, gn_own, gb_own, *grads = mlp_rows(
        count, 1, staged, after(n2_two, gn_peer), cotangent, expand_bias, bufs["e1"], bufs["s1"],
        (n2_peer, cot_peer, *more),
    )
    gb_two = (gb_own, gb_peer)

    def begin(grads, kind):
        if staged:
            return (grads[0], *[across(sent, count, 1) for sent in grads[1:]])
        done = lax.psum_scatter(
            ungroup(grads[0], count, kind), "fsdp", scatter_dimension=0, tiled=False
        )
        return (done[None],)

    def settle(state, stride, *others, behind=None):
        if not staged:
            return state
        return tuple(split(stride, *after(state, *others), behind=behind))

    def move(state, stride):
        return (state[0], across(state[1], count, stride)) if staged else state

    def apart(grads):
        return (grads[: len(grads) // 2], grads[len(grads) // 2 :])

    e1, s1 = apart(grads)
    s1, e1 = begin(s1, 1), begin(e1, 1)
    gm, gm_low, s22 = small(
        grad_middle_kernel, "grad_middle", [rows_f32, rows_bf, shape((4, d), F32)],
        middle_two, gn_own, got, cotangent, gains, wait=25 * 10**9,
    )
    s1, e1, gm, gm_low = sync(
        settle(s1, 2, behind=s22), settle(e1, 2, behind=s22), gm, gm_low
    )
    s1, e1 = move(s1, 2), move(e1, 2)
    gm_peer = swap(gm_low)
    weights = bufs["a1"]
    back_own = attend_backward(
        count, 1, False, kept_two[0][:3], gm_low, segments, thoughts, weights, False
    )
    back_peer = attend_backward(
        count, 1, True, kept_two[1][:3], after(gm_peer, back_own[0]), segments, slots_peer,
        weights, False,
    )
    s1, back_peer, back_own = sync(settle(s1, 4, back_peer[0]), back_peer, back_own)
    got = swap(back_peer[0])
    s1 = move(s1, 4)
    a1 = attend_grads(
        count, staged, n_two, (back_own[1], back_peer[1]), (gm_low, gm_peer),
        (kept_two[0][3], kept_two[1][3]),
    )
    a1 = begin(a1, 4)
    s1 = settle(s1, 8, got)
    e1 = settle(e1, 4, s1)
    s1, e1, a1, got, own = sync(s1, e1, settle(a1, 2, e1), got, back_own[0])
    s1, e1, a1 = move(s1, 8), move(e1, 4), move(a1, 2)
    grad_second, g_few, g_low, s21 = small(
        grad_second_kernel, "grad_second", [rows_f32, few_f32, few_bf, shape((2, d), F32)],
        second, own, got, gm, thoughts, gains,
    )
    pair_two = (back_own[2], back_peer[2])

    g_peer = swap(g_low)
    own, peer, gb_one, *m0 = mlp_backward(
        count, 0, staged, n2_few, (g_low, g_peer), expand_bias,
        bufs["e0"], bufs["s0"], False,
    )
    m0 = settle(begin(m0, 2), 2)
    gm_few, gm_low, s12 = small(
        grad_picked_kernel, "grad_picked", [few_f32, few_bf, shape((4, d), F32)],
        middle_few, own, swap(peer), g_few, gains,
    )
    gm_peer = swap(gm_low)
    weights = bufs["a0"]
    back_own = attend_backward(
        count, 0, False, kept_one[0][:3], gm_low, segments, thoughts, weights, True
    )
    e1 = settle(e1, 8, back_own[0])
    a1 = settle(a1, 4, e1)
    s1, e1, a1, m0, gm_peer, back_own = sync(s1, e1, a1, m0, gm_peer, back_own)
    e1, a1, m0 = move(e1, 8), move(a1, 4), move(m0, 2)
    back_peer = attend_backward(
        count, 0, True, kept_one[1][:3], gm_peer, segments, slots_peer, weights, True
    )
    got = swap(back_peer[0])
    a0 = attend_grads(
        count, staged, n_one, (back_own[1], back_peer[1]), (back_own[3], back_peer[3]),
        (kept_one[0][3], kept_one[1][3]),
    )
    pair_one = (back_own[2], back_peer[2])
    a1 = move(settle(a1, 8, got), 8)
    m0 = settle(m0, 4, a1, e1)
    a1, m0, a0, got, n2_one, peer_two = sync(
        a1, m0, settle(begin(a0, 4), 2, m0), got, n2_one, peer_two
    )
    m0, a0 = move(m0, 4), move(a0, 2)
    embedded_grad, vectors = small(
        grad_first_kernel, "grad_first",
        [rows_f32, shape((12 * d // width + 4 + 2 * (hidden // width), width), F32)],
        embedded, back_own[0], got, gm_few, grad_second, thoughts, gains,
        s22, s21, s12, pair_two[0], pair_one[0], pair_two[1], pair_one[1], *gb_two, gb_one,
    )
    shared = jnp.arange(vectors.shape[0])[:, None] < 12 * d // width
    vectors = vectors + jnp.where(shared, swap(vectors), 0.0)
    n2_peer = swap(after(n2_one, vectors))
    if staged:
        vectors = vectors + across(vectors, count, 1)
        m0 = settle(m0, 8, embedded_grad)
        m0, a0, vectors = sync(m0, settle(a0, 4, m0), vectors)
        m0, a0 = move(m0, 8), move(a0, 4)
    latent_own, latent_peer = mlp_forward(
        count, 0, (n2_one, n2_peer), expand_bias, bufs["e0"], bufs["s0"]
    )
    if staged:
        vectors = vectors + across(vectors, count, 2)
        m0 = (m0[0], hold(after(m0[1], latent_own)))
        m0, a0, vectors = sync(m0, settle(a0, 8, m0), vectors)
        a0 = move(a0, 8)
        total = (vectors + across(vectors, count, 4)) + (
            across(vectors, count, 8) + across(vectors, count, 12)
        )
    else:
        total = lax.psum(vectors, "fsdp")

    biases = branch_biases.astype(F32)
    latent_peer, peer_two = swap(latent_peer), swap(peer_two)
    latent = middle_one + (latent_own.astype(F32) + latent_peer.astype(F32)) + biases[0, 1]
    language = middle_two + (own_two.astype(F32) + peer_two.astype(F32)) + biases[1, 1]

    joint_grad, merge_grad, expand_grad, shrink_grad = finish((a0, m0, a1, e1, s1))
    vector = shape((2, 2, d), F32)
    gains_grad, shifts_grad, branch_grad, joint_bias_grad, expand_bias_grad = small(
        vectors_kernel, "vectors",
        [vector, vector, vector, shape((2, 2, width), F32), shape((2, hidden), F32)],
        total,
    )
    return (
        latent.astype(BF),
        language.astype(BF),
        embedded_grad,
        gains_grad,
        shifts_grad,
        joint_grad.transpose(0, 2, 1, 3),
        joint_bias_grad,
        merge_grad.transpose(0, 2, 1),
        expand_grad,
        expand_bias_grad,
        shrink_grad.transpose(0, 2, 1),
        branch_grad,
    )


def solution(mesh):
    placed = (
        P(("fsdp", "tensor"), None),
        P("fsdp", None),
        P(("fsdp", "tensor"), None),
        P(("fsdp", "tensor"), None),
        P(),
        P(),
        P(None, "fsdp", None, "tensor"),
        P(None, None, "tensor"),
        P(None, "tensor", "fsdp"),
        P(None, "fsdp", "tensor"),
        P(None, "tensor"),
        P(None, "tensor", "fsdp"),
        P(),
    )
    return jax.shard_map(
        partial(shards, mesh.shape["fsdp"]),
        mesh=mesh,
        in_specs=placed,
        out_specs=(
            P(("fsdp", "tensor"), None),
            P(("fsdp", "tensor"), None),
            P(("fsdp", "tensor"), None),
            P(),
            P(),
            P(None, "fsdp", None, "tensor"),
            P(None, None, "tensor"),
            P(None, "tensor", "fsdp"),
            P(None, "fsdp", "tensor"),
            P(None, "tensor"),
            P(None, "tensor", "fsdp"),
            P(),
        ),
        check_vma=False,
    )
```

```python
from functools import partial

import jax
import jax.numpy as jnp
from jax import lax
from jax.experimental import pallas as pl
from jax.experimental.pallas import tpu as pltpu
from jax.sharding import PartitionSpec as P

HEAD = 64
LANES = 128
BLOCK = 48
EPSILON = 1e-05
BF = jnp.bfloat16
F32 = jnp.float32
GELU_C = 0.7978845608028654
GELU_A = 0.044715
MIB = 1 << 20


def dot(a, b):
    return lax.dot_general(a, b, (((1,), (0,)), ((), ())), preferred_element_type=F32)


def dot_nt(a, b):
    return lax.dot_general(a, b, (((1,), (1,)), ((), ())), preferred_element_type=F32)


def dot_tn(a, b):
    return lax.dot_general(a, b, (((0,), (0,)), ((), ())), preferred_element_type=F32)


def vmem(mib):
    return pltpu.CompilerParams(vmem_limit_bytes=mib * MIB)


def cost(flops, moved, exps=0):
    return pl.CostEstimate(flops=flops, transcendentals=exps, bytes_accessed=moved)


VMEM = pl.BlockSpec(memory_space=pltpu.VMEM)
ANY = pl.BlockSpec(memory_space=pl.ANY)


def shape(dims, kind):
    return jax.ShapeDtypeStruct(tuple(dims), kind)


def across(value, count, stride):
    return lax.ppermute(value, "fsdp", [(place, place ^ stride) for place in range(count)])


def swap(value):
    return lax.ppermute(value, "tensor", [(0, 1), (1, 0)])


def after(value, *others):
    leaves, tree = jax.tree.flatten(value)
    held = lax.optimization_barrier(tuple(leaves) + tuple(jax.tree.leaves(others)))
    return jax.tree.unflatten(tree, held[: len(leaves)])


def sync(*values):
    leaves, tree = jax.tree.flatten(values)
    return jax.tree.unflatten(tree, lax.optimization_barrier(tuple(leaves)))


def hold_kernel(value_ref, token_ref):
    del value_ref
    token_ref[...] = jnp.zeros_like(token_ref)


def hold(value, wait=2 * 10**9):
    token = pl.pallas_call(
        hold_kernel,
        name="hold",
        out_shape=shape((8, LANES), F32),
        in_specs=[pl.BlockSpec(memory_space=pl.ANY)],
        compiler_params=vmem(1),
        cost_estimate=cost(wait, 4096),
    )(value)
    return after(value, token)


def join_kernel(own_ref, got_ref, out_ref):
    half = out_ref.shape[0] // 2
    for index in range(half):
        out_ref[index] = own_ref[index] if own_ref.ndim == 3 else own_ref[...]
        out_ref[half + index] = got_ref[index] if got_ref.ndim == 3 else got_ref[...]


JOIN_WAIT = 2 * 10**9
PIECES = 1
SPLIT_WAIT = {2: 0, 4: 25 * 10**9, 8: 2 * 10**9}


def join(own, got, wait=JOIN_WAIT):
    dims = own.shape[-2:]
    blocks = 2 if own.ndim == 2 else 2 * own.shape[0]
    return pl.pallas_call(
        join_kernel,
        name="join",
        out_shape=shape((blocks,) + dims, BF),
        in_specs=[VMEM] * 2,
        compiler_params=vmem(4),
        cost_estimate=cost(wait, 4 * blocks * dims[0] * dims[1]),
    )(own, got)


def load_blocks(bufs, target, columns=None):
    if len(bufs) == 1:
        target[...] = bufs[0][...] if columns is None else bufs[0][:, :, columns]
        return
    me = lax.axis_index("fsdp")
    for number, buf in enumerate(bufs):
        for block in range(buf.shape[0]):
            away = (number // 2) + 2 * (number % 2) + 4 * (block // 2) + 8 * (block % 2)
            at = jnp.bitwise_xor(me, away)
            target[at] = buf[block] if columns is None else buf[block, :, columns]


def store_blocks(value, outs, rows, columns=slice(None)):
    if len(outs) == 1:
        outs[0][:, rows, columns] = value
        return
    pairs = value.reshape((value.shape[0] // 2, 2) + value.shape[1:])
    first = lax.rem(lax.axis_index("fsdp"), 2) == 0
    outs[0][:, rows, columns] = jnp.where(first, pairs[:, 0], pairs[:, 1])
    sent = jnp.where(first, pairs[:, 1], pairs[:, 0])
    each = outs[1].shape[0]
    for index, out in enumerate(outs[1:]):
        out[:, rows, columns] = sent[index * each : (index + 1) * each]


def row_of(ref, layer, which):
    return ref[layer].astype(F32)[which : which + 1, :]


def statistics(rows):
    mean = jnp.mean(rows, axis=-1, keepdims=True)
    center = rows - mean
    scale = lax.rsqrt(jnp.mean(center * center, axis=-1, keepdims=True) + EPSILON)
    return (center * scale, scale)


def norm_backward(rows, grad, gain):
    unit, scale = statistics(rows)
    e = grad * gain
    back = scale * (
        e
        - jnp.mean(e, axis=-1, keepdims=True)
        - unit * jnp.mean(e * unit, axis=-1, keepdims=True)
    )
    return (
        back,
        jnp.sum(grad * unit, axis=0, keepdims=True),
        jnp.sum(grad, axis=0, keepdims=True),
    )


def column(row):
    wide = jnp.broadcast_to(row.astype(F32), (8, row.shape[1]))
    return wide.T[:, 0:1]


def place_rows(slots_ref, less, seq):
    slots = slots_ref.shape[1]
    wanted = column(slots_ref[...]) - float(less)
    places = lax.broadcasted_iota(jnp.int32, (slots, seq), 1).astype(F32)
    return wanted == places


def place_columns(slots_ref, less, seq):
    slots = slots_ref.shape[1]
    wanted = slots_ref[...] - less
    places = lax.broadcasted_iota(jnp.int32, (seq, slots), 0)
    return wanted == places


def ones(hit):
    return jnp.where(hit, 1.0, 0.0).astype(BF)


def exact_pick(hit, value):
    high = value.astype(BF)
    rest = value - high.astype(F32)
    middle = rest.astype(BF)
    low = (rest - middle.astype(F32)).astype(BF)
    return dot(hit, high) + dot(hit, middle) + dot(hit, low)


def pack_kernel(jt_ref, mt_ref, a_ref):
    rows = mt_ref.shape[1]
    for which in range(3):
        a_ref[which * rows : (which + 1) * rows, :] = jt_ref[0, which]
    a_ref[3 * rows :, :] = mt_ref[0]


def start_kernel(
    jt_ref, mt_ref, ex_ref, sh_ref, x_ref, gain_ref, shift_ref,
    n_ref, next_ref, e0_ref, s0_ref, a1_ref, e1_ref, s1_ref,
):
    unit, _ = statistics(x_ref[...].astype(F32))
    n_ref[...] = (unit * row_of(gain_ref, 0, 0) + row_of(shift_ref, 0, 0)).astype(BF)
    next_ref[...] = (unit * row_of(gain_ref, 1, 0) + row_of(shift_ref, 1, 0)).astype(BF)
    rows = mt_ref.shape[1]
    for which in range(3):
        a1_ref[which * rows : (which + 1) * rows, :] = jt_ref[1, which]
    a1_ref[3 * rows :, :] = mt_ref[1]
    for layer, (e_ref, s_ref) in enumerate(((e0_ref, s0_ref), (e1_ref, s1_ref))):
        e_ref[...] = ex_ref[layer]
        s_ref[...] = sh_ref[layer]


def segment_row(seg_ref, peer):
    mine = lax.axis_index("tensor")
    which = (1 - mine) if peer else mine
    both = seg_ref[...].astype(F32)
    row = jnp.where(which == 0, both[0:1, :], both[1:2, :])
    return row


def lane_masks(rows):
    lane = lax.broadcasted_iota(jnp.int32, (rows, LANES), 1)
    return (lane < HEAD, lane >= HEAD)


def attend_forward_kernel(count, layer, peer, arrays, n_ref, seg_ref, bias_ref, *refs):
    bufs = refs[:arrays]
    part_ref, q_ref, k_ref, v_ref, mixed_ref, w_ref, neg_ref = refs[arrays:]
    load_blocks(bufs, w_ref)
    seq, d = n_ref.shape
    width = q_ref.shape[1]
    half = seq // 2
    row = segment_row(seg_ref, peer)
    rows = lax.broadcasted_iota(jnp.int32, (seq, seq), 0)
    cols = lax.broadcasted_iota(jnp.int32, (seq, seq), 1)
    allowed = (column(row) == row) & (cols <= rows)
    neg_ref[...] = jnp.where(allowed, 0.0, -1e30)
    n = n_ref[...]

    def weight(which):
        return w_ref[:, which * BLOCK : (which + 1) * BLOCK, :].reshape(d, width)

    q_ref[...] = (dot(n, weight(0)) + row_of(bias_ref, layer, 0)).astype(BF)
    k_ref[...] = dot(n, weight(1)).astype(BF)
    v_ref[...] = (dot(n, weight(2)) + row_of(bias_ref, layer, 1)).astype(BF)
    masks = lane_masks(half)
    for pair in range(width // LANES):
        lanes = slice(pair * LANES, (pair + 1) * LANES)
        for part in range(2):
            top = slice(part * half, (part + 1) * half)
            keys = slice(0, (part + 1) * half)
            qp = q_ref[top, lanes] * BF(HEAD ** (-0.5))
            kp = k_ref[keys, lanes]
            vp = v_ref[keys, lanes]
            found = []
            for mask in masks:
                s = dot_nt(jnp.where(mask, qp, BF(0)), kp) + neg_ref[top, keys]
                e = jnp.exp(s - jnp.max(s, axis=-1, keepdims=True))
                scale = 1.0 / jnp.sum(e, axis=-1, keepdims=True)
                found.append(dot((e * scale).astype(BF), vp))
            mixed_ref[top, lanes] = jnp.where(masks[0], found[0], found[1]).astype(BF)
    part_ref[...] = dot_nt(mixed_ref[...], weight(3)).astype(BF)


def attend_forward(count, layer, peer, n, segments, bias, bufs):
    seq, d = n.shape
    width = bufs[0].shape[-1]
    rows = shape((seq, width), BF)
    return pl.pallas_call(
        partial(attend_forward_kernel, count, layer, peer, len(bufs)),
        name="attend_forward",
        out_shape=[shape((seq, d), BF), rows, rows, rows, rows],
        in_specs=[VMEM] * (3 + len(bufs)),
        scratch_shapes=[
            pltpu.VMEM((d // BLOCK, 4 * BLOCK, width), BF),
            pltpu.VMEM((seq, seq), F32),
        ],
        compiler_params=vmem(16),
        cost_estimate=cost(
            8 * seq * d * width + 4 * seq * seq * width,
            8 * d * width + 4 * seq * d + 8 * seq * width,
            seq * seq * width // HEAD,
        ),
    )(n, segments, bias, *bufs)


def attend_backward_kernel(
    count, layer, peer, picked, arrays,
    q_ref, k_ref, v_ref, gm_ref, seg_ref, slots_ref, *refs,
):
    bufs = refs[:arrays]
    refs = refs[arrays:]
    if picked:
        gn_ref, dj_ref, gb_ref, wide_ref, w_ref, neg_ref, gx_ref, qx_ref = refs
    else:
        gn_ref, dj_ref, gb_ref, w_ref, neg_ref, gx_ref = refs
    load_blocks(bufs, w_ref)
    seq, width = q_ref.shape
    d = gm_ref.shape[1]
    half = seq // 2
    row = segment_row(seg_ref, peer)
    if picked:
        slots = gm_ref.shape[0]
        hit = place_rows(slots_ref, 1, seq)
        at = column(slots_ref[...]) - 1.0
        own = jnp.sum(jnp.where(hit, row, 0.0), axis=-1, keepdims=True)
        cols = lax.broadcasted_iota(jnp.int32, (slots, seq), 1).astype(F32)
        neg_ref[...] = jnp.where((own == row) & (cols <= at), 0.0, -1e30)
        qx_ref[...] = dot(ones(hit), q_ref[...]).astype(BF)
        parts = [(slice(0, slots), slice(0, seq))]
        queries = qx_ref
    else:
        rows = lax.broadcasted_iota(jnp.int32, (seq, seq), 0)
        cols = lax.broadcasted_iota(jnp.int32, (seq, seq), 1)
        allowed = (column(row) == row) & (cols <= rows)
        neg_ref[...] = jnp.where(allowed, 0.0, -1e30)
        parts = [
            (slice(part * half, (part + 1) * half), slice(0, (part + 1) * half))
            for part in range(2)
        ]
        queries = q_ref

    def weight(which):
        return w_ref[:, which * BLOCK : (which + 1) * BLOCK, :].reshape(d, width)

    gx_ref[...] = dot(gm_ref[...], weight(3)).astype(BF)
    if picked:
        back = ones(place_columns(slots_ref, 1, seq))
        wide_ref[...] = dot(back, gm_ref[...]).astype(BF)
    masks = lane_masks(parts[0][0].stop)
    for pair in range(width // LANES):
        lanes = slice(pair * LANES, (pair + 1) * LANES)
        dk = [None, None]
        dv = [None, None]
        dq_all = []
        for top, keys in parts:
            qp = queries[top, lanes]
            kp = k_ref[keys, lanes]
            vp = v_ref[keys, lanes]
            gp = gx_ref[top, lanes]
            dq, dk_now, dv_now = [], [], []
            for mask in masks:
                qm = jnp.where(mask, qp, BF(0)) * BF(HEAD ** (-0.5))
                s = dot_nt(qm, kp) + neg_ref[top, keys]
                e = jnp.exp(s - jnp.max(s, axis=-1, keepdims=True))
                p = e * (1.0 / jnp.sum(e, axis=-1, keepdims=True))
                gprobs = dot_nt(jnp.where(mask, gp, BF(0)) * BF(HEAD ** (-0.5)), vp)
                inner = jnp.sum(gprobs * p, axis=-1, keepdims=True)
                ds = (p * (gprobs - inner)).astype(BF)
                dq.append(dot(ds, kp))
                dk_now.append(dot_tn(ds, qp))
                dv_now.append(dot_tn(p.astype(BF), gp))
            dq_all.append(jnp.where(masks[0], dq[0], dq[1]))
            key_mask = lane_masks(half)[0]
            for block in range(keys.stop // half):
                at = slice(block * half, (block + 1) * half)
                k_new = jnp.where(key_mask, dk_now[0][at], dk_now[1][at])
                v_new = jnp.where(key_mask, dv_now[0][at], dv_now[1][at])
                dk[block] = k_new if dk[block] is None else dk[block] + k_new
                dv[block] = v_new if dv[block] is None else dv[block] + v_new
        gb_ref[0:1, lanes] = sum(jnp.sum(one, axis=0, keepdims=True) for one in dq_all)
        gb_ref[1:2, lanes] = sum(jnp.sum(one, axis=0, keepdims=True) for one in dv)
        if picked:
            dj_ref[0, :, lanes] = dot(back, dq_all[0].astype(BF)).astype(BF)
        else:
            for (top, _), one in zip(parts, dq_all):
                dj_ref[0, top, lanes] = one.astype(BF)
        for block in range(2):
            at = slice(block * half, (block + 1) * half)
            dj_ref[1, at, lanes] = dk[block].astype(BF)
            dj_ref[2, at, lanes] = dv[block].astype(BF)
    gn = dot_nt(dj_ref[0], weight(0))
    gn = gn + dot_nt(dj_ref[1], weight(1))
    gn = gn + dot_nt(dj_ref[2], weight(2))
    gn_ref[...] = gn.astype(BF)


def attend_backward(count, layer, peer, kept, gm, segments, slots, bufs, picked):
    q, k, v = kept
    seq, width = q.shape
    rows, d = gm.shape
    outs = [shape((seq, d), BF), shape((3, seq, width), BF), shape((2, width), F32)]
    scratch = [
        pltpu.VMEM((d // BLOCK, 4 * BLOCK, width), BF),
        pltpu.VMEM((rows, seq), F32),
        pltpu.VMEM((rows, width), BF),
    ]
    if picked:
        outs.append(shape((seq, d), BF))
        scratch.append(pltpu.VMEM((rows, width), BF))
    return pl.pallas_call(
        partial(attend_backward_kernel, count, layer, peer, picked, len(bufs)),
        name="attend_backward",
        out_shape=outs,
        in_specs=[VMEM] * (6 + len(bufs)),
        scratch_shapes=scratch,
        compiler_params=vmem(16),
        cost_estimate=cost(
            2 * rows * d * width + 6 * seq * d * width + 10 * rows * seq * width,
            8 * d * width + 4 * seq * d + 12 * seq * width,
            rows * seq * width // HEAD,
        ),
    )(q, k, v, gm, segments, slots, *bufs)


def attend_grads_kernel(n0_ref, n1_ref, d0_ref, d1_ref, g0_ref, g1_ref, m0_ref, m1_ref, *outs):
    d = n0_ref.shape[1]
    width = m0_ref.shape[1]
    groups = d // BLOCK
    nt = [n0_ref[...].T, n1_ref[...].T]
    for which in range(3):
        total = dot(nt[0], d0_ref[which]) + dot(nt[1], d1_ref[which])
        store_blocks(
            total.astype(BF).reshape(groups, BLOCK, width),
            outs,
            slice(which * BLOCK, (which + 1) * BLOCK),
        )
    total = dot(g0_ref[...].T, m0_ref[...]) + dot(g1_ref[...].T, m1_ref[...])
    store_blocks(
        total.astype(BF).reshape(groups, BLOCK, width), outs, slice(3 * BLOCK, 4 * BLOCK)
    )


def grad_shapes(count, groups, rows, width, split, pieces=1):
    if split:
        blocks = count // 2
        return [shape((blocks, rows, width), BF)] + [
            shape((blocks // pieces, rows, width), BF)
        ] * pieces
    return [shape((groups, rows, width), BF)]


def attend_grads(count, split, n, dj, gm, mixed):
    seq, d = n[0].shape
    width = mixed[0].shape[1]
    outs = grad_shapes(count, d // BLOCK, 4 * BLOCK, width, split, PIECES)
    return pl.pallas_call(
        attend_grads_kernel,
        name="attend_grads",
        out_shape=outs,
        in_specs=[VMEM] * 8,
        compiler_params=vmem(16),
        cost_estimate=cost(16 * seq * d * width, 16 * d * width + 8 * seq * d),
    )(*n, *dj, *gm, *mixed)


def chunk_of(hidden):
    return 512 if hidden % 512 == 0 else hidden


def mlp_forward_kernel(count, layer, arrays, n0_ref, n1_ref, be_ref, *refs):
    e_bufs, s_bufs = refs[:arrays], refs[arrays : 2 * arrays]
    out0_ref, out1_ref, n_ref, acc_ref, we_ref, ws_ref = refs[2 * arrays :]
    rows, d = n0_ref.shape
    hidden = e_bufs[0].shape[2]
    chunk = chunk_of(hidden)
    n_ref[:rows, :] = n0_ref[...]
    n_ref[rows:, :] = n1_ref[...]
    acc_ref[...] = jnp.zeros_like(acc_ref)

    @pl.loop(0, hidden // chunk)
    def _(index):
        cols = pl.ds(pl.multiple_of(index * chunk, chunk), chunk)
        load_blocks(e_bufs, we_ref, cols)
        load_blocks(s_bufs, ws_ref, cols)
        shift = be_ref[:, cols].astype(F32)[layer : layer + 1, :]
        u = dot(n_ref[...], we_ref[...].reshape(d, chunk)) + shift
        t = jnp.tanh(GELU_C * (u + GELU_A * (u * u * u)))
        active = (0.5 * u * (1.0 + t)).astype(BF)
        acc_ref[...] = acc_ref[...] + dot_nt(active, ws_ref[...].reshape(d, chunk))

    out0_ref[...] = acc_ref[:rows, :].astype(BF)
    out1_ref[...] = acc_ref[rows:, :].astype(BF)


def mlp_forward(count, layer, n, be, e_bufs, s_bufs):
    rows, d = n[0].shape
    hidden = e_bufs[0].shape[-1]
    return pl.pallas_call(
        partial(mlp_forward_kernel, count, layer, len(e_bufs)),
        name="mlp_forward",
        out_shape=[shape((rows, d), BF)] * 2,
        in_specs=[VMEM] * (3 + 2 * len(e_bufs)),
        scratch_shapes=[
            pltpu.VMEM((2 * rows, d), BF),
            pltpu.VMEM((2 * rows, d), F32),
            pltpu.VMEM((d // BLOCK, BLOCK, chunk_of(hidden)), BF),
            pltpu.VMEM((d // BLOCK, BLOCK, chunk_of(hidden)), BF),
        ],
        compiler_params=vmem(16),
        cost_estimate=cost(
            8 * rows * d * hidden, 4 * d * hidden + 8 * rows * d, 2 * rows * hidden
        ),
    )(*n, be, *e_bufs, *s_bufs)


def gelu_parts(u):
    square = u * u
    t = jnp.tanh(GELU_C * (u + GELU_A * (square * u)))
    lean = 0.5 * (1.0 + t)
    slope = lean + (0.5 * u) * (1.0 - t * t) * (GELU_C + (3.0 * GELU_C * GELU_A) * square)
    return (u * lean, slope)


def mlp_rows_kernel(layer, arrays, whole, n_ref, g_ref, be_ref, *refs):
    bufs, refs = refs[:arrays], refs[arrays:]
    if whole:
        n1_ref, g1_ref, a1_ref, h1_ref, out_ref, gn_ref, gb_ref, *outs = refs[:-7]
        acc_ref, gacc_ref, we_ref, ws_ref, nt_ref, gt_ref, hold_ref = refs[-7:]
    else:
        out_ref, gn_ref, gb_ref, a_ref, h_ref, acc_ref, gacc_ref, we_ref, ws_ref = refs
    rows, d = n_ref.shape
    hidden = bufs[0].shape[2]
    chunk = chunk_of(hidden)
    groups = d // BLOCK
    if whole:
        nt_ref[:, :rows] = n_ref[...].T
        nt_ref[:, rows:] = n1_ref[...].T
        gt_ref[:, :rows] = g_ref[...].T
        gt_ref[:, rows:] = g1_ref[...].T
    acc_ref[...] = jnp.zeros_like(acc_ref)
    gacc_ref[...] = jnp.zeros_like(gacc_ref)

    @pl.loop(0, hidden // chunk)
    def _(index):
        cols = pl.ds(pl.multiple_of(index * chunk, chunk), chunk)
        load_blocks(bufs[: arrays // 2], we_ref, cols)
        load_blocks(bufs[arrays // 2 :], ws_ref, cols)
        we = we_ref[...].reshape(d, chunk)
        ws = ws_ref[...].reshape(d, chunk)
        shift = be_ref[:, cols].astype(F32)[layer : layer + 1, :]
        active, slope = gelu_parts(dot(n_ref[...], we) + shift)
        active = active.astype(BF)
        gh = dot(g_ref[...], ws) * slope
        gb_ref[:, cols] = jnp.sum(gh, axis=0, keepdims=True)
        gh = gh.astype(BF)
        gacc_ref[...] = gacc_ref[...] + dot_nt(gh, we)
        acc_ref[...] = acc_ref[...] + dot_nt(active, ws)
        if whole:
            hold_ref[:rows, :] = gh
            hold_ref[rows:, :] = h1_ref[:, cols]
            ge = dot(nt_ref[...], hold_ref[...]).astype(BF)
            hold_ref[:rows, :] = active
            hold_ref[rows:, :] = a1_ref[:, cols]
            gs = dot(gt_ref[...], hold_ref[...]).astype(BF)
            half = len(outs) // 2
            every = slice(0, BLOCK)
            store_blocks(ge.reshape(groups, BLOCK, chunk), outs[:half], every, cols)
            store_blocks(gs.reshape(groups, BLOCK, chunk), outs[half:], every, cols)
        else:
            a_ref[:, cols] = active
            h_ref[:, cols] = gh

    gn_ref[...] = gacc_ref[...].astype(BF)
    out_ref[...] = acc_ref[...].astype(BF)


def mlp_rows(count, layer, split, n, g, be, e_bufs, s_bufs, other=()):
    rows, d = n.shape
    bufs = (*e_bufs, *s_bufs)
    hidden = bufs[0].shape[-1]
    chunk = chunk_of(hidden)
    groups = d // BLOCK
    whole = bool(other)
    half = shape((rows, d), BF)
    outs = [half, half, shape((1, hidden), F32)]
    blocks = pltpu.VMEM((groups, BLOCK, chunk), BF)
    scratch = [pltpu.VMEM((rows, d), F32)] * 2 + [blocks] * 2
    if whole:
        outs += 2 * grad_shapes(count, groups, BLOCK, hidden, split)
        scratch += [pltpu.VMEM((d, 2 * rows), BF)] * 2 + [pltpu.VMEM((2 * rows, chunk), BF)]
    else:
        outs += [shape((rows, hidden), BF)] * 2
    return pl.pallas_call(
        partial(mlp_rows_kernel, layer, len(bufs), whole),
        name="mlp_whole" if whole else "mlp_rows",
        out_shape=outs,
        in_specs=[VMEM] * (3 + len(bufs) + len(other)),
        scratch_shapes=scratch,
        compiler_params=vmem(24),
        cost_estimate=cost(
            (16 if whole else 8) * rows * d * hidden,
            8 * d * hidden + 16 * rows * d,
            rows * hidden,
        ),
    )(n, g, be, *bufs, *other)


def mlp_backward_kernel(count, layer, arrays, full, outputs, n0_ref, n1_ref, g0_ref, g1_ref, be_ref, *refs):
    e_bufs, s_bufs = refs[:arrays], refs[arrays : 2 * arrays]
    refs = refs[2 * arrays :]
    if full:
        out0_ref, out1_ref, refs = refs[0], refs[1], refs[2:]
    gn0_ref, gn1_ref, gb_ref = refs[:3]
    outs = refs[3 : 3 + outputs]
    refs = refs[3 + outputs :]
    n_ref, g_ref, nt_ref, gt_ref, gacc_ref, we_ref, ws_ref = refs[:7]
    if full:
        acc_ref = refs[7]
    rows, d = n0_ref.shape
    hidden = e_bufs[0].shape[2]
    chunk = chunk_of(hidden)
    groups = d // BLOCK
    n_ref[:rows, :] = n0_ref[...]
    n_ref[rows:, :] = n1_ref[...]
    g_ref[:rows, :] = g0_ref[...]
    g_ref[rows:, :] = g1_ref[...]
    nt_ref[...] = n_ref[...].T
    gt_ref[...] = g_ref[...].T
    gacc_ref[...] = jnp.zeros_like(gacc_ref)
    if full:
        acc_ref[...] = jnp.zeros_like(acc_ref)

    @pl.loop(0, hidden // chunk)
    def _(index):
        cols = pl.ds(pl.multiple_of(index * chunk, chunk), chunk)
        load_blocks(e_bufs, we_ref, cols)
        load_blocks(s_bufs, ws_ref, cols)
        we = we_ref[...].reshape(d, chunk)
        ws = ws_ref[...].reshape(d, chunk)
        shift = be_ref[:, cols].astype(F32)[layer : layer + 1, :]
        u = dot(n_ref[...], we) + shift
        square = u * u
        t = jnp.tanh(GELU_C * (u + GELU_A * (square * u)))
        lean = 0.5 * (1.0 + t)
        active = (u * lean).astype(BF)
        slope = lean + (0.5 * u) * (1.0 - t * t) * (GELU_C + (3.0 * GELU_C * GELU_A) * square)
        gh = dot(g_ref[...], ws) * slope
        gb_ref[:, cols] = jnp.sum(gh, axis=0, keepdims=True)
        gh = gh.astype(BF)
        ge = dot(nt_ref[...], gh).astype(BF)
        gs = dot(gt_ref[...], active).astype(BF)
        ge, gs = ge.reshape(groups, BLOCK, chunk), gs.reshape(groups, BLOCK, chunk)
        if full:
            store_blocks(ge, outs[: outputs // 2], slice(0, BLOCK), cols)
            store_blocks(gs, outs[outputs // 2 :], slice(0, BLOCK), cols)
        else:
            store_blocks(ge, outs, slice(0, BLOCK), cols)
            store_blocks(gs, outs, slice(BLOCK, 2 * BLOCK), cols)
        gacc_ref[...] = gacc_ref[...] + dot_nt(gh, we)
        if full:
            acc_ref[...] = acc_ref[...] + dot_nt(active, ws)

    gn0_ref[...] = gacc_ref[:rows, :].astype(BF)
    gn1_ref[...] = gacc_ref[rows:, :].astype(BF)
    if full:
        out0_ref[...] = acc_ref[:rows, :].astype(BF)
        out1_ref[...] = acc_ref[rows:, :].astype(BF)


def mlp_backward(count, layer, split, n, g, be, e_bufs, s_bufs, full):
    rows, d = n[0].shape
    hidden = e_bufs[0].shape[-1]
    groups = d // BLOCK
    half = shape((rows, d), BF)
    if full:
        grads = 2 * grad_shapes(count, groups, BLOCK, hidden, split)
    else:
        grads = grad_shapes(count, groups, 2 * BLOCK, hidden, split)
    blocks = pltpu.VMEM((groups, BLOCK, chunk_of(hidden)), BF)
    return pl.pallas_call(
        partial(mlp_backward_kernel, count, layer, len(e_bufs), full, len(grads)),
        name="mlp_backward",
        out_shape=[half] * (4 if full else 2) + [shape((1, hidden), F32)] + grads,
        in_specs=[VMEM] * (5 + 2 * len(e_bufs)),
        scratch_shapes=[
            pltpu.VMEM((2 * rows, d), BF),
            pltpu.VMEM((2 * rows, d), BF),
            pltpu.VMEM((d, 2 * rows), BF),
            pltpu.VMEM((d, 2 * rows), BF),
            pltpu.VMEM((2 * rows, d), F32),
            blocks,
            blocks,
        ]
        + ([pltpu.VMEM((2 * rows, d), F32)] if full else []),
        compiler_params=vmem(28),
        cost_estimate=cost(
            (24 if full else 20) * rows * d * hidden,
            8 * d * hidden + 16 * rows * d,
            2 * rows * hidden,
        ),
    )(*n, *g, be, *e_bufs, *s_bufs)


def middle_kernel(layer, x_ref, own_ref, got_ref, slots_ref, gain_ref, shift_ref, bias_ref, *outs):
    middle = (
        x_ref[...].astype(F32)
        + (own_ref[...].astype(F32) + got_ref[...].astype(F32))
        + row_of(bias_ref, layer, 0)
    )
    unit, _ = statistics(middle)
    normed = (unit * row_of(gain_ref, layer, 1) + row_of(shift_ref, layer, 1)).astype(BF)
    outs[0][...] = middle
    outs[1][...] = normed
    if layer == 0:
        hit = ones(place_rows(slots_ref, 1, x_ref.shape[0]))
        outs[2][...] = exact_pick(hit, middle)
        outs[3][...] = dot(hit, normed).astype(BF)


def second_kernel(
    x_ref, mid_ref, own_ref, got_ref, slots_ref, gain_ref, shift_ref, bias_ref,
    out_ref, n_ref, few_ref,
):
    seq = x_ref.shape[0]
    latent = (
        mid_ref[...]
        + (own_ref[...].astype(F32) + got_ref[...].astype(F32))
        + row_of(bias_ref, 0, 1)
    )
    known = column(slots_ref[...]) >= 1.0
    latent = jnp.where(known, latent, 0.0).astype(BF)
    hit = place_columns(slots_ref, 0, seq)
    occupied = jnp.sum(jnp.where(hit, 1.0, 0.0), axis=-1, keepdims=True)
    second = x_ref[...].astype(F32) * (1.0 - occupied) + dot(ones(hit), latent)
    unit, _ = statistics(second)
    out_ref[...] = second
    few, _ = statistics(latent.astype(F32))
    few_ref[...] = (few * row_of(gain_ref, 1, 0) + row_of(shift_ref, 1, 0)).astype(BF)
    n_ref[...] = (unit * row_of(gain_ref, 1, 0) + row_of(shift_ref, 1, 0)).astype(BF)


def blend_kernel(early_ref, few_ref, slots_ref, out_ref):
    hit = ones(place_columns(slots_ref, 0, early_ref.shape[0]))
    placed = dot(hit, few_ref[...])
    taken = jnp.sum(hit.astype(F32), axis=-1, keepdims=True) > 0.5
    out_ref[...] = jnp.where(taken, placed, early_ref[...].astype(F32)).astype(BF)


def grad_middle_kernel(mid_ref, own_ref, got_ref, cot_ref, gain_ref, out_ref, low_ref, sum_ref):
    cot = cot_ref[...].astype(F32)
    grad = own_ref[...].astype(F32) + got_ref[...].astype(F32)
    back, gain, shift = norm_backward(mid_ref[...], grad, row_of(gain_ref, 1, 1))
    total = cot + back
    out_ref[...] = total
    low_ref[...] = total.astype(BF)
    sum_ref[0:1, :] = gain
    sum_ref[1:2, :] = shift
    sum_ref[2:3, :] = jnp.sum(total, axis=0, keepdims=True)
    sum_ref[3:4, :] = jnp.sum(cot, axis=0, keepdims=True)


def grad_second_kernel(
    x_ref, own_ref, got_ref, gm_ref, slots_ref, gain_ref, out_ref, pick_ref, low_ref, sum_ref
):
    grad = own_ref[...].astype(F32) + got_ref[...].astype(F32)
    back, gain, shift = norm_backward(x_ref[...], grad, row_of(gain_ref, 1, 0))
    total = gm_ref[...] + back
    out_ref[...] = total
    hit = place_rows(slots_ref, 0, x_ref.shape[0])
    known = column(slots_ref[...]) >= 1.0
    pick = jnp.where(known, exact_pick(ones(hit), total), 0.0)
    pick_ref[...] = pick
    low_ref[...] = pick.astype(BF)
    sum_ref[0:1, :] = gain
    sum_ref[1:2, :] = shift


def grad_picked_kernel(mid_ref, own_ref, got_ref, pick_ref, gain_ref, out_ref, low_ref, sum_ref):
    grad = own_ref[...].astype(F32) + got_ref[...].astype(F32)
    back, gain, shift = norm_backward(mid_ref[...], grad, row_of(gain_ref, 0, 1))
    pick = pick_ref[...]
    total = pick + back
    out_ref[...] = total
    low_ref[...] = total.astype(BF)
    sum_ref[0:1, :] = gain
    sum_ref[1:2, :] = shift
    sum_ref[2:3, :] = jnp.sum(total, axis=0, keepdims=True)
    sum_ref[3:4, :] = jnp.sum(pick, axis=0, keepdims=True)


def grad_first_kernel(
    x_ref, own_ref, got_ref, gm_ref, second_ref, slots_ref, gain_ref,
    s22_ref, s21_ref, s12_ref, pair1_ref, pair0_ref, peer1_ref, peer0_ref, be1_ref, more1_ref, be0_ref,
    out_ref, sum_ref,
):
    seq, d = x_ref.shape
    grad = own_ref[...].astype(F32) + got_ref[...].astype(F32)
    back, gain, shift = norm_backward(x_ref[...].astype(F32), grad, row_of(gain_ref, 0, 0))
    hit = place_columns(slots_ref, 0, seq)
    occupied = jnp.sum(jnp.where(hit, 1.0, 0.0), axis=-1, keepdims=True)
    source = ones(place_columns(slots_ref, 1, seq))
    out_ref[...] = second_ref[...] * (1.0 - occupied) + (exact_pick(source, gm_ref[...]) + back)
    width = pair0_ref.shape[1]
    for index, row in enumerate(
        (
            gain, s12_ref[0:1, :], s21_ref[0:1, :], s22_ref[0:1, :],
            shift, s12_ref[1:2, :], s21_ref[1:2, :], s22_ref[1:2, :],
            s12_ref[2:3, :], s12_ref[3:4, :], s22_ref[2:3, :], s22_ref[3:4, :],
        )
    ):
        for part in range(d // width):
            at = index * (d // width) + part
            sum_ref[at : at + 1, :] = row[:, part * width : (part + 1) * width]
    first = 12 * (d // width)
    sum_ref[first : first + 2, :] = pair0_ref[...] + peer0_ref[...]
    sum_ref[first + 2 : first + 4, :] = pair1_ref[...] + peer1_ref[...]
    hidden = be0_ref.shape[1]
    for layer, row in enumerate((be0_ref[...], be1_ref[...] + more1_ref[...])):
        for part in range(hidden // width):
            at = first + 4 + layer * (hidden // width) + part
            sum_ref[at : at + 1, :] = row[:, part * width : (part + 1) * width]


def vectors_kernel(sum_ref, gains_ref, shifts_ref, branch_ref, pair_ref, hidden_ref):
    d = gains_ref.shape[2]
    width = sum_ref.shape[1]
    index = 0
    for ref in (gains_ref, shifts_ref, branch_ref):
        for layer in range(2):
            for which in range(2):
                for part in range(d // width):
                    ref[layer, which : which + 1, part * width : (part + 1) * width] = sum_ref[
                        index : index + 1, :
                    ]
                    index += 1
    for layer in range(2):
        pair_ref[layer] = sum_ref[index : index + 2, :]
        index += 2
    for layer in range(2):
        for part in range(hidden_ref.shape[1] // width):
            hidden_ref[layer : layer + 1, part * width : (part + 1) * width] = sum_ref[
                index : index + 1, :
            ]
            index += 1


def small(kernel, name, outs, *args, wait=0):
    moved = sum(a.size * a.dtype.itemsize for a in args) + sum(
        o.size * o.dtype.itemsize for o in outs
    )
    return pl.pallas_call(
        kernel,
        name=name,
        out_shape=outs,
        in_specs=[VMEM] * len(args),
        compiler_params=vmem(24),
        cost_estimate=cost(4 * moved + wait, moved),
    )(*args)


def split_kernel(stride, keep_ref, *refs):
    *got_refs, kept_ref, sent_ref = refs
    each = got_refs[0].shape[0]
    bit = lax.rem(lax.axis_index("fsdp") // stride, 2)
    for index in range(kept_ref.shape[0]):
        got_ref, first = got_refs[2 * index // each], 2 * index // each * each
        for out, place in ((kept_ref, bit), (sent_ref, 1 - bit)):
            at = 2 * index + place
            got = got_ref[at - first].astype(F32)
            out[index] = (keep_ref[at].astype(F32) + got).astype(BF)


def split_kernel_of(stride, used, behind):
    def kernel(*refs):
        split_kernel(stride, *refs[:used], *refs[used + behind :])

    return kernel


def split(stride, keep, *got, behind=None):
    blocks, rows, width = keep.shape
    return pl.pallas_call(
        split_kernel_of(stride, 1 + len(got), behind is not None),
        name="split",
        out_shape=[shape((blocks // 2, rows, width), BF)] * 2,
        in_specs=[VMEM] * (1 + len(got)) + [ANY] * (behind is not None),
        compiler_params=vmem(8),
        cost_estimate=cost(keep.size + SPLIT_WAIT[stride], 6 * keep.size),
    )(keep, *got, *(() if behind is None else (behind,)))


def finish_kernel(counts, *refs):
    joint_ref, merge_ref, expand_ref, shrink_ref = refs[-4:]
    totals = []
    first = 0
    for number in counts:
        total = refs[first][0].astype(F32)
        for ref in refs[first + 1 : first + number]:
            total = total + ref[0].astype(F32)
        totals.append(total)
        first += number
    rows = merge_ref.shape[1]
    attend, both = totals[:2]
    half = both.shape[0] // 2
    sums = ((attend, both[:half, :], both[half:, :]), totals[2:])
    for layer, (attend, expand, shrink) in enumerate(sums):
        for which in range(3):
            joint_ref[layer, which] = attend[which * rows : (which + 1) * rows, :]
        merge_ref[layer] = attend[3 * rows :, :]
        expand_ref[layer] = expand
        shrink_ref[layer] = shrink


def finish(states):
    _, rows, width = states[0][0].shape
    hidden = states[1][0].shape[2]
    rows = rows // 4
    outs = [shape((2, 3, rows, width), F32), shape((2, rows, width), F32)]
    outs += [shape((2, rows, hidden), F32)] * 2
    counts = tuple(len(state) for state in states)
    return small(
        partial(finish_kernel, counts), "finish", outs, *[one for state in states for one in state]
    )


def regroup(array, count, kinds):
    rows = array.shape[0] * array.shape[1] // kinds // BLOCK
    each = array.shape[1] // kinds
    width = array.shape[2]
    split = array.reshape(array.shape[0], kinds, each, width).transpose(1, 0, 2, 3)
    return split.reshape(kinds, rows, BLOCK, width).transpose(1, 0, 2, 3).reshape(
        rows, kinds * BLOCK, width
    )


def ungroup(array, count, kinds):
    width = array.shape[2]
    split = array.reshape(array.shape[0], kinds, BLOCK, width).transpose(1, 0, 2, 3)
    each = array.shape[0] * BLOCK // count
    return split.reshape(kinds, count, each, width).transpose(1, 0, 2, 3).reshape(
        count, kinds * each, width
    )


def shards(
    count,
    embedded,
    segments,
    thoughts,
    cotangent,
    gains,
    shifts,
    joint_weight,
    joint_bias,
    merge_weight,
    expand_weight,
    expand_bias,
    shrink_weight,
    branch_biases,
):
    seq, d = embedded.shape
    rows_each = joint_weight.shape[1]
    width = joint_weight.shape[3]
    hidden = expand_weight.shape[2]
    slots = thoughts.shape[1]
    staged = rows_each == BLOCK and count == 16
    rows_f32, rows_bf = shape((seq, d), F32), shape((seq, d), BF)
    few_f32, few_bf = shape((slots, d), F32), shape((slots, d), BF)
    ins = (
        joint_weight.transpose(0, 2, 1, 3),
        merge_weight.transpose(0, 2, 1),
        expand_weight,
        shrink_weight.transpose(0, 2, 1),
    )
    bufs = {}

    def first_step(own, *others, wait=JOIN_WAIT):
        return join(after(own, *others), across(own, count, 8), wait)

    def next_step(own, *others, wait=JOIN_WAIT):
        return join(after(own, *others), across(own, count, 4), wait)

    def third_step(own):
        return (own, across(own, count, 2))

    def last_step(both):
        return [*both, across(both[0], count, 1), across(both[1], count, 1)]

    if staged:
        attend, plain = shape((4 * rows_each, width), BF), shape((rows_each, hidden), BF)
        (a0,) = small(pack_kernel, "pack", [attend], *ins[:2])
        normed, early, e0, s0, a1, e1, s1 = small(
            start_kernel, "start", [rows_bf, rows_bf, plain, plain, attend, plain, plain],
            *ins, embedded, gains, shifts,
        )
    else:
        first = embedded.astype(F32)
        center = first - jnp.mean(first, axis=-1, keepdims=True)
        scale = lax.rsqrt(jnp.mean(center * center, axis=-1, keepdims=True) + EPSILON)
        normed = (
            center * scale * gains[0, 0].astype(F32) + shifts[0, 0].astype(F32)
        ).astype(BF)
        for layer in range(2):
            attend = jnp.concatenate(
                (ins[0][layer].reshape(3 * rows_each, width), ins[1][layer]), axis=0
            )
            for name, one, kind in (("a", attend, 4), ("e", ins[2][layer], 1), ("s", ins[3][layer], 1)):
                whole = lax.all_gather(one, "fsdp", axis=0, tiled=False)
                bufs[f"{name}{layer}"] = [regroup(whole, count, kind)]

    slots_peer = swap(thoughts)
    normed_peer = swap(normed)

    if staged:
        a0, e0 = sync(first_step(a0), e0)
        cot_peer = hold(swap(cotangent), 4 * 10**9)
        a0, e0, s0, cot_peer, early_peer = sync(
            next_step(a0, cot_peer, wait=10**10), first_step(e0), s0, cot_peer, swap(early)
        )
        a0, e0, s0, a1, normed_peer, slots_peer = sync(
            third_step(a0), next_step(e0), first_step(s0), a1, normed_peer, slots_peer
        )
        bufs["a0"] = last_step(a0)
    else:
        cot_peer = swap(cotangent)

    def attention(layer, own, peer):
        weights = bufs[f"a{layer}"]
        part_peer, *kept_peer = attend_forward(count, layer, True, peer, segments, joint_bias, weights)
        got = swap(part_peer)
        part_own, *kept_own = attend_forward(
            count, layer, False, after(own, part_peer), segments, joint_bias, weights
        )
        return (part_own, got, (own, peer), (kept_own, kept_peer))

    part, got, n_one, kept_one = attention(0, normed, normed_peer)
    if staged:
        e0, s0, a1, part, e1 = sync(
            third_step(e0), next_step(s0, part), first_step(a1, part), part, e1
        )
        bufs["e0"] = last_step(e0)
    middle_one, n2_one, middle_few, n2_few = small(
        partial(middle_kernel, 0), "middle", [rows_f32, rows_bf, few_f32, few_bf],
        embedded, part, got, thoughts, gains, shifts, branch_biases, wait=10**10,
    )
    n2_few = (n2_few, swap(n2_few))
    if staged:
        s0, a1, e1, s1, n2_few, bufs["e0"] = sync(
            third_step(s0), next_step(a1), first_step(e1), s1, n2_few, bufs["e0"]
        )
        bufs["s0"] = last_step(s0)
    own, peer = mlp_forward(count, 0, n2_few, expand_bias, bufs["e0"], bufs["s0"])
    second, normed, few = small(
        second_kernel, "second", [rows_f32, rows_bf, few_bf],
        embedded, middle_few, own, swap(peer), thoughts, gains, shifts, branch_biases,
    )
    if staged:
        (normed_peer,) = small(blend_kernel, "blend", [rows_bf], early_peer, swap(few), slots_peer)
    else:
        normed_peer = swap(normed)

    if staged:
        a1, e1, s1, normed, normed_peer = sync(
            third_step(a1), next_step(e1, normed), first_step(s1, normed), normed, normed_peer
        )
        bufs["a1"] = last_step(a1)
    part, got, n_two, kept_two = attention(1, normed, normed_peer)
    if staged:
        e1, s1, part = sync(third_step(e1), next_step(s1, part), part)
        bufs["e1"] = last_step(e1)
    middle_two, n2_two = small(
        partial(middle_kernel, 1), "middle", [rows_f32, rows_bf],
        second, part, got, thoughts, gains, shifts, branch_biases,
    )
    n2_peer = swap(n2_two)
    if staged:
        s1, n2_two, n2_peer, bufs["e1"] = sync(third_step(s1), n2_two, n2_peer, bufs["e1"])
        bufs["s1"] = last_step(s1)
    peer_two, gn_peer, gb_peer, *more = mlp_rows(
        count, 1, staged, n2_peer, cot_peer, expand_bias, bufs["e1"], bufs["s1"]
    )
    got = swap(gn_peer)
    own_two, gn_own, gb_own, *grads = mlp_rows(
        count, 1, staged, after(n2_two, gn_peer), cotangent, expand_bias, bufs["e1"], bufs["s1"],
        (n2_peer, cot_peer, *more),
    )
    gb_two = (gb_own, gb_peer)

    def begin(grads, kind):
        if staged:
            return (grads[0], *[across(sent, count, 1) for sent in grads[1:]])
        done = lax.psum_scatter(
            ungroup(grads[0], count, kind), "fsdp", scatter_dimension=0, tiled=False
        )
        return (done[None],)

    def settle(state, stride, *others, behind=None):
        if not staged:
            return state
        return tuple(split(stride, *after(state, *others), behind=behind))

    def move(state, stride):
        return (state[0], across(state[1], count, stride)) if staged else state

    def apart(grads):
        return (grads[: len(grads) // 2], grads[len(grads) // 2 :])

    e1, s1 = apart(grads)
    s1, e1 = begin(s1, 1), begin(e1, 1)
    gm, gm_low, s22 = small(
        grad_middle_kernel, "grad_middle", [rows_f32, rows_bf, shape((4, d), F32)],
        middle_two, gn_own, got, cotangent, gains, wait=25 * 10**9,
    )
    s1, e1, gm, gm_low = sync(
        settle(s1, 2, behind=s22), settle(e1, 2, behind=s22), gm, gm_low
    )
    s1, e1 = move(s1, 2), move(e1, 2)
    gm_peer = swap(gm_low)
    weights = bufs["a1"]
    back_own = attend_backward(
        count, 1, False, kept_two[0][:3], gm_low, segments, thoughts, weights, False
    )
    back_peer = attend_backward(
        count, 1, True, kept_two[1][:3], after(gm_peer, back_own[0]), segments, slots_peer,
        weights, False,
    )
    s1, back_peer, back_own = sync(settle(s1, 4, back_peer[0]), back_peer, back_own)
    got = swap(back_peer[0])
    s1 = move(s1, 4)
    a1 = attend_grads(
        count, staged, n_two, (back_own[1], back_peer[1]), (gm_low, gm_peer),
        (kept_two[0][3], kept_two[1][3]),
    )
    a1 = begin(a1, 4)
    s1 = settle(s1, 8, got)
    e1 = settle(e1, 4, s1)
    s1, e1, a1, got, own = sync(s1, e1, settle(a1, 2, e1), got, back_own[0])
    s1, e1, a1 = move(s1, 8), move(e1, 4), move(a1, 2)
    grad_second, g_few, g_low, s21 = small(
        grad_second_kernel, "grad_second", [rows_f32, few_f32, few_bf, shape((2, d), F32)],
        second, own, got, gm, thoughts, gains,
    )
    pair_two = (back_own[2], back_peer[2])

    g_peer = swap(g_low)
    own, peer, gb_one, *m0 = mlp_backward(
        count, 0, staged, n2_few, (g_low, g_peer), expand_bias,
        bufs["e0"], bufs["s0"], False,
    )
    m0 = settle(begin(m0, 2), 2)
    gm_few, gm_low, s12 = small(
        grad_picked_kernel, "grad_picked", [few_f32, few_bf, shape((4, d), F32)],
        middle_few, own, swap(peer), g_few, gains,
    )
    gm_peer = swap(gm_low)
    weights = bufs["a0"]
    back_own = attend_backward(
        count, 0, False, kept_one[0][:3], gm_low, segments, thoughts, weights, True
    )
    e1 = settle(e1, 8, back_own[0])
    a1 = settle(a1, 4, e1)
    s1, e1, a1, m0, gm_peer, back_own = sync(s1, e1, a1, m0, gm_peer, back_own)
    e1, a1, m0 = move(e1, 8), move(a1, 4), move(m0, 2)
    back_peer = attend_backward(
        count, 0, True, kept_one[1][:3], gm_peer, segments, slots_peer, weights, True
    )
    got = swap(back_peer[0])
    a0 = attend_grads(
        count, staged, n_one, (back_own[1], back_peer[1]), (back_own[3], back_peer[3]),
        (kept_one[0][3], kept_one[1][3]),
    )
    pair_one = (back_own[2], back_peer[2])
    a1 = move(settle(a1, 8, got), 8)
    m0 = settle(m0, 4, a1, e1)
    a1, m0, a0, got, n2_one, peer_two = sync(
        a1, m0, settle(begin(a0, 4), 2, m0), got, n2_one, peer_two
    )
    m0, a0 = move(m0, 4), move(a0, 2)
    embedded_grad, vectors = small(
        grad_first_kernel, "grad_first",
        [rows_f32, shape((12 * d // width + 4 + 2 * (hidden // width), width), F32)],
        embedded, back_own[0], got, gm_few, grad_second, thoughts, gains,
        s22, s21, s12, pair_two[0], pair_one[0], pair_two[1], pair_one[1], *gb_two, gb_one,
    )
    shared = jnp.arange(vectors.shape[0])[:, None] < 12 * d // width
    vectors = vectors + jnp.where(shared, swap(vectors), 0.0)
    n2_peer = swap(after(n2_one, vectors))
    if staged:
        vectors = vectors + across(vectors, count, 1)
        m0 = settle(m0, 8, embedded_grad)
        m0, a0, vectors = sync(m0, settle(a0, 4, m0), vectors)
        m0, a0 = move(m0, 8), move(a0, 4)
    latent_own, latent_peer = mlp_forward(
        count, 0, (n2_one, n2_peer), expand_bias, bufs["e0"], bufs["s0"]
    )
    if staged:
        vectors = vectors + across(vectors, count, 2)
        m0 = (m0[0], hold(after(m0[1], latent_own)))
        m0, a0, vectors = sync(m0, settle(a0, 8, m0), vectors)
        a0 = move(a0, 8)
        total = (vectors + across(vectors, count, 4)) + (
            across(vectors, count, 8) + across(vectors, count, 12)
        )
    else:
        total = lax.psum(vectors, "fsdp")

    biases = branch_biases.astype(F32)
    latent_peer, peer_two = swap(latent_peer), swap(peer_two)
    latent = middle_one + (latent_own.astype(F32) + latent_peer.astype(F32)) + biases[0, 1]
    language = middle_two + (own_two.astype(F32) + peer_two.astype(F32)) + biases[1, 1]

    joint_grad, merge_grad, expand_grad, shrink_grad = finish((a0, m0, a1, e1, s1))
    vector = shape((2, 2, d), F32)
    gains_grad, shifts_grad, branch_grad, joint_bias_grad, expand_bias_grad = small(
        vectors_kernel, "vectors",
        [vector, vector, vector, shape((2, 2, width), F32), shape((2, hidden), F32)],
        total,
    )
    return (
        latent.astype(BF),
        language.astype(BF),
        embedded_grad,
        gains_grad,
        shifts_grad,
        joint_grad.transpose(0, 2, 1, 3),
        joint_bias_grad,
        merge_grad.transpose(0, 2, 1),
        expand_grad,
        expand_bias_grad,
        shrink_grad.transpose(0, 2, 1),
        branch_grad,
    )


def solution(mesh):
    placed = (
        P(("fsdp", "tensor"), None),
        P("fsdp", None),
        P(("fsdp", "tensor"), None),
        P(("fsdp", "tensor"), None),
        P(),
        P(),
        P(None, "fsdp", None, "tensor"),
        P(None, None, "tensor"),
        P(None, "tensor", "fsdp"),
        P(None, "fsdp", "tensor"),
        P(None, "tensor"),
        P(None, "tensor", "fsdp"),
        P(),
    )
    return jax.shard_map(
        partial(shards, mesh.shape["fsdp"]),
        mesh=mesh,
        in_specs=placed,
        out_specs=(
            P(("fsdp", "tensor"), None),
            P(("fsdp", "tensor"), None),
            P(("fsdp", "tensor"), None),
            P(),
            P(),
            P(None, "fsdp", None, "tensor"),
            P(None, None, "tensor"),
            P(None, "tensor", "fsdp"),
            P(None, "fsdp", "tensor"),
            P(None, "tensor"),
            P(None, "tensor", "fsdp"),
            P(),
        ),
        check_vma=False,
    )
```
